128 devices in a mesh: ty: 16 (over y, z_hi, core), tx: 8 (over x, z_lo).
Axes of the slice: x: 4, y: 4, z: 4 (z_hi: 2, z_lo: 2; z = z_hi * 2 + z_lo), core: 2. Of those that a mesh axis runs over, the one named last changes fastest.
Arguments:
- theta_start: float32 [32, 256, 2048], P(None, 'ty', 'tx'), may hold values from -6 to 6
- salt_start: float32 [32, 256, 2048], P(None, 'ty', 'tx'), may hold values from -6 to 6
- east_velocity: float32 [32, 256, 2048], P(None, 'ty', 'tx'), may hold values from -6 to 6
- north_velocity: float32 [32, 256, 2048], P(None, 'ty', 'tx'), may hold values from -6 to 6
- surface_start: float32 [256, 2048], P('ty', 'tx'), may hold values from -12 to 12
- wet_levels: int32 [256, 2048], P('ty', 'tx'), may hold values from 0 to 32, as said below
- face_frame: int32 [256, 2048], P('ty', 'tx'), may hold values from 0 to 3, as said below
- theta_sense: float32 [32, 256, 2048], P(None, 'ty', 'tx'), may hold values from -6 to 6
- salt_sense: float32 [32, 256, 2048], P(None, 'ty', 'tx'), may hold values from -6 to 6
- east_sense: float32 [32, 256, 2048], P(None, 'ty', 'tx'), may hold values from -6 to 6
- north_sense: float32 [32, 256, 2048], P(None, 'ty', 'tx'), may hold values from -6 to 6
- surface_sense: float32 [256, 2048], P('ty', 'tx'), may hold values from -12 to 12
Outputs:
- theta_adjoint: float32 [32, 256, 2048], P(None, 'ty', 'tx')
- salt_adjoint: float32 [32, 256, 2048], P(None, 'ty', 'tx')
- east_adjoint: float32 [32, 256, 2048], P(None, 'ty', 'tx')
- north_adjoint: float32 [32, 256, 2048], P(None, 'ty', 'tx')
- surface_adjoint: float32 [256, 2048], P('ty', 'tx')
The draws below stay inside these ranges and needn't reach their ends.
Inputs may be any that keep to these rules, and one draw needn't show every extreme that they name: `wet_levels`: level k (from 0) of a column is wet where k is below this number; 0 marks land. `face_frame`: constant over each of the 4 blocks of 512 columns, a different value in each block.
All inputs are finite; a program needn't handle non-finite values.
Results may differ from the reference program's by a relative error of at most 0.0003.
Values sent between devices are 32-bit elements; how exact they have to be, the bound alone decides.
No kernel may reach another device: no remote copies, remote signals or barrier semaphores. Data moves between devices by JAX's collectives and lax.ppermute only.
A program may use at most 64 MiB of HBM per device.

```python
import jax
import jax.numpy as jnp
from jax import lax

L = 32
ITERS = 3
FACES = 4
NY = 256
NX = 2048


def surface_draw(key):
    row_pos = (jnp.arange(NY).astype(jnp.float32) / max(NY - 1, 1))[:, None]
    col_pos = (jnp.arange(NX).astype(jnp.float32) / max(NX - 1, 1))[None, :]
    values = jnp.clip(jax.random.normal(key, (NY, NX)), -4.0, 4.0)
    return values * (1.0 + row_pos + col_pos)


def draw_surface_start(key, part):
    return surface_draw(jax.random.fold_in(key, 11)).astype(jnp.float32)


def draw_surface_sense(key, part):
    return surface_draw(jax.random.fold_in(key, 23)).astype(jnp.float32)


def draw_wet_levels(key, part):
    land_key, depth_key = jax.random.split(jax.random.fold_in(key, 37))
    land_roll = jax.random.randint(land_key, (NY, NX), 0, 5)
    depth_roll = jax.random.randint(depth_key, (NY, NX), 1, L + 1)
    return jnp.where(land_roll == 0, 0, depth_roll).astype(jnp.int32)


def draw_face_frame(key, part):
    frame_codes = jax.random.permutation(jax.random.fold_in(key, 41), FACES).astype(jnp.int32)
    face_index = jnp.arange(NX) // (NX // FACES)
    column_codes = jnp.take(frame_codes, face_index)
    return jnp.broadcast_to(column_codes[None, :], (NY, NX)).astype(jnp.int32)


def steps_of(key, extent, pieces, low, high):
    def one(position, shards_of):
        heights = jax.random.uniform(jax.random.fold_in(jax.random.fold_in(key, 6), position), (shards_of,), jnp.float32, low / len(pieces), high / len(pieces))
        return jnp.repeat(jnp.exp(heights), extent[position] // shards_of).reshape((-1,) + (1,) * (len(extent) - position - 1))

    loudness = one(*pieces[0])
    for cut in pieces[1:]:
        loudness = loudness * one(*cut)
    return loudness


def normal_values(stream_key, shape, scale, limit, cuts=(), kind=jnp.bfloat16):
    gain = steps_of(stream_key, shape, cuts, -0.22, 0.18) if cuts else 1.0
    drawn = jax.random.normal(stream_key, shape, jnp.float32) * scale * gain
    return jnp.minimum(jnp.maximum(drawn, -limit), limit).astype(kind)


def setup_inputs(seed: int = 0) -> dict:
    keys = jax.random.split(jax.random.key(seed), 13)
    theta_start = normal_values(keys[0], (L, NY, NX), 1.0, 6.0, ((1, 16), (2, 8)), jnp.float32)
    salt_start = normal_values(keys[1], (L, NY, NX), 1.0, 6.0, ((1, 16), (2, 8)), jnp.float32)
    east_velocity = normal_values(keys[2], (L, NY, NX), 1.0, 6.0, ((1, 16), (2, 8)), jnp.float32)
    north_velocity = normal_values(keys[3], (L, NY, NX), 1.0, 6.0, ((1, 16), (2, 8)), jnp.float32)
    surface_start = draw_surface_start(jax.random.fold_in(keys[12], 71), 0)
    wet_levels = draw_wet_levels(jax.random.fold_in(keys[12], 71), 0)
    face_frame = draw_face_frame(jax.random.fold_in(keys[12], 71), 0)
    theta_sense = normal_values(keys[7], (L, NY, NX), 1.0, 6.0, ((1, 16), (2, 8)), jnp.float32)
    salt_sense = normal_values(keys[8], (L, NY, NX), 1.0, 6.0, ((1, 16), (2, 8)), jnp.float32)
    east_sense = normal_values(keys[9], (L, NY, NX), 1.0, 6.0, ((1, 16), (2, 8)), jnp.float32)
    north_sense = normal_values(keys[10], (L, NY, NX), 1.0, 6.0, ((1, 16), (2, 8)), jnp.float32)
    surface_sense = draw_surface_sense(jax.random.fold_in(keys[12], 71), 0)
    return dict(theta_start=theta_start, salt_start=salt_start, east_velocity=east_velocity, north_velocity=north_velocity, surface_start=surface_start, wet_levels=wet_levels, face_frame=face_frame, theta_sense=theta_sense, salt_sense=salt_sense, east_sense=east_sense, north_sense=north_sense, surface_sense=surface_sense)


advect_rate = 0.2
gravity_step = 0.25
flux_step = 1.0
stiffness = 2.0


def rotate(east_part, north_part, frame_code):
    cos_factor = (frame_code == 0).astype(jnp.float32) - (frame_code == 2).astype(jnp.float32)
    sin_factor = (frame_code == 1).astype(jnp.float32) - (frame_code == 3).astype(jnp.float32)
    return cos_factor * east_part - sin_factor * north_part, sin_factor * east_part + cos_factor * north_part


def unrotate(east_part, north_part, frame_code):
    cos_factor = (frame_code == 0).astype(jnp.float32) - (frame_code == 2).astype(jnp.float32)
    sin_factor = (frame_code == 1).astype(jnp.float32) - (frame_code == 3).astype(jnp.float32)
    return cos_factor * east_part + sin_factor * north_part, cos_factor * north_part - sin_factor * east_part


def level_mask(depth_values, levels):
    level_index = jnp.arange(levels).astype(jnp.float32)
    return (level_index[:, None, None] < depth_values[None]).astype(jnp.float32)


def face_weights(depth_pad, levels):
    opened = (depth_pad > 0).astype(jnp.float32)
    rows_depth = depth_pad[1:-1, :]
    rows_open = opened[1:-1, :]
    weight_east = stiffness * rows_open[:, :-1] * rows_open[:, 1:] * jnp.minimum(rows_depth[:, :-1], rows_depth[:, 1:]) / levels
    cols_depth = depth_pad[:, 1:-1]
    cols_open = opened[:, 1:-1]
    weight_north = stiffness * cols_open[:-1] * cols_open[1:] * jnp.minimum(cols_depth[:-1], cols_depth[1:]) / levels
    return weight_east, weight_north


def apply_operator(padded, weight_east, weight_north):
    center = padded[1:-1, 1:-1]
    result = center + weight_east[:, 1:] * (center - padded[1:-1, 2:])
    result = result + weight_east[:, :-1] * (center - padded[1:-1, :-2])
    result = result + weight_north[1:, :] * (center - padded[2:, 1:-1])
    return result + weight_north[:-1, :] * (center - padded[:-2, 1:-1])


def divergence(east_pad, north_pad, depth_pad):
    opened = (depth_pad > 0).astype(jnp.float32)
    gate_east = opened[1:-1, :-1] * opened[1:-1, 1:]
    gate_north = opened[:-1, 1:-1] * opened[1:, 1:-1]
    flux_east = gate_east * 0.5 * (east_pad[1:-1, :-1] + east_pad[1:-1, 1:])
    flux_north = gate_north * 0.5 * (north_pad[:-1, 1:-1] + north_pad[1:, 1:-1])
    return (flux_east[:, 1:] - flux_east[:, :-1]) + (flux_north[1:] - flux_north[:-1])


def transport_adjoint(sense_pad, depth_pad):
    opened = (depth_pad > 0).astype(jnp.float32)
    gate_east = opened[1:-1, :-1] * opened[1:-1, 1:]
    gate_north = opened[:-1, 1:-1] * opened[1:, 1:-1]
    grad_east = flux_step * (sense_pad[1:-1, 1:] - sense_pad[1:-1, :-1]) * gate_east
    grad_north = flux_step * (sense_pad[1:, 1:-1] - sense_pad[:-1, 1:-1]) * gate_north
    return 0.5 * (grad_east[:, 1:] + grad_east[:, :-1]), 0.5 * (grad_north[1:] + grad_north[:-1])


def advect_adjoint(value_pad, sense_pad, velocity_pad, mask_pad, along_axis):
    span_size = value_pad.shape[along_axis] - 4

    def cut_span(values, offset, length_cut):
        return lax.slice_in_dim(values, offset, offset + length_cut, axis=along_axis)

    face_count = span_size + 3
    inner_count = span_size + 1
    face_mask = cut_span(mask_pad, 0, face_count) * cut_span(mask_pad, 1, face_count)
    face_vel = 0.5 * (cut_span(velocity_pad, 0, face_count) + cut_span(velocity_pad, 1, face_count))
    face_sense = advect_rate * (cut_span(sense_pad, 1, face_count) - cut_span(sense_pad, 0, face_count)) * face_mask
    value_sense = face_sense * face_vel
    face_value = (7.0 / 12.0) * (cut_span(value_pad, 1, inner_count) + cut_span(value_pad, 2, inner_count)) - (1.0 / 12.0) * (cut_span(value_pad, 0, inner_count) + cut_span(value_pad, 3, inner_count))
    vel_sense = cut_span(face_sense, 1, inner_count) * face_value
    value_back = (7.0 / 12.0) * (cut_span(value_sense, 2, span_size) + cut_span(value_sense, 1, span_size)) - (1.0 / 12.0) * (cut_span(value_sense, 3, span_size) + cut_span(value_sense, 0, span_size))
    velocity_back = 0.5 * (cut_span(vel_sense, 1, span_size) + cut_span(vel_sense, 0, span_size))
    return value_back, velocity_back


def tracer_adjoint(value_east, value_north, sense_east, sense_north, east_vel, north_vel, mask_east, mask_north, sense_here, east_axis):
    back_east, east_part = advect_adjoint(value_east, sense_east, east_vel, mask_east, east_axis)
    back_north, north_part = advect_adjoint(value_north, sense_north, north_vel, mask_north, east_axis - 1)
    return sense_here + back_east + back_north, east_part, north_part


def pad_surface(surface):
    return jnp.pad(surface, ((1, 1), (1, 1)))


def conjugate(operator, source, iterate):
    residual = source - operator(iterate)
    search = residual
    norm_now = jnp.sum(residual * residual)
    for iteration in range(ITERS):
        applied = operator(search)
        step_size = norm_now / jnp.sum(search * applied)
        iterate = iterate + step_size * search
        if iteration + 1 < ITERS:
            residual = residual - step_size * applied
            norm_next = jnp.sum(residual * residual)
            search = residual + (norm_next / norm_now) * search
            norm_now = norm_next
    return iterate


def level_work(slices):
    theta_level, salt_level, theta_sense_level, salt_sense_level, east_level, north_level, mask_level = slices

    def pad_east(values):
        return jnp.pad(values, ((0, 0), (2, 2)))

    def pad_north(values):
        return jnp.pad(values, ((2, 2), (0, 0)))

    east_vel = pad_east(east_level)
    north_vel = pad_north(north_level)
    mask_east = pad_east(mask_level)
    mask_north = pad_north(mask_level)
    theta_back, east_theta, north_theta = tracer_adjoint(pad_east(theta_level), pad_north(theta_level), pad_east(theta_sense_level), pad_north(theta_sense_level), east_vel, north_vel, mask_east, mask_north, theta_sense_level, 1)
    salt_back, east_salt, north_salt = tracer_adjoint(pad_east(salt_level), pad_north(salt_level), pad_east(salt_sense_level), pad_north(salt_sense_level), east_vel, north_vel, mask_east, mask_north, salt_sense_level, 1)
    return theta_back, salt_back, east_theta + east_salt, north_theta + north_salt


def reference(theta_start, salt_start, east_velocity, north_velocity, surface_start, wet_levels, face_frame, theta_sense, salt_sense, east_sense, north_sense, surface_sense):
    depth_field = wet_levels.astype(jnp.float32)
    wet_mask = level_mask(depth_field, L)
    east_glob, north_glob = rotate(east_velocity, north_velocity, face_frame)
    depth_pad = pad_surface(depth_field)
    weight_east, weight_north = face_weights(depth_pad, L)

    def operator(surface):
        return apply_operator(pad_surface(surface), weight_east, weight_north)

    east_transport = pad_surface(jnp.sum(wet_mask * east_glob, axis=0))
    north_transport = pad_surface(jnp.sum(wet_mask * north_glob, axis=0))
    source = surface_start - flux_step * divergence(east_transport, north_transport, depth_pad)
    surface_end = conjugate(operator, source, surface_start)
    end_pad = pad_surface(surface_end)
    east_end = wet_mask * (east_glob - gravity_step * 0.5 * (end_pad[1:-1, 2:] - end_pad[1:-1, :-2]))
    north_end = wet_mask * (north_glob - gravity_step * 0.5 * (end_pad[2:, 1:-1] - end_pad[:-2, 1:-1]))
    theta_adjoint, salt_adjoint, east_advect, north_advect = lax.map(level_work, (theta_start, salt_start, theta_sense, salt_sense, east_end, north_end, wet_mask))
    east_rotated, north_rotated = rotate(east_sense, north_sense, face_frame)
    east_total = east_rotated + east_advect
    north_total = north_rotated + north_advect
    east_column = pad_surface(jnp.sum(wet_mask * east_total, axis=0))
    north_column = pad_surface(jnp.sum(wet_mask * north_total, axis=0))
    surface_total = surface_sense + gravity_step * 0.5 * ((east_column[1:-1, 2:] - east_column[1:-1, :-2]) + (north_column[2:, 1:-1] - north_column[:-2, 1:-1]))
    surface_adjoint = conjugate(operator, surface_total, jnp.zeros_like(surface_total))
    back_east, back_north = transport_adjoint(pad_surface(surface_adjoint), depth_pad)
    east_grid = wet_mask * (east_total + back_east)
    north_grid = wet_mask * (north_total + back_north)
    east_adjoint, north_adjoint = unrotate(east_grid, north_grid, face_frame)
    return theta_adjoint, salt_adjoint, east_adjoint, north_adjoint, surface_adjoint
```

```python
import functools

import jax
import jax.numpy as jnp
from jax import lax
from jax.experimental import pallas as pl
from jax.experimental.pallas import tpu as pltpu
from jax.sharding import PartitionSpec as P

F32 = jnp.float32
LEVELS = 32
ROWS = 16
COLS = 256
WIDE = 384
TALL = 32
CHUNK = 8
STEPS = LEVELS // CHUNK
FIELDS = 7
D, X0, TE, TN, SS, CE, CN = range(FIELDS)
Y2D = 320
YE = Y2D + 8 * FIELDS
YROWS = YE + 16
XROWS = 112

RATE = 0.2
GRAVITY = 0.25
STIFF = 2.0 / LEVELS
K7 = 0.5 * RATE * 7.0 / 12.0
K1 = 0.5 * RATE / 12.0
ALL = ("ty", "tx")


def roll(x, shift, axis):
    return pltpu.roll(x, shift % x.shape[axis], axis)


def iota(shape, axis):
    return lax.broadcasted_iota(jnp.int32, shape, axis)


def frame(q_ref):
    q = q_ref[0:1, 0:1]
    one = jnp.ones((1, 1), F32)
    zero = jnp.zeros((1, 1), F32)
    cos = jnp.where(q == 0, one, zero) - jnp.where(q == 2, one, zero)
    sin = jnp.where(q == 1, one, zero) - jnp.where(q == 3, one, zero)
    return cos, sin


def face_levels(lev):
    lane = iota((ROWS, COLS), 1)
    row = iota((ROWS, COLS), 0)
    east = jnp.where(lane < COLS - 1, jnp.minimum(lev, roll(lev, -1, 1)), 0)
    north = jnp.where(row < ROWS - 1, jnp.minimum(lev, roll(lev, -1, 0)), 0)
    return east, north


def local_kernel(c1, c2, b1_in, b2_in, u_in, v_in, es_in, ns_in, lev_in, q_in, x0_in, ss_in,
                 yup, ydn, f2d, edges, et, nt, b1, b2, u, v, lev_ref, q_ref, t1, t2, es, ns,
                 x0_ref, ss_ref, sems, small_sems):
    small = ((q_in, q_ref), (lev_in, lev_ref), (x0_in, x0_ref), (ss_in, ss_ref))
    small = [pltpu.make_async_copy(a, b, small_sems.at[n]) for n, (a, b) in enumerate(small)]
    for c in small:
        c.start()
    moves = ((c1, t1), (c2, t2), (b1_in, b1), (b2_in, b2), (u_in, u), (v_in, v), (es_in, es), (ns_in, ns))

    def copy(n, g):
        at = pl.ds(g * CHUNK * ROWS, CHUNK * ROWS)
        return pltpu.make_async_copy(moves[n][0].at[at, :], moves[n][1].at[at, :], sems.at[n, g])

    for g in range(STEPS):
        for n in range(8):
            copy(n, g).start()
    for c in small:
        c.wait()
    cos, sin = frame(q_ref)
    lev = lev_ref[...]
    east_lev, north_lev = face_levels(lev)
    lane = iota((ROWS, COLS), 1)
    row = iota((ROWS, COLS), 0)
    lane128 = iota((ROWS, 128), 1)
    em = jnp.where(lane == 0, 0.0, -K1)
    ep = jnp.where(lane >= COLS - 2, 0.0, -K1)
    nm = jnp.where(row == 0, 0.0, -K1)
    np_ = jnp.where(row >= ROWS - 2, 0.0, -K1)
    line8 = iota((CHUNK, COLS), 0)
    f2d[...] = jnp.zeros_like(f2d)
    edges[...] = jnp.zeros_like(edges)

    def field(f):
        return slice(f * ROWS, (f + 1) * ROWS)

    def step(g, carry):
        for n in range(8):
            copy(n, g).wait()
        acc_u = jnp.zeros((ROWS, COLS), F32)
        acc_v = jnp.zeros((ROWS, COLS), F32)
        acc_e = jnp.zeros((ROWS, COLS), F32)
        acc_n = jnp.zeros((ROWS, COLS), F32)
        packs = [jnp.zeros((ROWS, 128), F32) for _ in range(5)]
        rows_at = pl.multiple_of(g * (CHUNK * ROWS), CHUNK * ROWS)
        for kk in range(CHUNK):
            k = g * CHUNK + kk
            here = pl.ds(rows_at + kk * ROWS, ROWS)
            m = lev > k
            me = east_lev > k
            mn = north_lev > k
            ve = None
            vn = None
            values = []
            for c_ref, b_ref in ((t1, b1), (t2, b2)):
                c = c_ref[here, :]
                b = b_ref[here, :]
                values.append((c, b))
                fe = jnp.where(me, roll(b, -1, 1) - b, 0.0)
                fn = jnp.where(mn, roll(b, -1, 0) - b, 0.0)
                ve_t = fe * (K7 * (c + roll(c, -1, 1)) + em * roll(c, 1, 1) + ep * roll(c, -2, 1))
                vn_t = fn * (K7 * (c + roll(c, -1, 0)) + nm * roll(c, 1, 0) + np_ * roll(c, -2, 0))
                ve = ve_t if ve is None else ve + ve_t
                vn = vn_t if vn is None else vn + vn_t
            es_k = es[here, :]
            ns_k = ns[here, :]
            u_k = u[here, :]
            v_k = v[here, :]
            et_k = cos * es_k - sin * ns_k + (ve + roll(ve, 1, 1))
            nt_k = sin * es_k + cos * ns_k + (vn + roll(vn, 1, 0))
            et[here, :] = et_k
            nt[here, :] = nt_k
            acc_e = acc_e + jnp.where(m, et_k, 0.0)
            acc_n = acc_n + jnp.where(m, nt_k, 0.0)
            acc_u = acc_u + jnp.where(m, u_k, 0.0)
            acc_v = acc_v + jnp.where(m, v_k, 0.0)

            def ends(x):
                return jnp.where(lane128 < 2, x[:, :128], x[:, 128:])

            spot = (lane128 // 4) == kk
            packed = [ends(values[0][0]), ends(values[1][0]), ends(values[0][1]), ends(values[1][1])]
            packed.append(cos * ends(u_k) - sin * ends(v_k))
            for n in range(5):
                packs[n] = jnp.where(spot, roll(packed[n], 4 * kk + 2, 1), packs[n])

        for n in range(5):
            at = slice(n * ROWS, (n + 1) * ROWS)
            edges[at, :] = edges[at, :] + pltpu.roll(packs[n], g * (4 * CHUNK), 1)
        f2d[field(TE), :] = f2d[field(TE), :] + (cos * acc_u - sin * acc_v)
        f2d[field(TN), :] = f2d[field(TN), :] + (sin * acc_u + cos * acc_v)
        f2d[field(CE), :] = f2d[field(CE), :] + acc_e
        f2d[field(CN), :] = f2d[field(CN), :] + acc_n

        for out, first in ((yup, ROWS - 2), (ydn, 0)):
            for r in range(2):
                def rows_of(ref):
                    got = jnp.zeros((CHUNK, COLS), F32)
                    block = ref.at[pl.ds(rows_at, CHUNK * ROWS), :]
                    for kk in range(CHUNK):
                        at = kk * ROWS + first + r
                        got = jnp.where(line8 == kk, block[at : at + 1, :], got)
                    return got

                picked = [rows_of(ref) for ref in (t1, t2, b1, b2)]
                picked.append(sin * rows_of(u) + cos * rows_of(v))
                for a in range(5):
                    at = pl.multiple_of((2 * a + r) * LEVELS + g * CHUNK, CHUNK)
                    out[pl.ds(at, CHUNK), :] = picked[a]
        return carry

    lax.fori_loop(0, STEPS, step, 0)
    f2d[field(D), :] = lev.astype(F32)
    f2d[field(X0), :] = x0_ref[...]
    f2d[field(SS), :] = ss_ref[...]
    for out, first in ((yup, 8), (ydn, 0)):
        for f in range(FIELDS):
            out[Y2D + 8 * f : Y2D + 8 * f + 8, :] = f2d[f * ROWS + first : f * ROWS + first + 8, :]
        for n in range(4):
            at = YE + 8 * (n // 2)
            side = 128 * (n % 2)
            out[at : at + 8, side : side + 128] = edges[n * ROWS + first : n * ROWS + first + 8, :]


def across(f, up, down, axis):
    return K7 * (f + roll(f, 1, axis)) + (up * roll(f, -1, axis) + down * roll(f, 2, axis))


def trims():
    lane = iota((ROWS, COLS), 1)
    row = iota((ROWS, COLS), 0)
    return (jnp.where(lane == COLS - 1, 0.0, -K1), jnp.where(lane == 0, 0.0, -K1),
            jnp.where(row == ROWS - 1, 0.0, -K1), jnp.where(row == 0, 0.0, -K1))


def row_boundary(low, high, lev_a2, lev_a1, lev_b1, lev_b2):
    level = iota((LEVELS, COLS), 0).astype(F32)
    mask_a = level < jnp.minimum(lev_a2, lev_a1)
    mask_0 = level < jnp.minimum(lev_a1, lev_b1)
    mask_b = level < jnp.minimum(lev_b1, lev_b2)

    def part(ref, a, r):
        return ref[(2 * a + r) * LEVELS : (2 * a + r + 1) * LEVELS, :]

    va = v0 = vb = None
    diffs = []
    for t in range(2):
        ca2, ca1 = part(low, t, 0), part(low, t, 1)
        cb1, cb2 = part(high, t, 0), part(high, t, 1)
        ga2, ga1 = part(low, 2 + t, 0), part(low, 2 + t, 1)
        gb1, gb2 = part(high, 2 + t, 0), part(high, 2 + t, 1)
        fa = jnp.where(mask_a, ga1 - ga2, 0.0)
        f0 = jnp.where(mask_0, gb1 - ga1, 0.0)
        fb = jnp.where(mask_b, gb2 - gb1, 0.0)
        diffs.append((fa, f0, fb))
        fa = fa * (-K1 * cb1)
        f0 = f0 * (K7 * (ca1 + cb1) - K1 * (ca2 + cb2))
        fb = fb * (-K1 * ca1)
        va = fa if va is None else va + fa
        v0 = f0 if v0 is None else v0 + f0
        vb = fb if vb is None else vb + fb
    vel = [part(low, 4, 0), part(low, 4, 1), part(high, 4, 0), part(high, 4, 1)]
    return va, va + v0, v0 + vb, vb, diffs, vel


def rows_kernel(ylo, yhi, yup, ydn, f2d, edges, xr, xl, ext, edges_ext, nt_fix, row_seam):
    d0 = f2d[0:1, :]
    d1 = f2d[1:2, :]
    d14 = f2d[ROWS - 2 : ROWS - 1, :]
    d15 = f2d[ROWS - 1 : ROWS, :]
    lo = row_boundary(ylo, ydn, ylo[Y2D + 6 : Y2D + 7, :], ylo[Y2D + 7 : Y2D + 8, :], d0, d1)
    hi = row_boundary(yup, yhi, d14, d15, yhi[Y2D : Y2D + 1, :], yhi[Y2D + 1 : Y2D + 2, :])
    for side, (out, at) in enumerate(((lo, 0), (hi, 1))):
        diffs, vel = out[4], out[5]
        for i in range(2):
            spot = (6 * side + i) * LEVELS
            row_seam[spot : spot + LEVELS, :] = vel[at + i] + vel[at + i + 1]
            for t in range(2):
                spot = (6 * side + 2 + 2 * t + i) * LEVELS
                row_seam[spot : spot + LEVELS, :] = diffs[t][at + i]
    for n, value in enumerate((lo[2], lo[3], hi[0], hi[1])):
        nt_fix[n * LEVELS : (n + 1) * LEVELS, :] = value
    for f in range(FIELDS):
        ext[f * TALL : f * TALL + ROWS, :] = f2d[f * ROWS : (f + 1) * ROWS, :]
        ext[f * TALL + 16 : f * TALL + 24, :] = yhi[Y2D + 8 * f : Y2D + 8 * f + 8, :]
        ext[f * TALL + 24 : f * TALL + 32, :] = ylo[Y2D + 8 * f : Y2D + 8 * f + 8, :]
    spots = ((30, lo[0]), (31, lo[1]), (0, lo[2]), (1, lo[3]),
             (14, hi[0]), (15, hi[1]), (16, hi[2]), (17, hi[3]))
    for r, value in spots:
        at = slice(CN * TALL + r, CN * TALL + r + 1)
        ext[at, :] = ext[at, :] + jnp.sum(value, axis=0, keepdims=True)
    for n in range(4):
        at = YE + 8 * (n // 2)
        side = 128 * (n % 2)
        edges_ext[n * TALL : n * TALL + ROWS, :] = edges[n * ROWS : (n + 1) * ROWS, :]
        edges_ext[n * TALL + 16 : n * TALL + 24, :] = yhi[at : at + 8, side : side + 128]
        edges_ext[n * TALL + 24 : n * TALL + 32, :] = ylo[at : at + 8, side : side + 128]
    lane = iota((TALL, 128), 1)
    pr = jnp.zeros((TALL, 128), F32)
    pl_ = jnp.zeros((TALL, 128), F32)
    for f in range(FIELDS):
        spot = (lane // 8) == f
        z = ext[f * TALL : (f + 1) * TALL, :]
        pr = jnp.where(spot, roll(z[:, 128:], 8 * f + 8, 1), pr)
        pl_ = jnp.where(spot, roll(z[:, :128], 8 * f, 1), pl_)
    xr[0:TALL, :] = pr
    xl[0:TALL, :] = pl_
    first = (lane % 4) < 2
    for pair in range(2):
        p = edges_ext[2 * pair * TALL : (2 * pair + 1) * TALL, :]
        s = edges_ext[(2 * pair + 1) * TALL : (2 * pair + 2) * TALL, :]
        at = slice((1 + pair) * TALL, (2 + pair) * TALL)
        xr[at, :] = jnp.where(first, p, roll(s, 2, 1))
        xl[at, :] = jnp.where(first, roll(s, -2, 1), p)
    xr[96:112, :] = edges[4 * ROWS : 5 * ROWS, :]
    xl[96:112, :] = edges[4 * ROWS : 5 * ROWS, :]


def spread(x):
    lane = iota(x.shape, 1)
    x = jnp.where(lane < 4, x, 0.0)
    for s in (4, 8, 16, 32, 64):
        x = x + roll(x, s, 1)
    return x


def seam(left_tile, right_tile):
    lane = iota(left_tile.shape, 1)
    return roll(jnp.where(lane >= 126, left_tile, right_tile), 2, 1)


def joined(lo_ref, hi_ref, edges_ext, pair, which, rows):
    own = edges_ext[(2 * pair + which) * TALL : (2 * pair + which) * TALL + rows, :]
    first = (iota((rows, 128), 1) % 4) < 2
    at = slice((1 + pair) * TALL, (1 + pair) * TALL + rows)
    lo = lo_ref[at, :]
    hi = hi_ref[at, :]
    if which == 1:
        lo = roll(lo, -2, 1)
        hi = roll(hi, 2, 1)
    return jnp.where(first, lo, own), jnp.where(first, own, hi)


def columns_kernel(xlo, xhi, ext, edges_ext, edges, he, hn, basis, et_fix, lane_seam, moments):
    lane = iota((TALL, 128), 1)
    group = lane % 4
    level = (lane // 4).astype(F32)
    tiles = []
    for f in range(FIELDS):
        z = ext[f * TALL : (f + 1) * TALL, :]
        right = roll(xhi[0:TALL, :], -8 * f, 1)
        left = roll(xlo[0:TALL, :], 120 - 8 * f, 1)
        third = jnp.where(lane < 8, right, jnp.where(lane >= 120, left, 0.0))
        tiles.append([z[:, :128], z[:, 128:], third])
    coef7 = jnp.where(group == 1, K7, 0.0)
    coefm = jnp.where((group == 1) | (group == 2), -K1, 0.0)
    coefp = jnp.where(group < 2, -K1, 0.0)
    cells = []
    for side in range(2):
        d = tiles[D]
        lev = spread(seam(d[2], d[0]) if side == 0 else seam(d[1], d[2]))
        wet = (level < jnp.minimum(lev, roll(lev, -1, 1))) & (group < 3)
        w = None
        for t in range(2):
            c = joined(xlo, xhi, edges_ext, 0, t, TALL)[side]
            b = joined(xlo, xhi, edges_ext, 1, t, TALL)[side]
            f = jnp.where(wet, roll(b, -1, 1) - b, 0.0)
            spot = (3 * side + 1 + t) * ROWS
            lane_seam[spot : spot + ROWS, :] = f[0:ROWS, :]
            term = f * (coef7 * (c + roll(c, -1, 1)) + coefm * roll(c, 1, 1) + coefp * roll(c, -2, 1))
            w = term if w is None else w + term
        cell = w + roll(w, 1, 1)
        cells.append(cell)
        total = cell
        for s in (4, 8, 16, 32, 64):
            total = total + roll(total, s, 1)
        total = roll(total, -2, 1)
        a, b = (2, 0) if side == 0 else (1, 2)
        tiles[CE][a] = tiles[CE][a] + jnp.where(lane >= 126, total, 0.0)
        tiles[CE][b] = tiles[CE][b] + jnp.where(lane < 2, total, 0.0)
    et_fix[...] = jnp.where(group < 2, cells[1], cells[0])[0:ROWS, :]
    own_u = edges[4 * ROWS : 5 * ROWS, :]
    half = group[0:ROWS, :] < 2
    for side, uu in enumerate((jnp.where(half, xlo[96:112, :], own_u), jnp.where(half, own_u, xhi[96:112, :]))):
        lane_seam[3 * side * ROWS : (3 * side + 1) * ROWS, :] = uu + roll(uu, -1, 1)

    full = [jnp.concatenate(t, axis=1) for t in tiles]
    d = full[D]
    near_e = jnp.minimum(d, roll(d, -1, 1))
    near_n = jnp.minimum(d, roll(d, -1, 0))
    we = STIFF * near_e
    wn = STIFF * near_n
    half_e = jnp.where(near_e > 0.0, 0.5, 0.0)
    half_n = jnp.where(near_n > 0.0, 0.5, 0.0)
    x0 = full[X0]
    flux_e = half_e * (full[TE] + roll(full[TE], -1, 1)) + we * (x0 - roll(x0, -1, 1))
    flux_n = half_n * (full[TN] + roll(full[TN], -1, 0)) + wn * (x0 - roll(x0, -1, 0))
    r = (roll(flux_e, 1, 1) - flux_e) + (roll(flux_n, 1, 0) - flux_n)
    b = full[SS] + (0.5 * GRAVITY) * (
        (roll(full[CE], -1, 1) - roll(full[CE], 1, 1)) + (roll(full[CN], -1, 0) - roll(full[CN], 1, 0))
    )

    def own_sum(x):
        part = x[0:ROWS, 0:128] + x[0:ROWS, 128:256]
        return jnp.sum(part, axis=0, keepdims=True)

    sums = []
    for n, start in enumerate((r, b)):
        vec = start
        for power in range(3):
            basis[(4 * n + power) * TALL : (4 * n + power + 1) * TALL, :] = vec
            sums.append(own_sum(vec * vec))
            de = vec - roll(vec, -1, 1)
            dn = vec - roll(vec, -1, 0)
            he = we * de
            hn = wn * dn
            sums.append(own_sum(he * de + hn * dn))
            if power < 2:
                vec = (he - roll(he, 1, 1)) + (hn - roll(hn, 1, 0))
    basis[3 * TALL : 4 * TALL, :] = x0
    basis[7 * TALL : 8 * TALL, :] = d
    spot_lane = iota((1, 128), 1)
    line = jnp.zeros((1, 128), F32)
    for n, s in enumerate(sums):
        line = line + jnp.where(spot_lane == n, jnp.sum(s, axis=1, keepdims=True), 0.0)
    moments[...] = jnp.broadcast_to(line, (128, 128))


def safe_ratio(top, bottom, limit):
    ok = bottom > 0.0
    return jnp.clip(jnp.where(ok, top / jnp.where(ok, bottom, 1.0), 0.0), 0.0, limit)


def solve_small(m):
    bound = 8.0 * STIFF * LEVELS
    a0 = m[1] / m[0]
    n1 = m[2] - a0 * m[1]
    b1 = safe_ratio(n1, m[0], bound * bound)
    a1 = safe_ratio(m[3] - a0 * (2.0 * m[2] - a0 * m[1]), n1, bound)
    s = a0 + a1
    t = a0 * a1 - b1
    n2 = m[4] - s * m[3] + t * m[2]
    b2 = safe_ratio(n2, n1, bound * bound)
    top = m[5] - 2.0 * s * m[4] + (s * s + 2.0 * t) * m[3] - 2.0 * s * t * m[2] + t * t * m[1]
    a2 = safe_ratio(top, n2, bound)
    e2 = 1.0 + a2
    e1 = jnp.maximum(1.0 + a1 - b2 / e2, 1.0)
    e0 = jnp.maximum(1.0 + a0 - b1 / e1, 1.0)
    y0 = 1.0 / e0
    y1 = -y0 / e1
    y2 = -y1 / e2
    return y0 - a0 * y1 + t * y2, y1 - s * y2, y2


def vec(ref, n):
    return ref[n * TALL : (n + 1) * TALL, :]


def prepare_kernel(u, v, q_ref, he, hn):
    cos, sin = frame(q_ref)

    def step(g, carry):
        for kk in range(4):
            here = pl.ds(pl.multiple_of(g * (4 * ROWS), 4 * ROWS) + kk * ROWS, ROWS)
            east = cos * u[here, :] - sin * v[here, :]
            north = sin * u[here, :] + cos * v[here, :]
            he[here, :] = east + roll(east, -1, 1)
            hn[here, :] = north + roll(north, -1, 0)
        return carry

    lax.fori_loop(0, LEVELS // 4, step, 0)


def final_kernel(mom, basis, row_seam, nt_fix, lane_seam, et_fix, lev_ref, q_ref, b1, b2, he_ref, hn_ref,
                 et, nt, th_out, sa_out, ea_out, na_out, xb,
                 row_fix, lane_fix, th, sa, ea, na, out_sems):
    outs = ((th, th_out), (sa, sa_out), (ea, ea_out), (na, na_out))

    def put(n, g):
        at = pl.ds(g * CHUNK * ROWS, CHUNK * ROWS)
        return pltpu.make_async_copy(outs[n][0].at[at, :], outs[n][1].at[at, :], out_sems.at[n, g])

    cos, sin = frame(q_ref)
    lev = lev_ref[...]
    lane = iota((ROWS, COLS), 1)
    line = jnp.sum(mom[...], axis=0, keepdims=True)
    spot = iota((1, 128), 1)
    m = [jnp.sum(jnp.where(spot == n, line, 0.0), axis=1, keepdims=True) for n in range(12)]
    cf = solve_small(m[0:6])
    cb = solve_small(m[6:12])
    end = vec(basis, 3) + (cf[0] * vec(basis, 0) + cf[1] * vec(basis, 1) + cf[2] * vec(basis, 2))
    adj = cb[0] * vec(basis, 4) + cb[1] * vec(basis, 5) + cb[2] * vec(basis, 6)
    d = vec(basis, 7)
    xb[...] = adj[0:ROWS, 0:COLS]
    ge = (0.5 * GRAVITY) * (roll(end, -1, 1) - roll(end, 1, 1))
    gn = (0.5 * GRAVITY) * (roll(end, -1, 0) - roll(end, 1, 0))
    wide_e = ge + roll(ge, -1, 1)
    wide_n = gn + roll(gn, -1, 0)
    sum_e = wide_e[0:ROWS, 0:COLS]
    sum_n = wide_n[0:ROWS, 0:COLS]
    fe = jnp.where(jnp.minimum(d, roll(d, -1, 1)) > 0.0, 0.5 * (roll(adj, -1, 1) - adj), 0.0)
    fn = jnp.where(jnp.minimum(d, roll(d, -1, 0)) > 0.0, 0.5 * (roll(adj, -1, 0) - adj), 0.0)
    be = (fe + roll(fe, 1, 1))[0:ROWS, 0:COLS]
    bn = (fn + roll(fn, 1, 0))[0:ROWS, 0:COLS]

    for side, first in enumerate((-2, 15)):
        vel = []
        for i in range(2):
            r = (first + i) % TALL
            vel.append(row_seam[(6 * side + i) * LEVELS : (6 * side + i + 1) * LEVELS, :] - wide_n[r : r + 1, 0:COLS])
        for t in range(2):
            spots = [(6 * side + 2 + 2 * t + i) * LEVELS for i in range(2)]
            qa, qb = [row_seam[s : s + LEVELS, :] * w for s, w in zip(spots, vel)]
            values = (K7 * qb - K1 * qa, -K1 * qb) if side == 0 else (-K1 * qa, K7 * qa - K1 * qb)
            for i in range(2):
                at = (4 * t + 2 * side + i) * LEVELS
                row_fix[at : at + LEVELS, :] = values[i]
    group = iota((ROWS, 128), 1) % 4
    tiles = [wide_e[0:ROWS, 128 * n : 128 * n + 128] for n in range(3)]
    for side in range(2):
        gg = spread(seam(tiles[2], tiles[0]) if side == 0 else seam(tiles[1], tiles[2]))
        vel = lane_seam[3 * side * ROWS : (3 * side + 1) * ROWS, :] - gg
        keep = (group < 2) if side == 0 else ((group == 1) | (group == 2))
        for t in range(2):
            spot = (3 * side + 1 + t) * ROWS
            f = jnp.where(keep, lane_seam[spot : spot + ROWS, :] * vel, 0.0)
            at = slice(t * ROWS, (t + 1) * ROWS)
            if side == 0:
                fix = jnp.where(group == 2, K7 * roll(f, 1, 1), 0.0) - K1 * roll(f, 2, 1)
                lane_fix[at, :] = jnp.where(group >= 2, fix, 0.0)
            else:
                fix = jnp.where(group == 1, K7 * f, 0.0) - K1 * roll(f, -1, 1)
                lane_fix[at, :] = jnp.where(group < 2, fix, lane_fix[at, :])

    east_lev, north_lev = face_levels(lev)
    ep, em, np_, nm = trims()
    edge = (lane < 2) | (lane >= COLS - 2)
    line8 = iota((8, COLS), 0)

    def step(g, carry):
        turn = 128 - g * (4 * CHUNK)
        packs = [lane_fix[0:ROWS, :], lane_fix[ROWS : 2 * ROWS, :], et_fix[...]]
        packs = [pltpu.roll(p, turn, 1) for p in packs]

        def fix_rows(ref, n):
            return ref.at[pl.ds(pl.multiple_of(n * LEVELS + g * CHUNK, CHUNK), CHUNK), :]

        fixes = [[fix_rows(row_fix, n) for n in range(4)], [fix_rows(row_fix, 4 + n) for n in range(4)],
                 [fix_rows(nt_fix, n) for n in range(4)]]
        rows_at = pl.multiple_of(g * (CHUNK * ROWS), CHUNK * ROWS)
        for kk in range(CHUNK):
            k = g * CHUNK + kk
            here = pl.ds(rows_at + kk * ROWS, ROWS)
            m = lev > k
            me = east_lev > k
            mn = north_lev > k

            def lane_fixed(x, n):
                z = roll(packs[n], -(4 * kk + 2), 1)
                return jnp.where(edge, x + jnp.concatenate([z, z], axis=1), x)

            def row_fixed(x, n):
                r0, r1, r14, r15 = [f[kk : kk + 1, :] for f in fixes[n]]
                top = jnp.where(line8 == 0, r0, jnp.where(line8 == 1, r1, 0.0))
                low = jnp.where(line8 == 6, r14, jnp.where(line8 == 7, r15, 0.0))
                return x + jnp.concatenate([top, low], axis=0)

            he = he_ref[here, :] - sum_e
            hn = hn_ref[here, :] - sum_n
            for n, (b_ref, out) in enumerate(((b1, th), (b2, sa))):
                b = b_ref[here, :]
                fe = jnp.where(me, roll(b, -1, 1) - b, 0.0)
                fn = jnp.where(mn, roll(b, -1, 0) - b, 0.0)
                x = b + across(fe * he, ep, em, 1) + across(fn * hn, np_, nm, 0)
                out[here, :] = row_fixed(lane_fixed(x, n), n)
            eg = jnp.where(m, lane_fixed(et[here, :], 2) + be, 0.0)
            ng = jnp.where(m, row_fixed(nt[here, :], 2) + bn, 0.0)
            ea[here, :] = cos * eg + sin * ng
            na[here, :] = cos * ng - sin * eg
        for n in range(4):
            put(n, g).start()
        return carry

    lax.fori_loop(0, STEPS, step, 0)
    for g in range(STEPS):
        for n in range(4):
            put(n, g).wait()


def params(mib):
    return pltpu.CompilerParams(vmem_limit_bytes=mib * 1024 * 1024)


def far(x):
    return pltpu.with_memory_space_constraint(x, pltpu.HBM)


def sds(*shape):
    return jax.ShapeDtypeStruct(shape, F32)


def on_device(theta_start, salt_start, east_velocity, north_velocity, surface_start, wet_levels,
              face_frame, theta_sense, salt_sense, east_sense, north_sense, surface_sense):
    flat = lambda x: x.reshape(LEVELS * ROWS, COLS)
    c1, c2, u, v = map(flat, (theta_start, salt_start, east_velocity, north_velocity))
    b1, b2, es, ns = map(flat, (theta_sense, salt_sense, east_sense, north_sense))
    vol = sds(LEVELS * ROWS, COLS)
    c1, c2, b1, b2, u, v, es, ns = [far(x) for x in (c1, c2, b1, b2, u, v, es, ns)]
    hbm = pl.BlockSpec(memory_space=pltpu.HBM)
    vmem = pl.BlockSpec(memory_space=pltpu.VMEM)
    cubes = pltpu.VMEM((LEVELS * ROWS, COLS), F32)
    sems = lambda n: pltpu.SemaphoreType.DMA((n, STEPS))
    yup, ydn, f2d, edges, et, nt, b1, b2, u, v, lev, turns = pl.pallas_call(
        local_kernel,
        in_specs=[hbm] * 12,
        out_specs=[vmem] * 12,
        out_shape=[sds(YROWS, COLS), sds(YROWS, COLS), sds(FIELDS * ROWS, COLS), sds(5 * ROWS, 128)] + [vol] * 6
        + [jax.ShapeDtypeStruct((ROWS, COLS), jnp.int32)] * 2,
        scratch_shapes=[cubes] * 4
        + [pltpu.VMEM((ROWS, COLS), F32)] * 2 + [sems(8), pltpu.SemaphoreType.DMA((4,))],
        compiler_params=params(8),
        name="local",
    )(c1, c2, b1, b2, u, v, es, ns, *[far(x) for x in (wet_levels, face_frame, surface_start, surface_sense)])

    ny = lax.axis_size("ty")
    nx = lax.axis_size("tx")
    up_y = [(i, i + 1) for i in range(ny - 1)]
    up_x = [(i, i + 1) for i in range(nx - 1)]
    back = lambda pairs: [(b, a) for a, b in pairs]
    ylo = lax.ppermute(yup, "ty", up_y)
    yhi = lax.ppermute(ydn, "ty", back(up_y))

    he, hn = pl.pallas_call(
        prepare_kernel,
        in_specs=[vmem] * 3,
        out_specs=[vmem] * 2,
        out_shape=[vol] * 2,
        compiler_params=params(4),
        cost_estimate=pl.CostEstimate(flops=2000000, bytes_accessed=2000000, transcendentals=0),
        name="prepare",
    )(u, v, turns)

    xr, xl, ext, edges_ext, nt_fix, row_seam = pl.pallas_call(
        rows_kernel,
        out_shape=[sds(XROWS, 128), sds(XROWS, 128), sds(FIELDS * TALL, COLS),
                   sds(4 * TALL, 128), sds(4 * LEVELS, COLS), sds(12 * LEVELS, COLS)],
        compiler_params=params(4),
        name="rows",
    )(ylo, yhi, yup, ydn, f2d, edges)
    xlo = lax.ppermute(xr, "tx", up_x)
    xhi = lax.ppermute(xl, "tx", back(up_x))

    basis, et_fix, lane_seam, moments = pl.pallas_call(
        columns_kernel,
        in_specs=[vmem] * 5 + [pl.BlockSpec(memory_space=pl.ANY)] * 2,
        out_shape=[sds(8 * TALL, WIDE), sds(ROWS, 128), sds(6 * ROWS, 128), sds(128, 128)],
        compiler_params=params(4),
        name="columns",
    )(xlo, xhi, ext, edges_ext, edges, he, hn)
    moments = lax.all_to_all(moments, ALL, 0, 0, tiled=True)
    th, sa, ea, na, xb = pl.pallas_call(
        final_kernel,
        in_specs=[vmem] * 14,
        out_specs=[hbm] * 4 + [vmem],
        out_shape=[vol] * 4 + [sds(ROWS, COLS)],
        scratch_shapes=[pltpu.VMEM((8 * LEVELS, COLS), F32), pltpu.VMEM((2 * ROWS, 128), F32)]
        + [cubes] * 4 + [sems(4)],
        compiler_params=params(8),
        name="final",
    )(moments, basis, row_seam, nt_fix, lane_seam, et_fix, lev, turns, b1, b2, he, hn, et, nt)
    cube = lambda x: x.reshape(LEVELS, ROWS, COLS)
    return cube(th), cube(sa), cube(ea), cube(na), xb


def solution(mesh):
    cube = P(None, "ty", "tx")
    plane = P("ty", "tx")
    return jax.shard_map(
        on_device,
        mesh=mesh,
        in_specs=(cube, cube, cube, cube, plane, plane, plane, cube, cube, cube, cube, plane),
        out_specs=(cube, cube, cube, cube, plane),
        check_vma=False,
    )
```

```python
import functools

import jax
import jax.numpy as jnp
from jax import lax
from jax.experimental import pallas as pl
from jax.experimental.pallas import tpu as pltpu
from jax.sharding import PartitionSpec as P

F32 = jnp.float32
BF16 = jnp.bfloat16
LEVELS = 32
ROWS = 16
COLS = 256
WIDE = 384
TALL = 32
CHUNK = 8
STEPS = LEVELS // CHUNK
FIELDS = 7
D, X0, TE, TN, SS, CE, CN = range(FIELDS)
Y2D = 320
YE = Y2D + 8 * FIELDS
YROWS = YE + 16
XROWS = 112

RATE = 0.2
GRAVITY = 0.25
STIFF = 2.0 / LEVELS
K7 = 0.5 * RATE * 7.0 / 12.0
K1 = 0.5 * RATE / 12.0
ALL = ("ty", "tx")


def roll(x, shift, axis):
    return pltpu.roll(x, shift % x.shape[axis], axis)


def iota(shape, axis):
    return lax.broadcasted_iota(jnp.int32, shape, axis)


def frame(q_ref):
    q = q_ref[...]
    cos = jnp.where(q == 0, 1.0, jnp.where(q == 2, -1.0, 0.0))
    sin = jnp.where(q == 1, 1.0, jnp.where(q == 3, -1.0, 0.0))
    return cos, sin


def face_levels(lev):
    lane = iota((ROWS, COLS), 1)
    row = iota((ROWS, COLS), 0)
    east = jnp.where(lane < COLS - 1, jnp.minimum(lev, roll(lev, -1, 1)), 0)
    north = jnp.where(row < ROWS - 1, jnp.minimum(lev, roll(lev, -1, 0)), 0)
    return east, north


def split(x):
    hi = x.astype(BF16)
    return hi, (x - hi.astype(F32)).astype(BF16)


def band(delta, taps):
    out = jnp.zeros(delta.shape, F32)
    for at, value in taps:
        out = jnp.where(delta == at, value, out)
    return out


def fill_lanes(ref, taps):
    w = band(iota((COLS, COLS), 0) - iota((COLS, COLS), 1), taps).astype(BF16)
    ref[0:COLS, :] = w
    ref[COLS : 2 * COLS, :] = w


def fill_rows(ref, taps, ends):
    block = CHUNK * ROWS
    r = iota((block, block), 0)
    c = iota((block, block), 1)
    m = jnp.where((r // ROWS) == (c // ROWS), band(c - r, taps), 0.0)
    if ends:
        r = iota((4 * CHUNK, block), 0)
        c = iota((4 * CHUNK, block), 1)
        pick = r // CHUNK
        row = jnp.where(pick < 2, pick + ROWS - 2, pick - 2)
        e = jnp.where(c == (r % CHUNK) * ROWS + row, 1.0, 0.0)
        m = jnp.concatenate([m, e], axis=0)
    m = m.astype(BF16)
    ref[:, 0:block] = m
    ref[:, block : 2 * block] = m


def dot(a, b):
    return jnp.dot(a, b, preferred_element_type=F32)


VALUE_TAPS = ((0, 7.0), (1, 7.0), (-1, -1.0), (2, -1.0))
SENSE_TAPS = ((0, -1.0), (1, 1.0))
BACK_TAPS = ((0, 7.0), (-1, 7.0), (1, -1.0), (-2, -1.0))


def local_kernel(c1, c2, b1_in, b2_in, u_in, v_in, es_in, ns_in, lev_in, q_in, x0_in, ss_in,
                 yup, ydn, f2d, edges, et, nt, b1, b2, u, v, fe1, fe2, fn1, fn2, lev_ref, q_ref, t1, t2, es, ns,
                 x0_ref, ss_ref, wc, wb, kc, kb, ce, cn, be, bn, sems, small_sems):
    small = ((q_in, q_ref), (lev_in, lev_ref), (x0_in, x0_ref), (ss_in, ss_ref))
    small = [pltpu.make_async_copy(a, b, small_sems.at[n]) for n, (a, b) in enumerate(small)]
    for c in small:
        c.start()
    moves = ((c1, t1), (c2, t2), (b1_in, b1), (b2_in, b2), (u_in, u), (v_in, v), (es_in, es), (ns_in, ns))

    def copy(n, g):
        at = pl.ds(g * CHUNK * ROWS, CHUNK * ROWS)
        return pltpu.make_async_copy(moves[n][0].at[at, :], moves[n][1].at[at, :], sems.at[n, g])

    for g in range(STEPS):
        for n in range(8):
            copy(n, g).start()
    fill_lanes(wc, VALUE_TAPS)
    fill_lanes(wb, SENSE_TAPS)
    fill_rows(kc, VALUE_TAPS, True)
    fill_rows(kb, SENSE_TAPS, True)
    for c in small:
        c.wait()
    cos, sin = frame(q_ref)
    lev = lev_ref[...]
    east_lev, north_lev = face_levels(lev)
    lane = iota((ROWS, COLS), 1)
    row = iota((ROWS, COLS), 0)
    lane128 = iota((ROWS, 128), 1)
    line8 = iota((CHUNK, COLS), 0)
    f2d[...] = jnp.zeros_like(f2d)
    edges[...] = jnp.zeros_like(edges)

    def field(f):
        return slice(f * ROWS, (f + 1) * ROWS)

    def step(g, carry):
        for n in range(8):
            copy(n, g).wait()
        acc_u = jnp.zeros((ROWS, COLS), F32)
        acc_v = jnp.zeros((ROWS, COLS), F32)
        acc_e = jnp.zeros((ROWS, COLS), F32)
        acc_n = jnp.zeros((ROWS, COLS), F32)
        packs = [jnp.zeros((ROWS, 128), F32) for _ in range(5)]
        block = CHUNK * ROWS
        rows_at = pl.multiple_of(g * block, block)
        for a, (src, w, k_rows, east, north) in enumerate(
            ((t1, wc, kc, ce, cn), (t2, wc, kc, ce, cn), (b1, wb, kb, be, bn), (b2, wb, kb, be, bn))
        ):
            hi, lo = split(src[pl.ds(rows_at, block), :])
            at = slice((a % 2) * block, (a % 2 + 1) * block)
            east[at, :] = dot(jnp.concatenate([hi, lo], axis=1), w[...])
            both = dot(k_rows[...], jnp.concatenate([hi, lo], axis=0))
            north[at, :] = both[0:block, :]
            for n, (out, r) in enumerate(((yup, 0), (yup, 1), (ydn, 0), (ydn, 1))):
                spot = pl.multiple_of((2 * a + r) * LEVELS + g * CHUNK, CHUNK)
                out[pl.ds(spot, CHUNK), :] = both[block + n * CHUNK : block + (n + 1) * CHUNK, :]
        for kk in range(CHUNK):
            k = g * CHUNK + kk
            here = pl.ds(rows_at + kk * ROWS, ROWS)
            m = lev > k
            me = east_lev > k
            mn = north_lev > k
            ve = None
            vn = None
            for t, (fe_ref, fn_ref) in enumerate(((fe1, fn1), (fe2, fn2))):
                at = slice(t * block + kk * ROWS, t * block + (kk + 1) * ROWS)
                fe = jnp.where(me, be[at, :], 0.0)
                fn = jnp.where(mn, bn[at, :], 0.0)
                fe_ref[here, :] = fe
                fn_ref[here, :] = fn
                ve_t = fe * ce[at, :]
                vn_t = fn * cn[at, :]
                ve = ve_t if ve is None else ve + ve_t
                vn = vn_t if vn is None else vn + vn_t
            ve = K1 * ve
            vn = K1 * vn
            es_k = es[here, :]
            ns_k = ns[here, :]
            u_k = u[here, :]
            v_k = v[here, :]
            et_k = cos * es_k - sin * ns_k + (ve + roll(ve, 1, 1))
            nt_k = sin * es_k + cos * ns_k + (vn + roll(vn, 1, 0))
            et[here, :] = et_k
            nt[here, :] = nt_k
            acc_e = acc_e + jnp.where(m, et_k, 0.0)
            acc_n = acc_n + jnp.where(m, nt_k, 0.0)
            acc_u = acc_u + jnp.where(m, u_k, 0.0)
            acc_v = acc_v + jnp.where(m, v_k, 0.0)

            def ends(x):
                return jnp.where(lane128 < 2, x[:, :128], x[:, 128:])

            spot = (lane128 // 4) == kk
            packed = [ends(r[here, :]) for r in (t1, t2, b1, b2)]
            packed.append(cos[:, :128] * ends(u_k) - sin[:, :128] * ends(v_k))
            for n in range(5):
                packs[n] = jnp.where(spot, roll(packed[n], 4 * kk + 2, 1), packs[n])

        for n in range(5):
            at = slice(n * ROWS, (n + 1) * ROWS)
            edges[at, :] = edges[at, :] + pltpu.roll(packs[n], g * (4 * CHUNK), 1)
        f2d[field(TE), :] = f2d[field(TE), :] + (cos * acc_u - sin * acc_v)
        f2d[field(TN), :] = f2d[field(TN), :] + (sin * acc_u + cos * acc_v)
        f2d[field(CE), :] = f2d[field(CE), :] + acc_e
        f2d[field(CN), :] = f2d[field(CN), :] + acc_n

        for out, first in ((yup, ROWS - 2), (ydn, 0)):
            for r in range(2):
                def rows_of(ref):
                    got = jnp.zeros((CHUNK, COLS), F32)
                    block = ref.at[pl.ds(rows_at, CHUNK * ROWS), :]
                    for kk in range(CHUNK):
                        at = kk * ROWS + first + r
                        got = jnp.where(line8 == kk, block[at : at + 1, :], got)
                    return got

                at = pl.multiple_of((8 + r) * LEVELS + g * CHUNK, CHUNK)
                out[pl.ds(at, CHUNK), :] = sin[:CHUNK, :] * rows_of(u) + cos[:CHUNK, :] * rows_of(v)
        return carry

    lax.fori_loop(0, STEPS, step, 0)
    f2d[field(D), :] = lev.astype(F32)
    f2d[field(X0), :] = x0_ref[...]
    f2d[field(SS), :] = ss_ref[...]
    for out, first in ((yup, 8), (ydn, 0)):
        for f in range(FIELDS):
            out[Y2D + 8 * f : Y2D + 8 * f + 8, :] = f2d[f * ROWS + first : f * ROWS + first + 8, :]
        for n in range(4):
            at = YE + 8 * (n // 2)
            side = 128 * (n % 2)
            out[at : at + 8, side : side + 128] = edges[n * ROWS + first : n * ROWS + first + 8, :]


def row_boundary(low, high, lev_a2, lev_a1, lev_b1, lev_b2):
    level = iota((LEVELS, COLS), 0).astype(F32)
    mask_a = level < jnp.minimum(lev_a2, lev_a1)
    mask_0 = level < jnp.minimum(lev_a1, lev_b1)
    mask_b = level < jnp.minimum(lev_b1, lev_b2)

    def part(ref, a, r):
        return ref[(2 * a + r) * LEVELS : (2 * a + r + 1) * LEVELS, :]

    va = v0 = vb = None
    diffs = []
    for t in range(2):
        ca2, ca1 = part(low, t, 0), part(low, t, 1)
        cb1, cb2 = part(high, t, 0), part(high, t, 1)
        ga2, ga1 = part(low, 2 + t, 0), part(low, 2 + t, 1)
        gb1, gb2 = part(high, 2 + t, 0), part(high, 2 + t, 1)
        fa = jnp.where(mask_a, ga1 - ga2, 0.0)
        f0 = jnp.where(mask_0, gb1 - ga1, 0.0)
        fb = jnp.where(mask_b, gb2 - gb1, 0.0)
        diffs.append((fa, f0, fb))
        fa = fa * (-K1 * cb1)
        f0 = f0 * (K7 * (ca1 + cb1) - K1 * (ca2 + cb2))
        fb = fb * (-K1 * ca1)
        va = fa if va is None else va + fa
        v0 = f0 if v0 is None else v0 + f0
        vb = fb if vb is None else vb + fb
    vel = [part(low, 4, 0), part(low, 4, 1), part(high, 4, 0), part(high, 4, 1)]
    return va, va + v0, v0 + vb, vb, diffs, vel


def rows_kernel(ylo, yhi, yup, ydn, f2d, edges, xr, xl, ext, edges_ext, nt_fix, row_seam):
    d0 = f2d[0:1, :]
    d1 = f2d[1:2, :]
    d14 = f2d[ROWS - 2 : ROWS - 1, :]
    d15 = f2d[ROWS - 1 : ROWS, :]
    lo = row_boundary(ylo, ydn, ylo[Y2D + 6 : Y2D + 7, :], ylo[Y2D + 7 : Y2D + 8, :], d0, d1)
    hi = row_boundary(yup, yhi, d14, d15, yhi[Y2D : Y2D + 1, :], yhi[Y2D + 1 : Y2D + 2, :])
    for side, (out, at) in enumerate(((lo, 0), (hi, 1))):
        diffs, vel = out[4], out[5]
        for i in range(2):
            spot = (6 * side + i) * LEVELS
            row_seam[spot : spot + LEVELS, :] = vel[at + i] + vel[at + i + 1]
            for t in range(2):
                spot = (6 * side + 2 + 2 * t + i) * LEVELS
                row_seam[spot : spot + LEVELS, :] = diffs[t][at + i]
    for n, value in enumerate((lo[2], lo[3], hi[0], hi[1])):
        nt_fix[n * LEVELS : (n + 1) * LEVELS, :] = value
    for f in range(FIELDS):
        ext[f * TALL : f * TALL + ROWS, :] = f2d[f * ROWS : (f + 1) * ROWS, :]
        ext[f * TALL + 16 : f * TALL + 24, :] = yhi[Y2D + 8 * f : Y2D + 8 * f + 8, :]
        ext[f * TALL + 24 : f * TALL + 32, :] = ylo[Y2D + 8 * f : Y2D + 8 * f + 8, :]
    spots = ((30, lo[0]), (31, lo[1]), (0, lo[2]), (1, lo[3]),
             (14, hi[0]), (15, hi[1]), (16, hi[2]), (17, hi[3]))
    for r, value in spots:
        at = slice(CN * TALL + r, CN * TALL + r + 1)
        ext[at, :] = ext[at, :] + jnp.sum(value, axis=0, keepdims=True)
    for n in range(4):
        at = YE + 8 * (n // 2)
        side = 128 * (n % 2)
        edges_ext[n * TALL : n * TALL + ROWS, :] = edges[n * ROWS : (n + 1) * ROWS, :]
        edges_ext[n * TALL + 16 : n * TALL + 24, :] = yhi[at : at + 8, side : side + 128]
        edges_ext[n * TALL + 24 : n * TALL + 32, :] = ylo[at : at + 8, side : side + 128]
    lane = iota((TALL, 128), 1)
    pr = jnp.zeros((TALL, 128), F32)
    pl_ = jnp.zeros((TALL, 128), F32)
    for f in range(FIELDS):
        spot = (lane // 8) == f
        z = ext[f * TALL : (f + 1) * TALL, :]
        pr = jnp.where(spot, roll(z[:, 128:], 8 * f + 8, 1), pr)
        pl_ = jnp.where(spot, roll(z[:, :128], 8 * f, 1), pl_)
    xr[0:TALL, :] = pr
    xl[0:TALL, :] = pl_
    first = (lane % 4) < 2
    for pair in range(2):
        p = edges_ext[2 * pair * TALL : (2 * pair + 1) * TALL, :]
        s = edges_ext[(2 * pair + 1) * TALL : (2 * pair + 2) * TALL, :]
        at = slice((1 + pair) * TALL, (2 + pair) * TALL)
        xr[at, :] = jnp.where(first, p, roll(s, 2, 1))
        xl[at, :] = jnp.where(first, roll(s, -2, 1), p)
    xr[96:112, :] = edges[4 * ROWS : 5 * ROWS, :]
    xl[96:112, :] = edges[4 * ROWS : 5 * ROWS, :]


def spread(x):
    lane = iota(x.shape, 1)
    x = jnp.where(lane < 4, x, 0.0)
    for s in (4, 8, 16, 32, 64):
        x = x + roll(x, s, 1)
    return x


def seam(left_tile, right_tile):
    lane = iota(left_tile.shape, 1)
    return roll(jnp.where(lane >= 126, left_tile, right_tile), 2, 1)


def joined(lo_ref, hi_ref, edges_ext, pair, which, rows):
    own = edges_ext[(2 * pair + which) * TALL : (2 * pair + which) * TALL + rows, :]
    first = (iota((rows, 128), 1) % 4) < 2
    at = slice((1 + pair) * TALL, (1 + pair) * TALL + rows)
    lo = lo_ref[at, :]
    hi = hi_ref[at, :]
    if which == 1:
        lo = roll(lo, -2, 1)
        hi = roll(hi, 2, 1)
    return jnp.where(first, lo, own), jnp.where(first, own, hi)


def columns_kernel(xlo, xhi, ext, edges_ext, edges, he, hn, basis, et_fix, lane_seam, moments):
    lane = iota((TALL, 128), 1)
    group = lane % 4
    level = (lane // 4).astype(F32)
    tiles = []
    for f in range(FIELDS):
        z = ext[f * TALL : (f + 1) * TALL, :]
        right = roll(xhi[0:TALL, :], -8 * f, 1)
        left = roll(xlo[0:TALL, :], 120 - 8 * f, 1)
        third = jnp.where(lane < 8, right, jnp.where(lane >= 120, left, 0.0))
        tiles.append([z[:, :128], z[:, 128:], third])
    coef7 = jnp.where(group == 1, K7, 0.0)
    coefm = jnp.where((group == 1) | (group == 2), -K1, 0.0)
    coefp = jnp.where(group < 2, -K1, 0.0)
    cells = []
    for side in range(2):
        d = tiles[D]
        lev = spread(seam(d[2], d[0]) if side == 0 else seam(d[1], d[2]))
        wet = (level < jnp.minimum(lev, roll(lev, -1, 1))) & (group < 3)
        w = None
        for t in range(2):
            c = joined(xlo, xhi, edges_ext, 0, t, TALL)[side]
            b = joined(xlo, xhi, edges_ext, 1, t, TALL)[side]
            f = jnp.where(wet, roll(b, -1, 1) - b, 0.0)
            spot = (3 * side + 1 + t) * ROWS
            lane_seam[spot : spot + ROWS, :] = f[0:ROWS, :]
            term = f * (coef7 * (c + roll(c, -1, 1)) + coefm * roll(c, 1, 1) + coefp * roll(c, -2, 1))
            w = term if w is None else w + term
        cell = w + roll(w, 1, 1)
        cells.append(cell)
        total = cell
        for s in (4, 8, 16, 32, 64):
            total = total + roll(total, s, 1)
        total = roll(total, -2, 1)
        a, b = (2, 0) if side == 0 else (1, 2)
        tiles[CE][a] = tiles[CE][a] + jnp.where(lane >= 126, total, 0.0)
        tiles[CE][b] = tiles[CE][b] + jnp.where(lane < 2, total, 0.0)
    et_fix[...] = jnp.where(group < 2, cells[1], cells[0])[0:ROWS, :]
    own_u = edges[4 * ROWS : 5 * ROWS, :]
    half = group[0:ROWS, :] < 2
    for side, uu in enumerate((jnp.where(half, xlo[96:112, :], own_u), jnp.where(half, own_u, xhi[96:112, :]))):
        lane_seam[3 * side * ROWS : (3 * side + 1) * ROWS, :] = uu + roll(uu, -1, 1)

    full = [jnp.concatenate(t, axis=1) for t in tiles]
    d = full[D]
    near_e = jnp.minimum(d, roll(d, -1, 1))
    near_n = jnp.minimum(d, roll(d, -1, 0))
    we = STIFF * near_e
    wn = STIFF * near_n
    half_e = jnp.where(near_e > 0.0, 0.5, 0.0)
    half_n = jnp.where(near_n > 0.0, 0.5, 0.0)
    x0 = full[X0]
    flux_e = half_e * (full[TE] + roll(full[TE], -1, 1)) + we * (x0 - roll(x0, -1, 1))
    flux_n = half_n * (full[TN] + roll(full[TN], -1, 0)) + wn * (x0 - roll(x0, -1, 0))
    r = (roll(flux_e, 1, 1) - flux_e) + (roll(flux_n, 1, 0) - flux_n)
    b = full[SS] + (0.5 * GRAVITY) * (
        (roll(full[CE], -1, 1) - roll(full[CE], 1, 1)) + (roll(full[CN], -1, 0) - roll(full[CN], 1, 0))
    )

    def own_sum(x):
        part = x[0:ROWS, 0:128] + x[0:ROWS, 128:256]
        return jnp.sum(part, axis=0, keepdims=True)

    sums = []
    for n, start in enumerate((r, b)):
        vec = start
        for power in range(3):
            basis[(4 * n + power) * TALL : (4 * n + power + 1) * TALL, :] = vec
            sums.append(own_sum(vec * vec))
            de = vec - roll(vec, -1, 1)
            dn = vec - roll(vec, -1, 0)
            he = we * de
            hn = wn * dn
            sums.append(own_sum(he * de + hn * dn))
            if power < 2:
                vec = (he - roll(he, 1, 1)) + (hn - roll(hn, 1, 0))
    basis[3 * TALL : 4 * TALL, :] = x0
    basis[7 * TALL : 8 * TALL, :] = d
    spot_lane = iota((1, 128), 1)
    line = jnp.zeros((1, 128), F32)
    for n, s in enumerate(sums):
        line = line + jnp.where(spot_lane == n, jnp.sum(s, axis=1, keepdims=True), 0.0)
    moments[...] = jnp.broadcast_to(line, (128, 128))


def safe_ratio(top, bottom, limit):
    ok = bottom > 0.0
    return jnp.clip(jnp.where(ok, top / jnp.where(ok, bottom, 1.0), 0.0), 0.0, limit)


def solve_small(m):
    bound = 8.0 * STIFF * LEVELS
    a0 = m[1] / m[0]
    n1 = m[2] - a0 * m[1]
    b1 = safe_ratio(n1, m[0], bound * bound)
    a1 = safe_ratio(m[3] - a0 * (2.0 * m[2] - a0 * m[1]), n1, bound)
    s = a0 + a1
    t = a0 * a1 - b1
    n2 = m[4] - s * m[3] + t * m[2]
    b2 = safe_ratio(n2, n1, bound * bound)
    top = m[5] - 2.0 * s * m[4] + (s * s + 2.0 * t) * m[3] - 2.0 * s * t * m[2] + t * t * m[1]
    a2 = safe_ratio(top, n2, bound)
    e2 = 1.0 + a2
    e1 = jnp.maximum(1.0 + a1 - b2 / e2, 1.0)
    e0 = jnp.maximum(1.0 + a0 - b1 / e1, 1.0)
    y0 = 1.0 / e0
    y1 = -y0 / e1
    y2 = -y1 / e2
    return y0 - a0 * y1 + t * y2, y1 - s * y2, y2


def vec(ref, n):
    return ref[n * TALL : (n + 1) * TALL, :]


def prepare_kernel(u, v, q_ref, he, hn, wd, kd):
    cos, sin = frame(q_ref)
    cos = K1 * cos
    sin = K1 * sin
    fill_lanes(wd, BACK_TAPS)
    fill_rows(kd, BACK_TAPS, False)

    def step(g, carry):
        for kk in range(4):
            here = pl.ds(pl.multiple_of(g * (4 * ROWS), 4 * ROWS) + kk * ROWS, ROWS)
            east = cos * u[here, :] - sin * v[here, :]
            north = sin * u[here, :] + cos * v[here, :]
            he[here, :] = east + roll(east, -1, 1)
            hn[here, :] = north + roll(north, -1, 0)
        return carry

    lax.fori_loop(0, LEVELS // 4, step, 0)


def final_kernel(mom, basis, row_seam, nt_fix, lane_seam, et_fix, lev_ref, q_ref, b1, b2, he_ref, hn_ref,
                 fe1, fe2, fn1, fn2, wd, kd, et, nt, th_out, sa_out, ea_out, na_out, xb,
                 row_fix, lane_fix, th, sa, ea, na, out_sems):
    outs = ((th, th_out), (sa, sa_out), (ea, ea_out), (na, na_out))

    def put(n, g):
        at = pl.ds(g * CHUNK * ROWS, CHUNK * ROWS)
        return pltpu.make_async_copy(outs[n][0].at[at, :], outs[n][1].at[at, :], out_sems.at[n, g])

    cos, sin = frame(q_ref)
    lev = lev_ref[...]
    lane = iota((ROWS, COLS), 1)
    line = jnp.sum(mom[...], axis=0, keepdims=True)
    spot = iota((1, 128), 1)
    m = [jnp.sum(jnp.where(spot == n, line, 0.0), axis=1, keepdims=True) for n in range(12)]
    cf = solve_small(m[0:6])
    cb = solve_small(m[6:12])
    end = vec(basis, 3) + (cf[0] * vec(basis, 0) + cf[1] * vec(basis, 1) + cf[2] * vec(basis, 2))
    adj = cb[0] * vec(basis, 4) + cb[1] * vec(basis, 5) + cb[2] * vec(basis, 6)
    d = vec(basis, 7)
    xb[...] = adj[0:ROWS, 0:COLS]
    ge = (0.5 * GRAVITY) * (roll(end, -1, 1) - roll(end, 1, 1))
    gn = (0.5 * GRAVITY) * (roll(end, -1, 0) - roll(end, 1, 0))
    wide_e = ge + roll(ge, -1, 1)
    wide_n = gn + roll(gn, -1, 0)
    sum_e = K1 * wide_e[0:ROWS, 0:COLS]
    sum_n = K1 * wide_n[0:ROWS, 0:COLS]
    fe = jnp.where(jnp.minimum(d, roll(d, -1, 1)) > 0.0, 0.5 * (roll(adj, -1, 1) - adj), 0.0)
    fn = jnp.where(jnp.minimum(d, roll(d, -1, 0)) > 0.0, 0.5 * (roll(adj, -1, 0) - adj), 0.0)
    be = (fe + roll(fe, 1, 1))[0:ROWS, 0:COLS]
    bn = (fn + roll(fn, 1, 0))[0:ROWS, 0:COLS]

    for side, first in enumerate((-2, 15)):
        vel = []
        for i in range(2):
            r = (first + i) % TALL
            vel.append(row_seam[(6 * side + i) * LEVELS : (6 * side + i + 1) * LEVELS, :] - wide_n[r : r + 1, 0:COLS])
        for t in range(2):
            spots = [(6 * side + 2 + 2 * t + i) * LEVELS for i in range(2)]
            qa, qb = [row_seam[s : s + LEVELS, :] * w for s, w in zip(spots, vel)]
            values = (K7 * qb - K1 * qa, -K1 * qb) if side == 0 else (-K1 * qa, K7 * qa - K1 * qb)
            for i in range(2):
                at = (4 * t + 2 * side + i) * LEVELS
                row_fix[at : at + LEVELS, :] = values[i]
    group = iota((ROWS, 128), 1) % 4
    tiles = [wide_e[0:ROWS, 128 * n : 128 * n + 128] for n in range(3)]
    for side in range(2):
        gg = spread(seam(tiles[2], tiles[0]) if side == 0 else seam(tiles[1], tiles[2]))
        vel = lane_seam[3 * side * ROWS : (3 * side + 1) * ROWS, :] - gg
        keep = (group < 2) if side == 0 else ((group == 1) | (group == 2))
        for t in range(2):
            spot = (3 * side + 1 + t) * ROWS
            f = jnp.where(keep, lane_seam[spot : spot + ROWS, :] * vel, 0.0)
            at = slice(t * ROWS, (t + 1) * ROWS)
            if side == 0:
                fix = jnp.where(group == 2, K7 * roll(f, 1, 1), 0.0) - K1 * roll(f, 2, 1)
                lane_fix[at, :] = jnp.where(group >= 2, fix, 0.0)
            else:
                fix = jnp.where(group == 1, K7 * f, 0.0) - K1 * roll(f, -1, 1)
                lane_fix[at, :] = jnp.where(group < 2, fix, lane_fix[at, :])

    edge = (lane < 2) | (lane >= COLS - 2)
    line8 = iota((8, COLS), 0)

    def step(g, carry):
        turn = 128 - g * (4 * CHUNK)
        packs = [lane_fix[0:ROWS, :], lane_fix[ROWS : 2 * ROWS, :], et_fix[...]]
        packs = [pltpu.roll(p, turn, 1) for p in packs]

        def fix_rows(ref, n):
            return ref.at[pl.ds(pl.multiple_of(n * LEVELS + g * CHUNK, CHUNK), CHUNK), :]

        fixes = [[fix_rows(row_fix, n) for n in range(4)], [fix_rows(row_fix, 4 + n) for n in range(4)],
                 [fix_rows(nt_fix, n) for n in range(4)]]
        block = CHUNK * ROWS
        rows_at = pl.multiple_of(g * block, block)
        for fe_ref, fn_ref, b_ref, out in ((fe1, fn1, b1, th), (fe2, fn2, b2, sa)):
            flow_e = []
            flow_n = []
            for kk in range(CHUNK):
                here = pl.ds(rows_at + kk * ROWS, ROWS)
                flow_e.append(fe_ref[here, :] * (he_ref[here, :] - sum_e))
                flow_n.append(fn_ref[here, :] * (hn_ref[here, :] - sum_n))
            east = dot(jnp.concatenate(split(jnp.concatenate(flow_e, axis=0)), axis=1), wd[...])
            north = dot(kd[...], jnp.concatenate(split(jnp.concatenate(flow_n, axis=0)), axis=0))
            at = pl.ds(rows_at, block)
            out[at, :] = b_ref[at, :] + (east + north)
        for kk in range(CHUNK):
            k = g * CHUNK + kk
            here = pl.ds(rows_at + kk * ROWS, ROWS)
            m = lev > k

            def lane_fixed(x, n):
                z = roll(packs[n], -(4 * kk + 2), 1)
                return jnp.where(edge, x + jnp.concatenate([z, z], axis=1), x)

            def row_fixed(x, n):
                r0, r1, r14, r15 = [f[kk : kk + 1, :] for f in fixes[n]]
                top = jnp.where(line8 == 0, r0, jnp.where(line8 == 1, r1, 0.0))
                low = jnp.where(line8 == 6, r14, jnp.where(line8 == 7, r15, 0.0))
                return x + jnp.concatenate([top, low], axis=0)

            for n, out in enumerate((th, sa)):
                out[here, :] = row_fixed(lane_fixed(out[here, :], n), n)
            eg = jnp.where(m, lane_fixed(et[here, :], 2) + be, 0.0)
            ng = jnp.where(m, row_fixed(nt[here, :], 2) + bn, 0.0)
            ea[here, :] = cos * eg + sin * ng
            na[here, :] = cos * ng - sin * eg
        for n in range(4):
            put(n, g).start()
        return carry

    lax.fori_loop(0, STEPS, step, 0)
    for g in range(STEPS):
        for n in range(4):
            put(n, g).wait()


def params(mib):
    return pltpu.CompilerParams(vmem_limit_bytes=mib * 1024 * 1024)


def far(x):
    return pltpu.with_memory_space_constraint(x, pltpu.HBM)


def sds(*shape):
    return jax.ShapeDtypeStruct(shape, F32)


def on_device(theta_start, salt_start, east_velocity, north_velocity, surface_start, wet_levels,
              face_frame, theta_sense, salt_sense, east_sense, north_sense, surface_sense):
    flat = lambda x: x.reshape(LEVELS * ROWS, COLS)
    c1, c2, u, v = map(flat, (theta_start, salt_start, east_velocity, north_velocity))
    b1, b2, es, ns = map(flat, (theta_sense, salt_sense, east_sense, north_sense))
    vol = sds(LEVELS * ROWS, COLS)
    c1, c2, b1, b2, u, v, es, ns = [far(x) for x in (c1, c2, b1, b2, u, v, es, ns)]
    hbm = pl.BlockSpec(memory_space=pltpu.HBM)
    vmem = pl.BlockSpec(memory_space=pltpu.VMEM)
    cubes = pltpu.VMEM((LEVELS * ROWS, COLS), F32)
    sems = lambda n: pltpu.SemaphoreType.DMA((n, STEPS))
    yup, ydn, f2d, edges, et, nt, b1, b2, u, v, fe1, fe2, fn1, fn2, lev, turns = pl.pallas_call(
        local_kernel,
        in_specs=[hbm] * 12,
        out_specs=[vmem] * 16,
        out_shape=[sds(YROWS, COLS), sds(YROWS, COLS), sds(FIELDS * ROWS, COLS), sds(5 * ROWS, 128)] + [vol] * 10
        + [jax.ShapeDtypeStruct((ROWS, COLS), jnp.int32)] * 2,
        scratch_shapes=[cubes] * 4
        + [pltpu.VMEM((ROWS, COLS), F32)] * 2 + [pltpu.VMEM((2 * COLS, COLS), BF16)] * 2
        + [pltpu.VMEM((CHUNK * (ROWS + 4), 2 * CHUNK * ROWS), BF16)] * 2
        + [pltpu.VMEM((2 * CHUNK * ROWS, COLS), F32)] * 4 + [sems(8), pltpu.SemaphoreType.DMA((4,))],
        compiler_params=params(10),
        name="local",
    )(c1, c2, b1, b2, u, v, es, ns, *[far(x) for x in (wet_levels, face_frame, surface_start, surface_sense)])

    ny = lax.axis_size("ty")
    nx = lax.axis_size("tx")
    up_y = [(i, i + 1) for i in range(ny - 1)]
    up_x = [(i, i + 1) for i in range(nx - 1)]
    back = lambda pairs: [(b, a) for a, b in pairs]
    ylo = lax.ppermute(yup, "ty", up_y)
    yhi = lax.ppermute(ydn, "ty", back(up_y))

    he, hn, wd, kd = pl.pallas_call(
        prepare_kernel,
        in_specs=[vmem] * 3,
        out_specs=[vmem] * 4,
        out_shape=[vol] * 2 + [jax.ShapeDtypeStruct((2 * COLS, COLS), BF16),
                               jax.ShapeDtypeStruct((CHUNK * ROWS, 2 * CHUNK * ROWS), BF16)],
        compiler_params=params(4),
        cost_estimate=pl.CostEstimate(flops=2000000, bytes_accessed=2000000, transcendentals=0),
        name="prepare",
    )(u, v, turns)

    xr, xl, ext, edges_ext, nt_fix, row_seam = pl.pallas_call(
        rows_kernel,
        out_shape=[sds(XROWS, 128), sds(XROWS, 128), sds(FIELDS * TALL, COLS),
                   sds(4 * TALL, 128), sds(4 * LEVELS, COLS), sds(12 * LEVELS, COLS)],
        compiler_params=params(4),
        name="rows",
    )(ylo, yhi, yup, ydn, f2d, edges)
    xlo = lax.ppermute(xr, "tx", up_x)
    xhi = lax.ppermute(xl, "tx", back(up_x))

    basis, et_fix, lane_seam, moments = pl.pallas_call(
        columns_kernel,
        in_specs=[vmem] * 5 + [pl.BlockSpec(memory_space=pl.ANY)] * 2,
        out_shape=[sds(8 * TALL, WIDE), sds(ROWS, 128), sds(6 * ROWS, 128), sds(128, 128)],
        compiler_params=params(4),
        name="columns",
    )(xlo, xhi, ext, edges_ext, edges, he, hn)
    moments = lax.all_to_all(moments, ALL, 0, 0, tiled=True)
    th, sa, ea, na, xb = pl.pallas_call(
        final_kernel,
        in_specs=[vmem] * 20,
        out_specs=[hbm] * 4 + [vmem],
        out_shape=[vol] * 4 + [sds(ROWS, COLS)],
        scratch_shapes=[pltpu.VMEM((8 * LEVELS, COLS), F32), pltpu.VMEM((2 * ROWS, 128), F32)]
        + [cubes] * 4 + [sems(4)],
        compiler_params=params(8),
        name="final",
    )(moments, basis, row_seam, nt_fix, lane_seam, et_fix, lev, turns, b1, b2, he, hn, fe1, fe2, fn1, fn2, wd, kd, et, nt)
    cube = lambda x: x.reshape(LEVELS, ROWS, COLS)
    return cube(th), cube(sa), cube(ea), cube(na), xb


def solution(mesh):
    cube = P(None, "ty", "tx")
    plane = P("ty", "tx")
    return jax.shard_map(
        on_device,
        mesh=mesh,
        in_specs=(cube, cube, cube, cube, plane, plane, plane, cube, cube, cube, cube, plane),
        out_specs=(cube, cube, cube, cube, plane),
        check_vma=False,
    )
```

```python
import functools

import jax
import jax.numpy as jnp
from jax import lax
from jax.experimental import pallas as pl
from jax.experimental.pallas import tpu as pltpu
from jax.sharding import PartitionSpec as P

F32 = jnp.float32
BF16 = jnp.bfloat16
LEVELS = 32
ROWS = 16
COLS = 256
WIDE = 384
TALL = 32
CHUNK = 8
STEPS = LEVELS // CHUNK
FIELDS = 7
D, X0, TE, TN, SS, CE, CN = range(FIELDS)
Y2D = 320
YE = Y2D + 8 * FIELDS
YROWS = YE + 16
XROWS = 112

RATE = 0.2
GRAVITY = 0.25
STIFF = 2.0 / LEVELS
K7 = 0.5 * RATE * 7.0 / 12.0
K1 = 0.5 * RATE / 12.0
ALL = ("ty", "tx")


def roll(x, shift, axis):
    return pltpu.roll(x, shift % x.shape[axis], axis)


def iota(shape, axis):
    return lax.broadcasted_iota(jnp.int32, shape, axis)


def frame(q_ref):
    q = q_ref[...]
    cos = jnp.where(q == 0, 1.0, jnp.where(q == 2, -1.0, 0.0))
    sin = jnp.where(q == 1, 1.0, jnp.where(q == 3, -1.0, 0.0))
    return cos, sin


def face_levels(lev):
    lane = iota((ROWS, COLS), 1)
    row = iota((ROWS, COLS), 0)
    east = jnp.where(lane < COLS - 1, jnp.minimum(lev, roll(lev, -1, 1)), 0)
    north = jnp.where(row < ROWS - 1, jnp.minimum(lev, roll(lev, -1, 0)), 0)
    return east, north


def split(x):
    hi = x.astype(BF16)
    return hi, (x - hi.astype(F32)).astype(BF16)


def odd_place(axis):
    return lax.rem(lax.axis_index(axis), 2)


def band(delta, taps):
    out = jnp.zeros(delta.shape, F32)
    for at, value in taps:
        out = jnp.where(delta == at, value, out)
    return out


def fill_lanes(ref, taps):
    w = band(iota((COLS, COLS), 0) - iota((COLS, COLS), 1), taps).astype(BF16)
    ref[0:COLS, :] = w
    ref[COLS : 2 * COLS, :] = w


def fill_rows(ref, taps, first_far=None):
    block = CHUNK * ROWS
    r = iota((block, block), 0)
    c = iota((block, block), 1)
    m = jnp.where((r // ROWS) == (c // ROWS), band(c - r, taps), 0.0)
    if first_far is not None:
        r = iota((4 * CHUNK, block), 0)
        c = iota((4 * CHUNK, block), 1)
        pick = r // CHUNK
        row = jnp.where(pick < 2, pick + first_far, pick - 2 + (ROWS - 2 - first_far))
        e = jnp.where(c == (r % CHUNK) * ROWS + row, 1.0, 0.0)
        m = jnp.concatenate([m, e], axis=0)
    m = m.astype(BF16)
    ref[:, 0:block] = m
    ref[:, block : 2 * block] = m


def dot(a, b):
    return jnp.dot(a, b, preferred_element_type=F32)


VALUE_TAPS = ((0, 7.0), (1, 7.0), (-1, -1.0), (2, -1.0))
SENSE_TAPS = ((0, -1.0), (1, 1.0))
BACK_TAPS = ((0, 7.0), (-1, 7.0), (1, -1.0), (-2, -1.0))


def local_kernel(c1, c2, b1_in, b2_in, u_in, v_in, es_in, ns_in, lev_in, q_in, x0_in, ss_in,
                 yfar, ynear, f2d, edges, et, nt, b1, b2, u, v, fe1, fe2, fn1, fn2, lev_ref, q_ref, t1, t2, es, ns,
                 x0_ref, ss_ref, wc, wb, kc, kb, ce, cn, be, bn, sems, small_sems):
    small = ((q_in, q_ref), (lev_in, lev_ref), (x0_in, x0_ref), (ss_in, ss_ref))
    small = [pltpu.make_async_copy(a, b, small_sems.at[n]) for n, (a, b) in enumerate(small)]
    for c in small:
        c.start()
    moves = ((c1, t1), (c2, t2), (b1_in, b1), (b2_in, b2), (u_in, u), (v_in, v), (es_in, es), (ns_in, ns))

    def copy(n, g):
        at = pl.ds(g * CHUNK * ROWS, CHUNK * ROWS)
        return pltpu.make_async_copy(moves[n][0].at[at, :], moves[n][1].at[at, :], sems.at[n, g])

    for g in range(STEPS):
        for n in range(8):
            copy(n, g).start()
    fill_lanes(wc, VALUE_TAPS)
    fill_lanes(wb, SENSE_TAPS)
    odd = odd_place("ty")
    fill_rows(kc, VALUE_TAPS, odd * (ROWS - 2))
    fill_rows(kb, SENSE_TAPS, odd * (ROWS - 2))
    for c in small:
        c.wait()
    cos, sin = frame(q_ref)
    lev = lev_ref[...]
    east_lev, north_lev = face_levels(lev)
    lane = iota((ROWS, COLS), 1)
    row = iota((ROWS, COLS), 0)
    lane128 = iota((ROWS, 128), 1)
    line8 = iota((CHUNK, COLS), 0)
    f2d[...] = jnp.zeros_like(f2d)
    edges[...] = jnp.zeros_like(edges)

    def field(f):
        return slice(f * ROWS, (f + 1) * ROWS)

    def step(g, carry):
        for n in range(8):
            copy(n, g).wait()
        acc_u = jnp.zeros((ROWS, COLS), F32)
        acc_v = jnp.zeros((ROWS, COLS), F32)
        acc_e = jnp.zeros((ROWS, COLS), F32)
        acc_n = jnp.zeros((ROWS, COLS), F32)
        packs = [jnp.zeros((ROWS, 128), F32) for _ in range(5)]
        block = CHUNK * ROWS
        rows_at = pl.multiple_of(g * block, block)
        for a, (src, w, k_rows, east, north) in enumerate(
            ((t1, wc, kc, ce, cn), (t2, wc, kc, ce, cn), (b1, wb, kb, be, bn), (b2, wb, kb, be, bn))
        ):
            hi, lo = split(src[pl.ds(rows_at, block), :])
            at = slice((a % 2) * block, (a % 2 + 1) * block)
            east[at, :] = dot(jnp.concatenate([hi, lo], axis=1), w[...])
            both = dot(k_rows[...], jnp.concatenate([hi, lo], axis=0))
            north[at, :] = both[0:block, :]
            for n, (out, r) in enumerate(((yfar, 0), (yfar, 1), (ynear, 0), (ynear, 1))):
                spot = pl.multiple_of((2 * a + r) * LEVELS + g * CHUNK, CHUNK)
                out[pl.ds(spot, CHUNK), :] = both[block + n * CHUNK : block + (n + 1) * CHUNK, :]
        for kk in range(CHUNK):
            k = g * CHUNK + kk
            here = pl.ds(rows_at + kk * ROWS, ROWS)
            m = lev > k
            me = east_lev > k
            mn = north_lev > k
            ve = None
            vn = None
            for t, (fe_ref, fn_ref) in enumerate(((fe1, fn1), (fe2, fn2))):
                at = slice(t * block + kk * ROWS, t * block + (kk + 1) * ROWS)
                fe = jnp.where(me, be[at, :], 0.0)
                fn = jnp.where(mn, bn[at, :], 0.0)
                fe_ref[here, :] = fe
                fn_ref[here, :] = fn
                ve_t = fe * ce[at, :]
                vn_t = fn * cn[at, :]
                ve = ve_t if ve is None else ve + ve_t
                vn = vn_t if vn is None else vn + vn_t
            ve = K1 * ve
            vn = K1 * vn
            es_k = es[here, :]
            ns_k = ns[here, :]
            u_k = u[here, :]
            v_k = v[here, :]
            et_k = cos * es_k - sin * ns_k + (ve + roll(ve, 1, 1))
            nt_k = sin * es_k + cos * ns_k + (vn + roll(vn, 1, 0))
            et[here, :] = et_k
            nt[here, :] = nt_k
            acc_e = acc_e + jnp.where(m, et_k, 0.0)
            acc_n = acc_n + jnp.where(m, nt_k, 0.0)
            acc_u = acc_u + jnp.where(m, u_k, 0.0)
            acc_v = acc_v + jnp.where(m, v_k, 0.0)

            def ends(x):
                return jnp.where(lane128 < 2, x[:, :128], x[:, 128:])

            spot = (lane128 // 4) == kk
            packed = [ends(r[here, :]) for r in (t1, t2, b1, b2)]
            packed.append(cos[:, :128] * ends(u_k) - sin[:, :128] * ends(v_k))
            for n in range(5):
                packs[n] = jnp.where(spot, roll(packed[n], 4 * kk + 2, 1), packs[n])

        for n in range(5):
            at = slice(n * ROWS, (n + 1) * ROWS)
            edges[at, :] = edges[at, :] + pltpu.roll(packs[n], g * (4 * CHUNK), 1)
        f2d[field(TE), :] = f2d[field(TE), :] + (cos * acc_u - sin * acc_v)
        f2d[field(TN), :] = f2d[field(TN), :] + (sin * acc_u + cos * acc_v)
        f2d[field(CE), :] = f2d[field(CE), :] + acc_e
        f2d[field(CN), :] = f2d[field(CN), :] + acc_n

        def rows_of(ref, r):
            got = jnp.zeros((CHUNK, COLS), F32)
            block = ref.at[pl.ds(rows_at, CHUNK * ROWS), :]
            for kk in range(CHUNK):
                at = kk * ROWS + r
                got = jnp.where(line8 == kk, block[at : at + 1, :], got)
            return got

        for r in range(2):
            high, low = [sin[:CHUNK, :] * rows_of(u, n + r) + cos[:CHUNK, :] * rows_of(v, n + r) for n in (ROWS - 2, 0)]
            at = pl.ds(pl.multiple_of((8 + r) * LEVELS + g * CHUNK, CHUNK), CHUNK)
            yfar[at, :] = jnp.where(odd == 1, high, low)
            ynear[at, :] = jnp.where(odd == 1, low, high)
        return carry

    lax.fori_loop(0, STEPS, step, 0)
    f2d[field(D), :] = lev.astype(F32)
    f2d[field(X0), :] = x0_ref[...]
    f2d[field(SS), :] = ss_ref[...]
    for out, first in ((yfar, 8 * odd), (ynear, 8 - 8 * odd)):
        for f in range(FIELDS):
            at = pl.ds(pl.multiple_of(f * ROWS + first, 8), 8)
            out[Y2D + 8 * f : Y2D + 8 * f + 8, :] = f2d[at, :]
        for n in range(4):
            at = YE + 8 * (n // 2)
            side = 128 * (n % 2)
            out[at : at + 8, side : side + 128] = edges[pl.ds(pl.multiple_of(n * ROWS + first, 8), 8), :]


def row_boundary(low, high, lev_a2, lev_a1, lev_b1, lev_b2):
    level = iota((LEVELS, COLS), 0).astype(F32)
    mask_a = level < jnp.minimum(lev_a2, lev_a1)
    mask_0 = level < jnp.minimum(lev_a1, lev_b1)
    mask_b = level < jnp.minimum(lev_b1, lev_b2)

    def part(ref, a, r):
        return ref[(2 * a + r) * LEVELS : (2 * a + r + 1) * LEVELS, :]

    va = v0 = vb = None
    diffs = []
    for t in range(2):
        ca2, ca1 = part(low, t, 0), part(low, t, 1)
        cb1, cb2 = part(high, t, 0), part(high, t, 1)
        ga2, ga1 = part(low, 2 + t, 0), part(low, 2 + t, 1)
        gb1, gb2 = part(high, 2 + t, 0), part(high, 2 + t, 1)
        fa = jnp.where(mask_a, ga1 - ga2, 0.0)
        f0 = jnp.where(mask_0, gb1 - ga1, 0.0)
        fb = jnp.where(mask_b, gb2 - gb1, 0.0)
        diffs.append((fa, f0, fb))
        fa = fa * (-K1 * cb1)
        f0 = f0 * (K7 * (ca1 + cb1) - K1 * (ca2 + cb2))
        fb = fb * (-K1 * ca1)
        va = fa if va is None else va + fa
        v0 = f0 if v0 is None else v0 + f0
        vb = fb if vb is None else vb + fb
    vel = [part(low, 4, 0), part(low, 4, 1), part(high, 4, 0), part(high, 4, 1)]
    return va, va + v0, v0 + vb, vb, diffs, vel


def rows_kernel(far_in, near_in, far_out, near_out, *rest):
    odd = odd_place("ty")

    @pl.when(odd == 1)
    def _():
        rows_body(near_in, far_in, far_out, near_out, *rest)

    @pl.when(odd == 0)
    def _():
        rows_body(far_in, near_in, near_out, far_out, *rest)


def rows_body(ylo, yhi, yup, ydn, f2d, edges, xfar, xnear, ext, edges_ext, nt_fix, row_seam):
    d0 = f2d[0:1, :]
    d1 = f2d[1:2, :]
    d14 = f2d[ROWS - 2 : ROWS - 1, :]
    d15 = f2d[ROWS - 1 : ROWS, :]
    lo = row_boundary(ylo, ydn, ylo[Y2D + 6 : Y2D + 7, :], ylo[Y2D + 7 : Y2D + 8, :], d0, d1)
    hi = row_boundary(yup, yhi, d14, d15, yhi[Y2D : Y2D + 1, :], yhi[Y2D + 1 : Y2D + 2, :])
    for side, (out, at) in enumerate(((lo, 0), (hi, 1))):
        diffs, vel = out[4], out[5]
        for i in range(2):
            spot = (6 * side + i) * LEVELS
            row_seam[spot : spot + LEVELS, :] = vel[at + i] + vel[at + i + 1]
            for t in range(2):
                spot = (6 * side + 2 + 2 * t + i) * LEVELS
                row_seam[spot : spot + LEVELS, :] = diffs[t][at + i]
    for n, value in enumerate((lo[2], lo[3], hi[0], hi[1])):
        nt_fix[n * LEVELS : (n + 1) * LEVELS, :] = value
    for f in range(FIELDS):
        ext[f * TALL : f * TALL + ROWS, :] = f2d[f * ROWS : (f + 1) * ROWS, :]
        ext[f * TALL + 16 : f * TALL + 24, :] = yhi[Y2D + 8 * f : Y2D + 8 * f + 8, :]
        ext[f * TALL + 24 : f * TALL + 32, :] = ylo[Y2D + 8 * f : Y2D + 8 * f + 8, :]
    spots = ((30, lo[0]), (31, lo[1]), (0, lo[2]), (1, lo[3]),
             (14, hi[0]), (15, hi[1]), (16, hi[2]), (17, hi[3]))
    for r, value in spots:
        at = slice(CN * TALL + r, CN * TALL + r + 1)
        ext[at, :] = ext[at, :] + jnp.sum(value, axis=0, keepdims=True)
    for n in range(4):
        at = YE + 8 * (n // 2)
        side = 128 * (n % 2)
        edges_ext[n * TALL : n * TALL + ROWS, :] = edges[n * ROWS : (n + 1) * ROWS, :]
        edges_ext[n * TALL + 16 : n * TALL + 24, :] = yhi[at : at + 8, side : side + 128]
        edges_ext[n * TALL + 24 : n * TALL + 32, :] = ylo[at : at + 8, side : side + 128]
    lane = iota((TALL, 128), 1)
    pr = jnp.zeros((TALL, 128), F32)
    pl_ = jnp.zeros((TALL, 128), F32)
    for f in range(FIELDS):
        spot = (lane // 8) == f
        z = ext[f * TALL : (f + 1) * TALL, :]
        pr = jnp.where(spot, roll(z[:, 128:], 8 * f + 8, 1), pr)
        pl_ = jnp.where(spot, roll(z[:, :128], 8 * f, 1), pl_)
    oddx = odd_place("tx") == 1

    def send(at, right, left):
        xfar[at, :] = jnp.where(oddx, right, left)
        xnear[at, :] = jnp.where(oddx, left, right)

    send(slice(0, TALL), pr, pl_)
    first = (lane % 4) < 2
    for pair in range(2):
        p = edges_ext[2 * pair * TALL : (2 * pair + 1) * TALL, :]
        s = edges_ext[(2 * pair + 1) * TALL : (2 * pair + 2) * TALL, :]
        at = slice((1 + pair) * TALL, (2 + pair) * TALL)
        send(at, jnp.where(first, p, roll(s, 2, 1)), jnp.where(first, roll(s, -2, 1), p))
    own = edges[4 * ROWS : 5 * ROWS, :]
    send(slice(96, 112), own, own)


def spread(x):
    lane = iota(x.shape, 1)
    x = jnp.where(lane < 4, x, 0.0)
    for s in (4, 8, 16, 32, 64):
        x = x + roll(x, s, 1)
    return x


def seam(left_tile, right_tile):
    lane = iota(left_tile.shape, 1)
    return roll(jnp.where(lane >= 126, left_tile, right_tile), 2, 1)


def joined(lo_ref, hi_ref, edges_ext, pair, which, rows):
    own = edges_ext[(2 * pair + which) * TALL : (2 * pair + which) * TALL + rows, :]
    first = (iota((rows, 128), 1) % 4) < 2
    at = slice((1 + pair) * TALL, (1 + pair) * TALL + rows)
    lo = lo_ref[at, :]
    hi = hi_ref[at, :]
    if which == 1:
        lo = roll(lo, -2, 1)
        hi = roll(hi, 2, 1)
    return jnp.where(first, lo, own), jnp.where(first, own, hi)


def columns_kernel(far_in, near_in, ext, edges_ext, edges, he, hn, basis, et_fix, lane_seam, moments):
    oddx = odd_place("tx") == 1
    xlo = jnp.where(oddx, near_in[...], far_in[...])
    xhi = jnp.where(oddx, far_in[...], near_in[...])
    lane = iota((TALL, 128), 1)
    group = lane % 4
    level = (lane // 4).astype(F32)
    tiles = []
    for f in range(FIELDS):
        z = ext[f * TALL : (f + 1) * TALL, :]
        right = roll(xhi[0:TALL, :], -8 * f, 1)
        left = roll(xlo[0:TALL, :], 120 - 8 * f, 1)
        third = jnp.where(lane < 8, right, jnp.where(lane >= 120, left, 0.0))
        tiles.append([z[:, :128], z[:, 128:], third])
    coef7 = jnp.where(group == 1, K7, 0.0)
    coefm = jnp.where((group == 1) | (group == 2), -K1, 0.0)
    coefp = jnp.where(group < 2, -K1, 0.0)
    cells = []
    for side in range(2):
        d = tiles[D]
        lev = spread(seam(d[2], d[0]) if side == 0 else seam(d[1], d[2]))
        wet = (level < jnp.minimum(lev, roll(lev, -1, 1))) & (group < 3)
        w = None
        for t in range(2):
            c = joined(xlo, xhi, edges_ext, 0, t, TALL)[side]
            b = joined(xlo, xhi, edges_ext, 1, t, TALL)[side]
            f = jnp.where(wet, roll(b, -1, 1) - b, 0.0)
            spot = (3 * side + 1 + t) * ROWS
            lane_seam[spot : spot + ROWS, :] = f[0:ROWS, :]
            term = f * (coef7 * (c + roll(c, -1, 1)) + coefm * roll(c, 1, 1) + coefp * roll(c, -2, 1))
            w = term if w is None else w + term
        cell = w + roll(w, 1, 1)
        cells.append(cell)
        total = cell
        for s in (4, 8, 16, 32, 64):
            total = total + roll(total, s, 1)
        total = roll(total, -2, 1)
        a, b = (2, 0) if side == 0 else (1, 2)
        tiles[CE][a] = tiles[CE][a] + jnp.where(lane >= 126, total, 0.0)
        tiles[CE][b] = tiles[CE][b] + jnp.where(lane < 2, total, 0.0)
    et_fix[...] = jnp.where(group < 2, cells[1], cells[0])[0:ROWS, :]
    own_u = edges[4 * ROWS : 5 * ROWS, :]
    half = group[0:ROWS, :] < 2
    for side, uu in enumerate((jnp.where(half, xlo[96:112, :], own_u), jnp.where(half, own_u, xhi[96:112, :]))):
        lane_seam[3 * side * ROWS : (3 * side + 1) * ROWS, :] = uu + roll(uu, -1, 1)

    full = [jnp.concatenate(t, axis=1) for t in tiles]
    d = full[D]
    near_e = jnp.minimum(d, roll(d, -1, 1))
    near_n = jnp.minimum(d, roll(d, -1, 0))
    we = STIFF * near_e
    wn = STIFF * near_n
    half_e = jnp.where(near_e > 0.0, 0.5, 0.0)
    half_n = jnp.where(near_n > 0.0, 0.5, 0.0)
    x0 = full[X0]
    flux_e = half_e * (full[TE] + roll(full[TE], -1, 1)) + we * (x0 - roll(x0, -1, 1))
    flux_n = half_n * (full[TN] + roll(full[TN], -1, 0)) + wn * (x0 - roll(x0, -1, 0))
    r = (roll(flux_e, 1, 1) - flux_e) + (roll(flux_n, 1, 0) - flux_n)
    b = full[SS] + (0.5 * GRAVITY) * (
        (roll(full[CE], -1, 1) - roll(full[CE], 1, 1)) + (roll(full[CN], -1, 0) - roll(full[CN], 1, 0))
    )

    def own_sum(x):
        part = x[0:ROWS, 0:128] + x[0:ROWS, 128:256]
        return jnp.sum(part, axis=0, keepdims=True)

    sums = []
    for n, start in enumerate((r, b)):
        vec = start
        for power in range(3):
            basis[(4 * n + power) * TALL : (4 * n + power + 1) * TALL, :] = vec
            sums.append(own_sum(vec * vec))
            de = vec - roll(vec, -1, 1)
            dn = vec - roll(vec, -1, 0)
            he = we * de
            hn = wn * dn
            sums.append(own_sum(he * de + hn * dn))
            if power < 2:
                vec = (he - roll(he, 1, 1)) + (hn - roll(hn, 1, 0))
    basis[3 * TALL : 4 * TALL, :] = x0
    basis[7 * TALL : 8 * TALL, :] = d
    spot_lane = iota((1, 128), 1)
    line = jnp.zeros((1, 128), F32)
    for n, s in enumerate(sums):
        line = line + jnp.where(spot_lane == n, jnp.sum(s, axis=1, keepdims=True), 0.0)
    moments[...] = jnp.broadcast_to(line, (128, 128))


def safe_ratio(top, bottom, limit):
    ok = bottom > 0.0
    return jnp.clip(jnp.where(ok, top / jnp.where(ok, bottom, 1.0), 0.0), 0.0, limit)


def solve_small(m):
    bound = 8.0 * STIFF * LEVELS
    a0 = m[1] / m[0]
    n1 = m[2] - a0 * m[1]
    b1 = safe_ratio(n1, m[0], bound * bound)
    a1 = safe_ratio(m[3] - a0 * (2.0 * m[2] - a0 * m[1]), n1, bound)
    s = a0 + a1
    t = a0 * a1 - b1
    n2 = m[4] - s * m[3] + t * m[2]
    b2 = safe_ratio(n2, n1, bound * bound)
    top = m[5] - 2.0 * s * m[4] + (s * s + 2.0 * t) * m[3] - 2.0 * s * t * m[2] + t * t * m[1]
    a2 = safe_ratio(top, n2, bound)
    e2 = 1.0 + a2
    e1 = jnp.maximum(1.0 + a1 - b2 / e2, 1.0)
    e0 = jnp.maximum(1.0 + a0 - b1 / e1, 1.0)
    y0 = 1.0 / e0
    y1 = -y0 / e1
    y2 = -y1 / e2
    return y0 - a0 * y1 + t * y2, y1 - s * y2, y2


def vec(ref, n):
    return ref[n * TALL : (n + 1) * TALL, :]


def prepare_kernel(u, v, q_ref, he, hn, wd, kd):
    cos, sin = frame(q_ref)
    cos = K1 * cos
    sin = K1 * sin
    fill_lanes(wd, BACK_TAPS)
    fill_rows(kd, BACK_TAPS)

    def step(g, carry):
        for kk in range(4):
            here = pl.ds(pl.multiple_of(g * (4 * ROWS), 4 * ROWS) + kk * ROWS, ROWS)
            east = cos * u[here, :] - sin * v[here, :]
            north = sin * u[here, :] + cos * v[here, :]
            he[here, :] = east + roll(east, -1, 1)
            hn[here, :] = north + roll(north, -1, 0)
        return carry

    lax.fori_loop(0, LEVELS // 4, step, 0)


def final_kernel(mom, basis, row_seam, nt_fix, lane_seam, et_fix, lev_ref, q_ref, b1, b2, he_ref, hn_ref,
                 fe1, fe2, fn1, fn2, wd, kd, et, nt, th_out, sa_out, ea_out, na_out, xb,
                 row_fix, lane_fix, th, sa, ea, na, out_sems):
    outs = ((th, th_out), (sa, sa_out), (ea, ea_out), (na, na_out))

    def put(n, g):
        at = pl.ds(g * CHUNK * ROWS, CHUNK * ROWS)
        return pltpu.make_async_copy(outs[n][0].at[at, :], outs[n][1].at[at, :], out_sems.at[n, g])

    cos, sin = frame(q_ref)
    lev = lev_ref[...]
    lane = iota((ROWS, COLS), 1)
    line = jnp.sum(mom[...], axis=0, keepdims=True)
    spot = iota((1, 128), 1)
    m = [jnp.sum(jnp.where(spot == n, line, 0.0), axis=1, keepdims=True) for n in range(12)]
    cf = solve_small(m[0:6])
    cb = solve_small(m[6:12])
    end = vec(basis, 3) + (cf[0] * vec(basis, 0) + cf[1] * vec(basis, 1) + cf[2] * vec(basis, 2))
    adj = cb[0] * vec(basis, 4) + cb[1] * vec(basis, 5) + cb[2] * vec(basis, 6)
    d = vec(basis, 7)
    xb[...] = adj[0:ROWS, 0:COLS]
    ge = (0.5 * GRAVITY) * (roll(end, -1, 1) - roll(end, 1, 1))
    gn = (0.5 * GRAVITY) * (roll(end, -1, 0) - roll(end, 1, 0))
    wide_e = ge + roll(ge, -1, 1)
    wide_n = gn + roll(gn, -1, 0)
    sum_e = K1 * wide_e[0:ROWS, 0:COLS]
    sum_n = K1 * wide_n[0:ROWS, 0:COLS]
    fe = jnp.where(jnp.minimum(d, roll(d, -1, 1)) > 0.0, 0.5 * (roll(adj, -1, 1) - adj), 0.0)
    fn = jnp.where(jnp.minimum(d, roll(d, -1, 0)) > 0.0, 0.5 * (roll(adj, -1, 0) - adj), 0.0)
    be = (fe + roll(fe, 1, 1))[0:ROWS, 0:COLS]
    bn = (fn + roll(fn, 1, 0))[0:ROWS, 0:COLS]

    for side, first in enumerate((-2, 15)):
        vel = []
        for i in range(2):
            r = (first + i) % TALL
            vel.append(row_seam[(6 * side + i) * LEVELS : (6 * side + i + 1) * LEVELS, :] - wide_n[r : r + 1, 0:COLS])
        for t in range(2):
            spots = [(6 * side + 2 + 2 * t + i) * LEVELS for i in range(2)]
            qa, qb = [row_seam[s : s + LEVELS, :] * w for s, w in zip(spots, vel)]
            values = (K7 * qb - K1 * qa, -K1 * qb) if side == 0 else (-K1 * qa, K7 * qa - K1 * qb)
            for i in range(2):
                at = (4 * t + 2 * side + i) * LEVELS
                row_fix[at : at + LEVELS, :] = values[i]
    group = iota((ROWS, 128), 1) % 4
    tiles = [wide_e[0:ROWS, 128 * n : 128 * n + 128] for n in range(3)]
    for side in range(2):
        gg = spread(seam(tiles[2], tiles[0]) if side == 0 else seam(tiles[1], tiles[2]))
        vel = lane_seam[3 * side * ROWS : (3 * side + 1) * ROWS, :] - gg
        keep = (group < 2) if side == 0 else ((group == 1) | (group == 2))
        for t in range(2):
            spot = (3 * side + 1 + t) * ROWS
            f = jnp.where(keep, lane_seam[spot : spot + ROWS, :] * vel, 0.0)
            at = slice(t * ROWS, (t + 1) * ROWS)
            if side == 0:
                fix = jnp.where(group == 2, K7 * roll(f, 1, 1), 0.0) - K1 * roll(f, 2, 1)
                lane_fix[at, :] = jnp.where(group >= 2, fix, 0.0)
            else:
                fix = jnp.where(group == 1, K7 * f, 0.0) - K1 * roll(f, -1, 1)
                lane_fix[at, :] = jnp.where(group < 2, fix, lane_fix[at, :])

    edge = (lane < 2) | (lane >= COLS - 2)
    line8 = iota((8, COLS), 0)

    def step(g, carry):
        turn = 128 - g * (4 * CHUNK)
        packs = [lane_fix[0:ROWS, :], lane_fix[ROWS : 2 * ROWS, :], et_fix[...]]
        packs = [pltpu.roll(p, turn, 1) for p in packs]

        def fix_rows(ref, n):
            return ref.at[pl.ds(pl.multiple_of(n * LEVELS + g * CHUNK, CHUNK), CHUNK), :]

        fixes = [[fix_rows(row_fix, n) for n in range(4)], [fix_rows(row_fix, 4 + n) for n in range(4)],
                 [fix_rows(nt_fix, n) for n in range(4)]]
        block = CHUNK * ROWS
        rows_at = pl.multiple_of(g * block, block)
        for fe_ref, fn_ref, b_ref, out in ((fe1, fn1, b1, th), (fe2, fn2, b2, sa)):
            flow_e = []
            flow_n = []
            for kk in range(CHUNK):
                here = pl.ds(rows_at + kk * ROWS, ROWS)
                flow_e.append(fe_ref[here, :] * (he_ref[here, :] - sum_e))
                flow_n.append(fn_ref[here, :] * (hn_ref[here, :] - sum_n))
            east = dot(jnp.concatenate(split(jnp.concatenate(flow_e, axis=0)), axis=1), wd[...])
            north = dot(kd[...], jnp.concatenate(split(jnp.concatenate(flow_n, axis=0)), axis=0))
            at = pl.ds(rows_at, block)
            out[at, :] = b_ref[at, :] + (east + north)
        for kk in range(CHUNK):
            k = g * CHUNK + kk
            here = pl.ds(rows_at + kk * ROWS, ROWS)
            m = lev > k

            def lane_fixed(x, n):
                z = roll(packs[n], -(4 * kk + 2), 1)
                return jnp.where(edge, x + jnp.concatenate([z, z], axis=1), x)

            def row_fixed(x, n):
                r0, r1, r14, r15 = [f[kk : kk + 1, :] for f in fixes[n]]
                top = jnp.where(line8 == 0, r0, jnp.where(line8 == 1, r1, 0.0))
                low = jnp.where(line8 == 6, r14, jnp.where(line8 == 7, r15, 0.0))
                return x + jnp.concatenate([top, low], axis=0)

            for n, out in enumerate((th, sa)):
                out[here, :] = row_fixed(lane_fixed(out[here, :], n), n)
            eg = jnp.where(m, lane_fixed(et[here, :], 2) + be, 0.0)
            ng = jnp.where(m, row_fixed(nt[here, :], 2) + bn, 0.0)
            ea[here, :] = cos * eg + sin * ng
            na[here, :] = cos * ng - sin * eg
        for n in range(4):
            put(n, g).start()
        return carry

    lax.fori_loop(0, STEPS, step, 0)
    for g in range(STEPS):
        for n in range(4):
            put(n, g).wait()


def params(mib):
    return pltpu.CompilerParams(vmem_limit_bytes=mib * 1024 * 1024)


def far(x):
    return pltpu.with_memory_space_constraint(x, pltpu.HBM)


def sds(*shape):
    return jax.ShapeDtypeStruct(shape, F32)


def swaps(count):
    far, near = [], []
    for i in range(count - 1):
        (far if i % 2 else near).extend([(i, i + 1), (i + 1, i)])
    return far, near


def on_device(theta_start, salt_start, east_velocity, north_velocity, surface_start, wet_levels,
              face_frame, theta_sense, salt_sense, east_sense, north_sense, surface_sense):
    flat = lambda x: x.reshape(LEVELS * ROWS, COLS)
    c1, c2, u, v = map(flat, (theta_start, salt_start, east_velocity, north_velocity))
    b1, b2, es, ns = map(flat, (theta_sense, salt_sense, east_sense, north_sense))
    vol = sds(LEVELS * ROWS, COLS)
    c1, c2, b1, b2, u, v, es, ns = [far(x) for x in (c1, c2, b1, b2, u, v, es, ns)]
    hbm = pl.BlockSpec(memory_space=pltpu.HBM)
    vmem = pl.BlockSpec(memory_space=pltpu.VMEM)
    cubes = pltpu.VMEM((LEVELS * ROWS, COLS), F32)
    sems = lambda n: pltpu.SemaphoreType.DMA((n, STEPS))
    yfar, ynear, f2d, edges, et, nt, b1, b2, u, v, fe1, fe2, fn1, fn2, lev, turns = pl.pallas_call(
        local_kernel,
        in_specs=[hbm] * 12,
        out_specs=[vmem] * 16,
        out_shape=[sds(YROWS, COLS), sds(YROWS, COLS), sds(FIELDS * ROWS, COLS), sds(5 * ROWS, 128)] + [vol] * 10
        + [jax.ShapeDtypeStruct((ROWS, COLS), jnp.int32)] * 2,
        scratch_shapes=[cubes] * 4
        + [pltpu.VMEM((ROWS, COLS), F32)] * 2 + [pltpu.VMEM((2 * COLS, COLS), BF16)] * 2
        + [pltpu.VMEM((CHUNK * (ROWS + 4), 2 * CHUNK * ROWS), BF16)] * 2
        + [pltpu.VMEM((2 * CHUNK * ROWS, COLS), F32)] * 4 + [sems(8), pltpu.SemaphoreType.DMA((4,))],
        compiler_params=params(10),
        name="local",
    )(c1, c2, b1, b2, u, v, es, ns, *[far(x) for x in (wet_levels, face_frame, surface_start, surface_sense)])

    y_far, y_near = swaps(lax.axis_size("ty"))
    x_far, x_near = swaps(lax.axis_size("tx"))
    yfar_in = lax.ppermute(yfar, "ty", y_far)
    ynear_in = lax.ppermute(ynear, "ty", y_near)

    he, hn, wd, kd = pl.pallas_call(
        prepare_kernel,
        in_specs=[vmem] * 3,
        out_specs=[vmem] * 4,
        out_shape=[vol] * 2 + [jax.ShapeDtypeStruct((2 * COLS, COLS), BF16),
                               jax.ShapeDtypeStruct((CHUNK * ROWS, 2 * CHUNK * ROWS), BF16)],
        compiler_params=params(4),
        cost_estimate=pl.CostEstimate(flops=2000000, bytes_accessed=2000000, transcendentals=0),
        name="prepare",
    )(u, v, turns)

    xfar, xnear, ext, edges_ext, nt_fix, row_seam = pl.pallas_call(
        rows_kernel,
        out_shape=[sds(XROWS, 128), sds(XROWS, 128), sds(FIELDS * TALL, COLS),
                   sds(4 * TALL, 128), sds(4 * LEVELS, COLS), sds(12 * LEVELS, COLS)],
        compiler_params=params(4),
        name="rows",
    )(yfar_in, ynear_in, yfar, ynear, f2d, edges)
    xfar_in = lax.ppermute(xfar, "tx", x_far)
    xnear_in = lax.ppermute(xnear, "tx", x_near)

    basis, et_fix, lane_seam, moments = pl.pallas_call(
        columns_kernel,
        in_specs=[vmem] * 5 + [pl.BlockSpec(memory_space=pl.ANY)] * 2,
        out_shape=[sds(8 * TALL, WIDE), sds(ROWS, 128), sds(6 * ROWS, 128), sds(128, 128)],
        compiler_params=params(4),
        name="columns",
    )(xfar_in, xnear_in, ext, edges_ext, edges, he, hn)
    moments = lax.all_to_all(moments, ALL, 0, 0, tiled=True)
    th, sa, ea, na, xb = pl.pallas_call(
        final_kernel,
        in_specs=[vmem] * 20,
        out_specs=[hbm] * 4 + [vmem],
        out_shape=[vol] * 4 + [sds(ROWS, COLS)],
        scratch_shapes=[pltpu.VMEM((8 * LEVELS, COLS), F32), pltpu.VMEM((2 * ROWS, 128), F32)]
        + [cubes] * 4 + [sems(4)],
        compiler_params=params(8),
        name="final",
    )(moments, basis, row_seam, nt_fix, lane_seam, et_fix, lev, turns, b1, b2, he, hn, fe1, fe2, fn1, fn2, wd, kd, et, nt)
    cube = lambda x: x.reshape(LEVELS, ROWS, COLS)
    return cube(th), cube(sa), cube(ea), cube(na), xb


def solution(mesh):
    cube = P(None, "ty", "tx")
    plane = P("ty", "tx")
    return jax.shard_map(
        on_device,
        mesh=mesh,
        in_specs=(cube, cube, cube, cube, plane, plane, plane, cube, cube, cube, cube, plane),
        out_specs=(cube, cube, cube, cube, plane),
        check_vma=False,
    )
```

```python
import functools

import jax
import jax.numpy as jnp
from jax import lax
from jax.experimental import pallas as pl
from jax.experimental.pallas import tpu as pltpu
from jax.sharding import PartitionSpec as P

F32 = jnp.float32
BF16 = jnp.bfloat16
LEVELS = 32
ROWS = 16
COLS = 256
WIDE = 384
TALL = 32
CHUNK = 8
STEPS = LEVELS // CHUNK
FIELDS = 7
D, X0, TE, TN, SS, CE, CN = range(FIELDS)
RAW_AT = {D: 320, X0: 328, SS: 336}
MADE_AT = {TE: 0, TN: 8, CE: 16, CN: 24}
YE = 32
RAW_ROWS = 344
MADE_ROWS = 48
XROWS = 112

RATE = 0.2
GRAVITY = 0.25
STIFF = 2.0 / LEVELS
K7 = 0.5 * RATE * 7.0 / 12.0
K1 = 0.5 * RATE / 12.0
ALL = ("ty", "tx")


def roll(x, shift, axis):
    return pltpu.roll(x, shift % x.shape[axis], axis)


def iota(shape, axis):
    return lax.broadcasted_iota(jnp.int32, shape, axis)


def frame(q_ref):
    q = q_ref[...]
    cos = jnp.where(q == 0, 1.0, jnp.where(q == 2, -1.0, 0.0))
    sin = jnp.where(q == 1, 1.0, jnp.where(q == 3, -1.0, 0.0))
    return cos, sin


def face_levels(lev):
    lane = iota((ROWS, COLS), 1)
    row = iota((ROWS, COLS), 0)
    east = jnp.where(lane < COLS - 1, jnp.minimum(lev, roll(lev, -1, 1)), 0)
    north = jnp.where(row < ROWS - 1, jnp.minimum(lev, roll(lev, -1, 0)), 0)
    return east, north


def split(x):
    hi = x.astype(BF16)
    return hi, (x - hi.astype(F32)).astype(BF16)


def odd_place(axis):
    return lax.rem(lax.axis_index(axis), 2)


def band(delta, taps):
    out = jnp.zeros(delta.shape, F32)
    for at, value in taps:
        out = jnp.where(delta == at, value, out)
    return out


def fill_lanes(ref, taps):
    w = band(iota((COLS, COLS), 0) - iota((COLS, COLS), 1), taps).astype(BF16)
    ref[0:COLS, :] = w
    ref[COLS : 2 * COLS, :] = w


def fill_rows(ref, taps):
    block = CHUNK * ROWS
    r = iota((block, block), 0)
    c = iota((block, block), 1)
    m = jnp.where((r // ROWS) == (c // ROWS), band(c - r, taps), 0.0).astype(BF16)
    ref[:, 0:block] = m
    ref[:, block : 2 * block] = m


def dot(a, b):
    return jnp.dot(a, b, preferred_element_type=F32)


VALUE_TAPS = ((0, 7.0), (1, 7.0), (-1, -1.0), (2, -1.0))
SENSE_TAPS = ((0, -1.0), (1, 1.0))
BACK_TAPS = ((0, 7.0), (-1, 7.0), (1, -1.0), (-2, -1.0))


def rows_of(ref, start, r):
    line = iota((CHUNK, COLS), 0)
    block = ref.at[pl.ds(start, CHUNK * ROWS), :]
    got = jnp.zeros((CHUNK, COLS), F32)
    for kk in range(CHUNK):
        at = kk * ROWS + r
        got = jnp.where(line == kk, block[at : at + 1, :], got)
    return got


def gather_kernel(c1_in, c2_in, b1_in, b2_in, u_in, v_in, lev_in, q_in, x0_in, ss_in,
                  far, near, c1, c2, b1, b2, u, v, lev, q, x0, ss, sems, small_sems):
    small = ((q_in, q), (lev_in, lev), (x0_in, x0), (ss_in, ss))
    small = [pltpu.make_async_copy(a, b, small_sems.at[n]) for n, (a, b) in enumerate(small)]
    moves = ((c1_in, c1), (c2_in, c2), (b1_in, b1), (b2_in, b2), (u_in, u), (v_in, v))

    def copy(n, g):
        at = pl.ds(g * CHUNK * ROWS, CHUNK * ROWS)
        return pltpu.make_async_copy(moves[n][0].at[at, :], moves[n][1].at[at, :], sems.at[n, g])

    for c in small:
        c.start()
    for g in range(STEPS):
        for n in range(6):
            copy(n, g).start()
    for c in small:
        c.wait()
    odd = odd_place("ty")
    cos, sin = frame(q)
    cos = cos[:CHUNK, :]
    sin = sin[:CHUNK, :]

    def step(g, carry):
        for n in range(6):
            copy(n, g).wait()
        start = pl.multiple_of(g * (CHUNK * ROWS), CHUNK * ROWS)
        for a in range(5):
            for r in range(2):
                if a < 4:
                    high, low = [rows_of(moves[a][1], start, n + r) for n in (ROWS - 2, 0)]
                else:
                    high, low = [sin * rows_of(u, start, n + r) + cos * rows_of(v, start, n + r) for n in (ROWS - 2, 0)]
                at = pl.ds(pl.multiple_of((2 * a + r) * LEVELS + g * CHUNK, CHUNK), CHUNK)
                far[at, :] = jnp.where(odd == 1, high, low)
                near[at, :] = jnp.where(odd == 1, low, high)
        return carry

    lax.fori_loop(0, STEPS, step, 0)
    for out, first in ((far, 8 * odd), (near, 8 - 8 * odd)):
        at = pl.ds(pl.multiple_of(first, 8), 8)
        out[RAW_AT[D] : RAW_AT[D] + 8, :] = lev[at, :].astype(F32)
        out[RAW_AT[X0] : RAW_AT[X0] + 8, :] = x0[at, :]
        out[RAW_AT[SS] : RAW_AT[SS] + 8, :] = ss[at, :]


def local_kernel(t1, t2, b1, b2, u, v, es_in, ns_in, lev_ref, q_ref, x0_ref, ss_ref,
                 far, near, f2d, edges, et, nt, fe1, fe2, fn1, fn2, es, ns, wc, wb, kc, kb, ce, cn, be, bn, sems):
    moves = ((es_in, es), (ns_in, ns))

    def copy(n, g):
        at = pl.ds(g * CHUNK * ROWS, CHUNK * ROWS)
        return pltpu.make_async_copy(moves[n][0].at[at, :], moves[n][1].at[at, :], sems.at[n, g])

    for g in range(STEPS):
        for n in range(2):
            copy(n, g).start()
    fill_lanes(wc, VALUE_TAPS)
    fill_lanes(wb, SENSE_TAPS)
    odd = odd_place("ty")
    fill_rows(kc, VALUE_TAPS)
    fill_rows(kb, SENSE_TAPS)
    cos, sin = frame(q_ref)
    lev = lev_ref[...]
    east_lev, north_lev = face_levels(lev)
    lane128 = iota((ROWS, 128), 1)
    f2d[...] = jnp.zeros_like(f2d)
    edges[...] = jnp.zeros_like(edges)

    def field(f):
        return slice(f * ROWS, (f + 1) * ROWS)

    def step(g, carry):
        acc_u = jnp.zeros((ROWS, COLS), F32)
        acc_v = jnp.zeros((ROWS, COLS), F32)
        acc_e = jnp.zeros((ROWS, COLS), F32)
        acc_n = jnp.zeros((ROWS, COLS), F32)
        packs = [jnp.zeros((ROWS, 128), F32) for _ in range(5)]
        block = CHUNK * ROWS
        rows_at = pl.multiple_of(g * block, block)
        for a, (src, w, k_rows, east, north) in enumerate(
            ((t1, wc, kc, ce, cn), (t2, wc, kc, ce, cn), (b1, wb, kb, be, bn), (b2, wb, kb, be, bn))
        ):
            hi, lo = split(src[pl.ds(rows_at, block), :])
            at = slice((a % 2) * block, (a % 2 + 1) * block)
            east[at, :] = dot(jnp.concatenate([hi, lo], axis=1), w[...])
            north[at, :] = dot(k_rows[...], jnp.concatenate([hi, lo], axis=0))
        for n in range(2):
            copy(n, g).wait()
        for kk in range(CHUNK):
            k = g * CHUNK + kk
            here = pl.ds(rows_at + kk * ROWS, ROWS)
            m = lev > k
            me = east_lev > k
            mn = north_lev > k
            ve = None
            vn = None
            for t, (fe_ref, fn_ref) in enumerate(((fe1, fn1), (fe2, fn2))):
                at = slice(t * block + kk * ROWS, t * block + (kk + 1) * ROWS)
                fe = jnp.where(me, be[at, :], 0.0)
                fn = jnp.where(mn, bn[at, :], 0.0)
                fe_ref[here, :] = fe
                fn_ref[here, :] = fn
                ve_t = fe * ce[at, :]
                vn_t = fn * cn[at, :]
                ve = ve_t if ve is None else ve + ve_t
                vn = vn_t if vn is None else vn + vn_t
            ve = K1 * ve
            vn = K1 * vn
            es_k = es[here, :]
            ns_k = ns[here, :]
            u_k = u[here, :]
            v_k = v[here, :]
            et_k = cos * es_k - sin * ns_k + (ve + roll(ve, 1, 1))
            nt_k = sin * es_k + cos * ns_k + (vn + roll(vn, 1, 0))
            et[here, :] = et_k
            nt[here, :] = nt_k
            acc_e = acc_e + jnp.where(m, et_k, 0.0)
            acc_n = acc_n + jnp.where(m, nt_k, 0.0)
            acc_u = acc_u + jnp.where(m, u_k, 0.0)
            acc_v = acc_v + jnp.where(m, v_k, 0.0)

            def ends(x):
                return jnp.where(lane128 < 2, x[:, :128], x[:, 128:])

            spot = (lane128 // 4) == kk
            packed = [ends(r[here, :]) for r in (t1, t2, b1, b2)]
            packed.append(cos[:, :128] * ends(u_k) - sin[:, :128] * ends(v_k))
            for n in range(5):
                packs[n] = jnp.where(spot, roll(packed[n], 4 * kk + 2, 1), packs[n])

        for n in range(5):
            at = slice(n * ROWS, (n + 1) * ROWS)
            edges[at, :] = edges[at, :] + pltpu.roll(packs[n], g * (4 * CHUNK), 1)
        f2d[field(TE), :] = f2d[field(TE), :] + (cos * acc_u - sin * acc_v)
        f2d[field(TN), :] = f2d[field(TN), :] + (sin * acc_u + cos * acc_v)
        f2d[field(CE), :] = f2d[field(CE), :] + acc_e
        f2d[field(CN), :] = f2d[field(CN), :] + acc_n
        return carry

    lax.fori_loop(0, STEPS, step, 0)
    f2d[field(D), :] = lev.astype(F32)
    f2d[field(X0), :] = x0_ref[...]
    f2d[field(SS), :] = ss_ref[...]
    for out, first in ((far, 8 * odd), (near, 8 - 8 * odd)):
        for f, spot in MADE_AT.items():
            out[spot : spot + 8, :] = f2d[pl.ds(pl.multiple_of(f * ROWS + first, 8), 8), :]
        for n in range(4):
            at = YE + 8 * (n // 2)
            side = 128 * (n % 2)
            out[at : at + 8, side : side + 128] = edges[pl.ds(pl.multiple_of(n * ROWS + first, 8), 8), :]


def row_boundary(low, high, lev_a2, lev_a1, lev_b1, lev_b2):
    level = iota((LEVELS, COLS), 0).astype(F32)
    mask_a = level < jnp.minimum(lev_a2, lev_a1)
    mask_0 = level < jnp.minimum(lev_a1, lev_b1)
    mask_b = level < jnp.minimum(lev_b1, lev_b2)

    def part(ref, a, r):
        return ref[(2 * a + r) * LEVELS : (2 * a + r + 1) * LEVELS, :]

    va = v0 = vb = None
    diffs = []
    for t in range(2):
        ca2, ca1 = part(low, t, 0), part(low, t, 1)
        cb1, cb2 = part(high, t, 0), part(high, t, 1)
        ga2, ga1 = part(low, 2 + t, 0), part(low, 2 + t, 1)
        gb1, gb2 = part(high, 2 + t, 0), part(high, 2 + t, 1)
        fa = jnp.where(mask_a, ga1 - ga2, 0.0)
        f0 = jnp.where(mask_0, gb1 - ga1, 0.0)
        fb = jnp.where(mask_b, gb2 - gb1, 0.0)
        diffs.append((fa, f0, fb))
        fa = fa * (-K1 * cb1)
        f0 = f0 * (K7 * (ca1 + cb1) - K1 * (ca2 + cb2))
        fb = fb * (-K1 * ca1)
        va = fa if va is None else va + fa
        v0 = f0 if v0 is None else v0 + f0
        vb = fb if vb is None else vb + fb
    vel = [part(low, 4, 0), part(low, 4, 1), part(high, 4, 0), part(high, 4, 1)]
    return va, va + v0, v0 + vb, vb, diffs, vel


def rows_kernel(far_in, near_in, far_out, near_out, made_far, made_near, *rest):
    odd = odd_place("ty")

    @pl.when(odd == 1)
    def _():
        rows_body(near_in, far_in, far_out, near_out, made_near, made_far, *rest)

    @pl.when(odd == 0)
    def _():
        rows_body(far_in, near_in, near_out, far_out, made_far, made_near, *rest)


def rows_body(ylo, yhi, yup, ydn, mlo, mhi, f2d, edges, xfar, xnear, ext, edges_ext, nt_fix, row_seam):
    d0 = f2d[0:1, :]
    d1 = f2d[1:2, :]
    d14 = f2d[ROWS - 2 : ROWS - 1, :]
    d15 = f2d[ROWS - 1 : ROWS, :]
    dlo = ylo[RAW_AT[D] : RAW_AT[D] + 8, :]
    dhi = yhi[RAW_AT[D] : RAW_AT[D] + 8, :]
    lo = row_boundary(ylo, ydn, dlo[6:7, :], dlo[7:8, :], d0, d1)
    hi = row_boundary(yup, yhi, d14, d15, dhi[0:1, :], dhi[1:2, :])
    for side, (out, at) in enumerate(((lo, 0), (hi, 1))):
        diffs, vel = out[4], out[5]
        for i in range(2):
            spot = (6 * side + i) * LEVELS
            row_seam[spot : spot + LEVELS, :] = vel[at + i] + vel[at + i + 1]
            for t in range(2):
                spot = (6 * side + 2 + 2 * t + i) * LEVELS
                row_seam[spot : spot + LEVELS, :] = diffs[t][at + i]
    for n, value in enumerate((lo[2], lo[3], hi[0], hi[1])):
        nt_fix[n * LEVELS : (n + 1) * LEVELS, :] = value
    for f in range(FIELDS):
        ext[f * TALL : f * TALL + ROWS, :] = f2d[f * ROWS : (f + 1) * ROWS, :]
        above, below, spot = (yhi, ylo, RAW_AT[f]) if f in RAW_AT else (mhi, mlo, MADE_AT[f])
        ext[f * TALL + 16 : f * TALL + 24, :] = above[spot : spot + 8, :]
        ext[f * TALL + 24 : f * TALL + 32, :] = below[spot : spot + 8, :]
    spots = ((30, lo[0]), (31, lo[1]), (0, lo[2]), (1, lo[3]),
             (14, hi[0]), (15, hi[1]), (16, hi[2]), (17, hi[3]))
    for r, value in spots:
        at = slice(CN * TALL + r, CN * TALL + r + 1)
        ext[at, :] = ext[at, :] + jnp.sum(value, axis=0, keepdims=True)
    for n in range(4):
        at = YE + 8 * (n // 2)
        side = 128 * (n % 2)
        edges_ext[n * TALL : n * TALL + ROWS, :] = edges[n * ROWS : (n + 1) * ROWS, :]
        edges_ext[n * TALL + 16 : n * TALL + 24, :] = mhi[at : at + 8, side : side + 128]
        edges_ext[n * TALL + 24 : n * TALL + 32, :] = mlo[at : at + 8, side : side + 128]
    lane = iota((TALL, 128), 1)
    pr = jnp.zeros((TALL, 128), F32)
    pl_ = jnp.zeros((TALL, 128), F32)
    for f in range(FIELDS):
        spot = (lane // 8) == f
        z = ext[f * TALL : (f + 1) * TALL, :]
        pr = jnp.where(spot, roll(z[:, 128:], 8 * f + 8, 1), pr)
        pl_ = jnp.where(spot, roll(z[:, :128], 8 * f, 1), pl_)
    oddx = odd_place("tx") == 1

    def send(at, right, left):
        xfar[at, :] = jnp.where(oddx, right, left)
        xnear[at, :] = jnp.where(oddx, left, right)

    send(slice(0, TALL), pr, pl_)
    first = (lane % 4) < 2
    for pair in range(2):
        p = edges_ext[2 * pair * TALL : (2 * pair + 1) * TALL, :]
        s = edges_ext[(2 * pair + 1) * TALL : (2 * pair + 2) * TALL, :]
        at = slice((1 + pair) * TALL, (2 + pair) * TALL)
        send(at, jnp.where(first, p, roll(s, 2, 1)), jnp.where(first, roll(s, -2, 1), p))
    own = edges[4 * ROWS : 5 * ROWS, :]
    send(slice(96, 112), own, own)


def spread(x):
    lane = iota(x.shape, 1)
    x = jnp.where(lane < 4, x, 0.0)
    for s in (4, 8, 16, 32, 64):
        x = x + roll(x, s, 1)
    return x


def seam(left_tile, right_tile):
    lane = iota(left_tile.shape, 1)
    return roll(jnp.where(lane >= 126, left_tile, right_tile), 2, 1)


def joined(lo_ref, hi_ref, edges_ext, pair, which, rows):
    own = edges_ext[(2 * pair + which) * TALL : (2 * pair + which) * TALL + rows, :]
    first = (iota((rows, 128), 1) % 4) < 2
    at = slice((1 + pair) * TALL, (1 + pair) * TALL + rows)
    lo = lo_ref[at, :]
    hi = hi_ref[at, :]
    if which == 1:
        lo = roll(lo, -2, 1)
        hi = roll(hi, 2, 1)
    return jnp.where(first, lo, own), jnp.where(first, own, hi)


def columns_kernel(far_in, near_in, ext, edges_ext, edges, he, hn, basis, et_fix, lane_seam, moments):
    oddx = odd_place("tx") == 1
    xlo = jnp.where(oddx, near_in[...], far_in[...])
    xhi = jnp.where(oddx, far_in[...], near_in[...])
    lane = iota((TALL, 128), 1)
    group = lane % 4
    level = (lane // 4).astype(F32)
    tiles = []
    for f in range(FIELDS):
        z = ext[f * TALL : (f + 1) * TALL, :]
        right = roll(xhi[0:TALL, :], -8 * f, 1)
        left = roll(xlo[0:TALL, :], 120 - 8 * f, 1)
        third = jnp.where(lane < 8, right, jnp.where(lane >= 120, left, 0.0))
        tiles.append([z[:, :128], z[:, 128:], third])
    coef7 = jnp.where(group == 1, K7, 0.0)
    coefm = jnp.where((group == 1) | (group == 2), -K1, 0.0)
    coefp = jnp.where(group < 2, -K1, 0.0)
    cells = []
    for side in range(2):
        d = tiles[D]
        lev = spread(seam(d[2], d[0]) if side == 0 else seam(d[1], d[2]))
        wet = (level < jnp.minimum(lev, roll(lev, -1, 1))) & (group < 3)
        w = None
        for t in range(2):
            c = joined(xlo, xhi, edges_ext, 0, t, TALL)[side]
            b = joined(xlo, xhi, edges_ext, 1, t, TALL)[side]
            f = jnp.where(wet, roll(b, -1, 1) - b, 0.0)
            spot = (3 * side + 1 + t) * ROWS
            lane_seam[spot : spot + ROWS, :] = f[0:ROWS, :]
            term = f * (coef7 * (c + roll(c, -1, 1)) + coefm * roll(c, 1, 1) + coefp * roll(c, -2, 1))
            w = term if w is None else w + term
        cell = w + roll(w, 1, 1)
        cells.append(cell)
        total = cell
        for s in (4, 8, 16, 32, 64):
            total = total + roll(total, s, 1)
        total = roll(total, -2, 1)
        a, b = (2, 0) if side == 0 else (1, 2)
        tiles[CE][a] = tiles[CE][a] + jnp.where(lane >= 126, total, 0.0)
        tiles[CE][b] = tiles[CE][b] + jnp.where(lane < 2, total, 0.0)
    et_fix[...] = jnp.where(group < 2, cells[1], cells[0])[0:ROWS, :]
    own_u = edges[4 * ROWS : 5 * ROWS, :]
    half = group[0:ROWS, :] < 2
    for side, uu in enumerate((jnp.where(half, xlo[96:112, :], own_u), jnp.where(half, own_u, xhi[96:112, :]))):
        lane_seam[3 * side * ROWS : (3 * side + 1) * ROWS, :] = uu + roll(uu, -1, 1)

    full = [jnp.concatenate(t, axis=1) for t in tiles]
    d = full[D]
    near_e = jnp.minimum(d, roll(d, -1, 1))
    near_n = jnp.minimum(d, roll(d, -1, 0))
    we = STIFF * near_e
    wn = STIFF * near_n
    half_e = jnp.where(near_e > 0.0, 0.5, 0.0)
    half_n = jnp.where(near_n > 0.0, 0.5, 0.0)
    x0 = full[X0]
    flux_e = half_e * (full[TE] + roll(full[TE], -1, 1)) + we * (x0 - roll(x0, -1, 1))
    flux_n = half_n * (full[TN] + roll(full[TN], -1, 0)) + wn * (x0 - roll(x0, -1, 0))
    r = (roll(flux_e, 1, 1) - flux_e) + (roll(flux_n, 1, 0) - flux_n)
    b = full[SS] + (0.5 * GRAVITY) * (
        (roll(full[CE], -1, 1) - roll(full[CE], 1, 1)) + (roll(full[CN], -1, 0) - roll(full[CN], 1, 0))
    )

    def own_sum(x):
        part = x[0:ROWS, 0:128] + x[0:ROWS, 128:256]
        return jnp.sum(part, axis=0, keepdims=True)

    sums = []
    for n, start in enumerate((r, b)):
        vec = start
        for power in range(3):
            basis[(4 * n + power) * TALL : (4 * n + power + 1) * TALL, :] = vec
            sums.append(own_sum(vec * vec))
            de = vec - roll(vec, -1, 1)
            dn = vec - roll(vec, -1, 0)
            he = we * de
            hn = wn * dn
            sums.append(own_sum(he * de + hn * dn))
            if power < 2:
                vec = (he - roll(he, 1, 1)) + (hn - roll(hn, 1, 0))
    basis[3 * TALL : 4 * TALL, :] = x0
    basis[7 * TALL : 8 * TALL, :] = d
    spot_lane = iota((1, 128), 1)
    line = jnp.zeros((1, 128), F32)
    for n, s in enumerate(sums):
        line = line + jnp.where(spot_lane == n, jnp.sum(s, axis=1, keepdims=True), 0.0)
    moments[...] = jnp.broadcast_to(line, (128, 128))


def safe_ratio(top, bottom, limit):
    ok = bottom > 0.0
    return jnp.clip(jnp.where(ok, top / jnp.where(ok, bottom, 1.0), 0.0), 0.0, limit)


def solve_small(m):
    bound = 8.0 * STIFF * LEVELS
    a0 = m[1] / m[0]
    n1 = m[2] - a0 * m[1]
    b1 = safe_ratio(n1, m[0], bound * bound)
    a1 = safe_ratio(m[3] - a0 * (2.0 * m[2] - a0 * m[1]), n1, bound)
    s = a0 + a1
    t = a0 * a1 - b1
    n2 = m[4] - s * m[3] + t * m[2]
    b2 = safe_ratio(n2, n1, bound * bound)
    top = m[5] - 2.0 * s * m[4] + (s * s + 2.0 * t) * m[3] - 2.0 * s * t * m[2] + t * t * m[1]
    a2 = safe_ratio(top, n2, bound)
    e2 = 1.0 + a2
    e1 = jnp.maximum(1.0 + a1 - b2 / e2, 1.0)
    e0 = jnp.maximum(1.0 + a0 - b1 / e1, 1.0)
    y0 = 1.0 / e0
    y1 = -y0 / e1
    y2 = -y1 / e2
    return y0 - a0 * y1 + t * y2, y1 - s * y2, y2


def vec(ref, n):
    return ref[n * TALL : (n + 1) * TALL, :]


def prepare_kernel(u, v, q_ref, he, hn, wd, kd):
    cos, sin = frame(q_ref)
    cos = K1 * cos
    sin = K1 * sin
    fill_lanes(wd, BACK_TAPS)
    fill_rows(kd, BACK_TAPS)

    def step(g, carry):
        for kk in range(4):
            here = pl.ds(pl.multiple_of(g * (4 * ROWS), 4 * ROWS) + kk * ROWS, ROWS)
            east = cos * u[here, :] - sin * v[here, :]
            north = sin * u[here, :] + cos * v[here, :]
            he[here, :] = east + roll(east, -1, 1)
            hn[here, :] = north + roll(north, -1, 0)
        return carry

    lax.fori_loop(0, LEVELS // 4, step, 0)


def final_kernel(mom, basis, row_seam, nt_fix, lane_seam, et_fix, lev_ref, q_ref, b1, b2, he_ref, hn_ref,
                 fe1, fe2, fn1, fn2, wd, kd, et, nt, th_out, sa_out, ea_out, na_out, xb,
                 row_fix, lane_fix, th, sa, ea, na, out_sems):
    outs = ((th, th_out), (sa, sa_out), (ea, ea_out), (na, na_out))

    def put(n, g):
        at = pl.ds(g * CHUNK * ROWS, CHUNK * ROWS)
        return pltpu.make_async_copy(outs[n][0].at[at, :], outs[n][1].at[at, :], out_sems.at[n, g])

    cos, sin = frame(q_ref)
    lev = lev_ref[...]
    lane = iota((ROWS, COLS), 1)
    line = jnp.sum(mom[...], axis=0, keepdims=True)
    spot = iota((1, 128), 1)
    m = [jnp.sum(jnp.where(spot == n, line, 0.0), axis=1, keepdims=True) for n in range(12)]
    cf = solve_small(m[0:6])
    cb = solve_small(m[6:12])
    end = vec(basis, 3) + (cf[0] * vec(basis, 0) + cf[1] * vec(basis, 1) + cf[2] * vec(basis, 2))
    adj = cb[0] * vec(basis, 4) + cb[1] * vec(basis, 5) + cb[2] * vec(basis, 6)
    d = vec(basis, 7)
    xb[...] = adj[0:ROWS, 0:COLS]
    ge = (0.5 * GRAVITY) * (roll(end, -1, 1) - roll(end, 1, 1))
    gn = (0.5 * GRAVITY) * (roll(end, -1, 0) - roll(end, 1, 0))
    wide_e = ge + roll(ge, -1, 1)
    wide_n = gn + roll(gn, -1, 0)
    sum_e = K1 * wide_e[0:ROWS, 0:COLS]
    sum_n = K1 * wide_n[0:ROWS, 0:COLS]
    fe = jnp.where(jnp.minimum(d, roll(d, -1, 1)) > 0.0, 0.5 * (roll(adj, -1, 1) - adj), 0.0)
    fn = jnp.where(jnp.minimum(d, roll(d, -1, 0)) > 0.0, 0.5 * (roll(adj, -1, 0) - adj), 0.0)
    be = (fe + roll(fe, 1, 1))[0:ROWS, 0:COLS]
    bn = (fn + roll(fn, 1, 0))[0:ROWS, 0:COLS]

    for side, first in enumerate((-2, 15)):
        vel = []
        for i in range(2):
            r = (first + i) % TALL
            vel.append(row_seam[(6 * side + i) * LEVELS : (6 * side + i + 1) * LEVELS, :] - wide_n[r : r + 1, 0:COLS])
        for t in range(2):
            spots = [(6 * side + 2 + 2 * t + i) * LEVELS for i in range(2)]
            qa, qb = [row_seam[s : s + LEVELS, :] * w for s, w in zip(spots, vel)]
            values = (K7 * qb - K1 * qa, -K1 * qb) if side == 0 else (-K1 * qa, K7 * qa - K1 * qb)
            for i in range(2):
                at = (4 * t + 2 * side + i) * LEVELS
                row_fix[at : at + LEVELS, :] = values[i]
    group = iota((ROWS, 128), 1) % 4
    tiles = [wide_e[0:ROWS, 128 * n : 128 * n + 128] for n in range(3)]
    for side in range(2):
        gg = spread(seam(tiles[2], tiles[0]) if side == 0 else seam(tiles[1], tiles[2]))
        vel = lane_seam[3 * side * ROWS : (3 * side + 1) * ROWS, :] - gg
        keep = (group < 2) if side == 0 else ((group == 1) | (group == 2))
        for t in range(2):
            spot = (3 * side + 1 + t) * ROWS
            f = jnp.where(keep, lane_seam[spot : spot + ROWS, :] * vel, 0.0)
            at = slice(t * ROWS, (t + 1) * ROWS)
            if side == 0:
                fix = jnp.where(group == 2, K7 * roll(f, 1, 1), 0.0) - K1 * roll(f, 2, 1)
                lane_fix[at, :] = jnp.where(group >= 2, fix, 0.0)
            else:
                fix = jnp.where(group == 1, K7 * f, 0.0) - K1 * roll(f, -1, 1)
                lane_fix[at, :] = jnp.where(group < 2, fix, lane_fix[at, :])

    edge = (lane < 2) | (lane >= COLS - 2)
    line8 = iota((8, COLS), 0)

    def step(g, carry):
        turn = 128 - g * (4 * CHUNK)
        packs = [lane_fix[0:ROWS, :], lane_fix[ROWS : 2 * ROWS, :], et_fix[...]]
        packs = [pltpu.roll(p, turn, 1) for p in packs]

        def fix_rows(ref, n):
            return ref.at[pl.ds(pl.multiple_of(n * LEVELS + g * CHUNK, CHUNK), CHUNK), :]

        fixes = [[fix_rows(row_fix, n) for n in range(4)], [fix_rows(row_fix, 4 + n) for n in range(4)],
                 [fix_rows(nt_fix, n) for n in range(4)]]
        block = CHUNK * ROWS
        rows_at = pl.multiple_of(g * block, block)
        for fe_ref, fn_ref, b_ref, out in ((fe1, fn1, b1, th), (fe2, fn2, b2, sa)):
            flow_e = []
            flow_n = []
            for kk in range(CHUNK):
                here = pl.ds(rows_at + kk * ROWS, ROWS)
                flow_e.append(fe_ref[here, :] * (he_ref[here, :] - sum_e))
                flow_n.append(fn_ref[here, :] * (hn_ref[here, :] - sum_n))
            east = dot(jnp.concatenate(split(jnp.concatenate(flow_e, axis=0)), axis=1), wd[...])
            north = dot(kd[...], jnp.concatenate(split(jnp.concatenate(flow_n, axis=0)), axis=0))
            at = pl.ds(rows_at, block)
            out[at, :] = b_ref[at, :] + (east + north)
        for kk in range(CHUNK):
            k = g * CHUNK + kk
            here = pl.ds(rows_at + kk * ROWS, ROWS)
            m = lev > k

            def lane_fixed(x, n):
                z = roll(packs[n], -(4 * kk + 2), 1)
                return jnp.where(edge, x + jnp.concatenate([z, z], axis=1), x)

            def row_fixed(x, n):
                r0, r1, r14, r15 = [f[kk : kk + 1, :] for f in fixes[n]]
                top = jnp.where(line8 == 0, r0, jnp.where(line8 == 1, r1, 0.0))
                low = jnp.where(line8 == 6, r14, jnp.where(line8 == 7, r15, 0.0))
                return x + jnp.concatenate([top, low], axis=0)

            for n, out in enumerate((th, sa)):
                out[here, :] = row_fixed(lane_fixed(out[here, :], n), n)
            eg = jnp.where(m, lane_fixed(et[here, :], 2) + be, 0.0)
            ng = jnp.where(m, row_fixed(nt[here, :], 2) + bn, 0.0)
            ea[here, :] = cos * eg + sin * ng
            na[here, :] = cos * ng - sin * eg
        for n in range(4):
            put(n, g).start()
        return carry

    lax.fori_loop(0, STEPS, step, 0)
    for g in range(STEPS):
        for n in range(4):
            put(n, g).wait()


def params(mib):
    return pltpu.CompilerParams(vmem_limit_bytes=mib * 1024 * 1024)


def far(x):
    return pltpu.with_memory_space_constraint(x, pltpu.HBM)


def sds(*shape):
    return jax.ShapeDtypeStruct(shape, F32)


def swaps(count):
    far, near = [], []
    for i in range(count - 1):
        (far if i % 2 else near).extend([(i, i + 1), (i + 1, i)])
    return far, near


def on_device(theta_start, salt_start, east_velocity, north_velocity, surface_start, wet_levels,
              face_frame, theta_sense, salt_sense, east_sense, north_sense, surface_sense):
    flat = lambda x: x.reshape(LEVELS * ROWS, COLS)
    c1, c2, u, v = map(flat, (theta_start, salt_start, east_velocity, north_velocity))
    b1, b2, es, ns = map(flat, (theta_sense, salt_sense, east_sense, north_sense))
    vol = sds(LEVELS * ROWS, COLS)
    c1, c2, b1, b2, u, v, es, ns = [far(x) for x in (c1, c2, b1, b2, u, v, es, ns)]
    hbm = pl.BlockSpec(memory_space=pltpu.HBM)
    vmem = pl.BlockSpec(memory_space=pltpu.VMEM)
    cubes = pltpu.VMEM((LEVELS * ROWS, COLS), F32)
    sems = lambda n: pltpu.SemaphoreType.DMA((n, STEPS))
    ints = jax.ShapeDtypeStruct((ROWS, COLS), jnp.int32)
    small = [far(x) for x in (wet_levels, face_frame, surface_start, surface_sense)]
    raw_far, raw_near, c1, c2, b1, b2, u, v, lev, turns, x0, ss = pl.pallas_call(
        gather_kernel,
        in_specs=[hbm] * 10,
        out_specs=[vmem] * 12,
        out_shape=[sds(RAW_ROWS, COLS)] * 2 + [vol] * 6 + [ints] * 2 + [sds(ROWS, COLS)] * 2,
        scratch_shapes=[sems(6), pltpu.SemaphoreType.DMA((4,))],
        compiler_params=params(4),
        cost_estimate=pl.CostEstimate(flops=4000000, bytes_accessed=6000000, transcendentals=0),
        name="gather",
    )(c1, c2, b1, b2, u, v, *small)
    y_far, y_near = swaps(lax.axis_size("ty"))
    x_far, x_near = swaps(lax.axis_size("tx"))
    raw_far_in = lax.ppermute(raw_far, "ty", y_far)
    raw_near_in = lax.ppermute(raw_near, "ty", y_near)

    made_far, made_near, f2d, edges, et, nt, fe1, fe2, fn1, fn2 = pl.pallas_call(
        local_kernel,
        in_specs=[vmem] * 6 + [hbm] * 2 + [vmem] * 4,
        out_specs=[vmem] * 10,
        out_shape=[sds(MADE_ROWS, COLS)] * 2 + [sds(FIELDS * ROWS, COLS), sds(5 * ROWS, 128)] + [vol] * 6,
        scratch_shapes=[cubes] * 2 + [pltpu.VMEM((2 * COLS, COLS), BF16)] * 2
        + [pltpu.VMEM((CHUNK * ROWS, 2 * CHUNK * ROWS), BF16)] * 2
        + [pltpu.VMEM((2 * CHUNK * ROWS, COLS), F32)] * 4 + [sems(2)],
        compiler_params=params(8),
        cost_estimate=pl.CostEstimate(flops=20000000, bytes_accessed=8000000, transcendentals=0),
        name="local",
    )(c1, c2, b1, b2, u, v, es, ns, lev, turns, x0, ss)
    made_far_in = lax.ppermute(made_far, "ty", y_far)
    made_near_in = lax.ppermute(made_near, "ty", y_near)

    he, hn, wd, kd = pl.pallas_call(
        prepare_kernel,
        in_specs=[vmem] * 3,
        out_specs=[vmem] * 4,
        out_shape=[vol] * 2 + [jax.ShapeDtypeStruct((2 * COLS, COLS), BF16),
                               jax.ShapeDtypeStruct((CHUNK * ROWS, 2 * CHUNK * ROWS), BF16)],
        compiler_params=params(4),
        cost_estimate=pl.CostEstimate(flops=2000000, bytes_accessed=2000000, transcendentals=0),
        name="prepare",
    )(u, v, turns)

    xfar, xnear, ext, edges_ext, nt_fix, row_seam = pl.pallas_call(
        rows_kernel,
        out_shape=[sds(XROWS, 128), sds(XROWS, 128), sds(FIELDS * TALL, COLS),
                   sds(4 * TALL, 128), sds(4 * LEVELS, COLS), sds(12 * LEVELS, COLS)],
        compiler_params=params(4),
        name="rows",
    )(raw_far_in, raw_near_in, raw_far, raw_near, made_far_in, made_near_in, f2d, edges)
    xfar_in = lax.ppermute(xfar, "tx", x_far)
    xnear_in = lax.ppermute(xnear, "tx", x_near)

    basis, et_fix, lane_seam, moments = pl.pallas_call(
        columns_kernel,
        in_specs=[vmem] * 5 + [pl.BlockSpec(memory_space=pl.ANY)] * 2,
        out_shape=[sds(8 * TALL, WIDE), sds(ROWS, 128), sds(6 * ROWS, 128), sds(128, 128)],
        compiler_params=params(4),
        name="columns",
    )(xfar_in, xnear_in, ext, edges_ext, edges, he, hn)
    moments = lax.all_to_all(moments, ALL, 0, 0, tiled=True)
    th, sa, ea, na, xb = pl.pallas_call(
        final_kernel,
        in_specs=[vmem] * 20,
        out_specs=[hbm] * 4 + [vmem],
        out_shape=[vol] * 4 + [sds(ROWS, COLS)],
        scratch_shapes=[pltpu.VMEM((8 * LEVELS, COLS), F32), pltpu.VMEM((2 * ROWS, 128), F32)]
        + [cubes] * 4 + [sems(4)],
        compiler_params=params(8),
        name="final",
    )(moments, basis, row_seam, nt_fix, lane_seam, et_fix, lev, turns, b1, b2, he, hn, fe1, fe2, fn1, fn2, wd, kd, et, nt)
    cube = lambda x: x.reshape(LEVELS, ROWS, COLS)
    return cube(th), cube(sa), cube(ea), cube(na), xb


def solution(mesh):
    cube = P(None, "ty", "tx")
    plane = P("ty", "tx")
    return jax.shard_map(
        on_device,
        mesh=mesh,
        in_specs=(cube, cube, cube, cube, plane, plane, plane, cube, cube, cube, cube, plane),
        out_specs=(cube, cube, cube, cube, plane),
        check_vma=False,
    )
```

```python
import functools

import jax
import jax.numpy as jnp
from jax import lax
from jax.experimental import pallas as pl
from jax.experimental.pallas import tpu as pltpu
from jax.sharding import PartitionSpec as P

F32 = jnp.float32
BF16 = jnp.bfloat16
LEVELS = 32
ROWS = 16
COLS = 256
WIDE = 384
TALL = 32
CHUNK = 8
STEPS = LEVELS // CHUNK
FIELDS = 7
D, X0, TE, TN, SS, CE, CN = range(FIELDS)
RAW_AT = {D: 320, X0: 328, SS: 336}
MADE_AT = {TE: 0, TN: 8, CE: 16, CN: 24}
YE = 32
RAW_ROWS = 344
MADE_ROWS = 48
XROWS = 96

RATE = 0.2
GRAVITY = 0.25
STIFF = 2.0 / LEVELS
K7 = 0.5 * RATE * 7.0 / 12.0
K1 = 0.5 * RATE / 12.0
ALL = ("ty", "tx")


def roll(x, shift, axis):
    return pltpu.roll(x, shift % x.shape[axis], axis)


def iota(shape, axis):
    return lax.broadcasted_iota(jnp.int32, shape, axis)


def frame(q_ref):
    q = q_ref[...]
    cos = jnp.where(q == 0, 1.0, jnp.where(q == 2, -1.0, 0.0))
    sin = jnp.where(q == 1, 1.0, jnp.where(q == 3, -1.0, 0.0))
    return cos, sin


def face_levels(lev):
    lane = iota((ROWS, COLS), 1)
    row = iota((ROWS, COLS), 0)
    east = jnp.where(lane < COLS - 1, jnp.minimum(lev, roll(lev, -1, 1)), 0)
    north = jnp.where(row < ROWS - 1, jnp.minimum(lev, roll(lev, -1, 0)), 0)
    return east, north


def split(x):
    hi = x.astype(BF16)
    return hi, (x - hi.astype(F32)).astype(BF16)


def odd_place(axis):
    return lax.rem(lax.axis_index(axis), 2)


def band(delta, taps):
    out = jnp.zeros(delta.shape, F32)
    for at, value in taps:
        out = jnp.where(delta == at, value, out)
    return out


def fill_lanes(ref, taps):
    w = band(iota((COLS, COLS), 0) - iota((COLS, COLS), 1), taps).astype(BF16)
    ref[0:COLS, :] = w
    ref[COLS : 2 * COLS, :] = w


def fill_rows(ref, taps):
    block = CHUNK * ROWS
    r = iota((block, block), 0)
    c = iota((block, block), 1)
    m = jnp.where((r // ROWS) == (c // ROWS), band(c - r, taps), 0.0).astype(BF16)
    ref[:, 0:block] = m
    ref[:, block : 2 * block] = m


def dot(a, b):
    return jnp.dot(a, b, preferred_element_type=F32)


VALUE_TAPS = ((0, 7.0), (1, 7.0), (-1, -1.0), (2, -1.0))
SENSE_TAPS = ((0, -1.0), (1, 1.0))
BACK_TAPS = ((0, 7.0), (-1, 7.0), (1, -1.0), (-2, -1.0))


def rows_of(ref, start, r):
    line = iota((CHUNK, COLS), 0)
    block = ref.at[pl.ds(start, CHUNK * ROWS), :]
    got = jnp.zeros((CHUNK, COLS), F32)
    for kk in range(CHUNK):
        at = kk * ROWS + r
        got = jnp.where(line == kk, block[at : at + 1, :], got)
    return got


def gather_kernel(c1_in, c2_in, b1_in, b2_in, u_in, v_in, lev_in, q_in, x0_in, ss_in,
                  far, near, c1, c2, b1, b2, u, v, lev, q, x0, ss, sems, small_sems):
    small = ((q_in, q), (lev_in, lev), (x0_in, x0), (ss_in, ss))
    small = [pltpu.make_async_copy(a, b, small_sems.at[n]) for n, (a, b) in enumerate(small)]
    moves = ((c1_in, c1), (c2_in, c2), (b1_in, b1), (b2_in, b2), (u_in, u), (v_in, v))

    def copy(n, g):
        at = pl.ds(g * CHUNK * ROWS, CHUNK * ROWS)
        return pltpu.make_async_copy(moves[n][0].at[at, :], moves[n][1].at[at, :], sems.at[n, g])

    for c in small:
        c.start()
    for g in range(STEPS):
        for n in range(6):
            copy(n, g).start()
    for c in small:
        c.wait()
    odd = odd_place("ty")
    cos, sin = frame(q)
    cos = cos[:CHUNK, :]
    sin = sin[:CHUNK, :]

    def step(g, carry):
        for n in range(6):
            copy(n, g).wait()
        start = pl.multiple_of(g * (CHUNK * ROWS), CHUNK * ROWS)
        for a in range(5):
            for r in range(2):
                if a < 4:
                    high, low = [rows_of(moves[a][1], start, n + r) for n in (ROWS - 2, 0)]
                else:
                    high, low = [sin * rows_of(u, start, n + r) + cos * rows_of(v, start, n + r) for n in (ROWS - 2, 0)]
                at = pl.ds(pl.multiple_of((2 * a + r) * LEVELS + g * CHUNK, CHUNK), CHUNK)
                far[at, :] = jnp.where(odd == 1, high, low)
                near[at, :] = jnp.where(odd == 1, low, high)
        return carry

    lax.fori_loop(0, STEPS, step, 0)
    for out, first in ((far, 8 * odd), (near, 8 - 8 * odd)):
        at = pl.ds(pl.multiple_of(first, 8), 8)
        out[RAW_AT[D] : RAW_AT[D] + 8, :] = lev[at, :].astype(F32)
        out[RAW_AT[X0] : RAW_AT[X0] + 8, :] = x0[at, :]
        out[RAW_AT[SS] : RAW_AT[SS] + 8, :] = ss[at, :]


def local_kernel(t1, t2, b1, b2, u, v, es_in, ns_in, lev_ref, q_ref, x0_ref, ss_ref,
                 far, near, f2d, edges, et, nt, fe1, fe2, fn1, fn2, es, ns, wc, wb, kc, kb, ce, cn, be, bn, sems):
    moves = ((es_in, es), (ns_in, ns))

    def copy(n, g):
        at = pl.ds(g * CHUNK * ROWS, CHUNK * ROWS)
        return pltpu.make_async_copy(moves[n][0].at[at, :], moves[n][1].at[at, :], sems.at[n, g])

    for g in range(STEPS):
        for n in range(2):
            copy(n, g).start()
    fill_lanes(wc, VALUE_TAPS)
    fill_lanes(wb, SENSE_TAPS)
    odd = odd_place("ty")
    fill_rows(kc, VALUE_TAPS)
    fill_rows(kb, SENSE_TAPS)
    cos, sin = frame(q_ref)
    lev = lev_ref[...]
    east_lev, north_lev = face_levels(lev)
    lane128 = iota((ROWS, 128), 1)
    f2d[...] = jnp.zeros_like(f2d)
    edges[...] = jnp.zeros_like(edges)

    def field(f):
        return slice(f * ROWS, (f + 1) * ROWS)

    def step(g, carry):
        acc_u = jnp.zeros((ROWS, COLS), F32)
        acc_v = jnp.zeros((ROWS, COLS), F32)
        acc_e = jnp.zeros((ROWS, COLS), F32)
        acc_n = jnp.zeros((ROWS, COLS), F32)
        packs = [jnp.zeros((ROWS, 128), F32) for _ in range(5)]
        block = CHUNK * ROWS
        rows_at = pl.multiple_of(g * block, block)
        at = pl.ds(rows_at, block)
        for one, two, w, k_rows, east, north in ((t1, t2, wc, kc, ce, cn), (b1, b2, wb, kb, be, bn)):
            hi1, lo1 = split(one[at, :])
            hi2, lo2 = split(two[at, :])
            hi = jnp.concatenate([hi1, hi2], axis=0)
            lo = jnp.concatenate([lo1, lo2], axis=0)
            east[...] = dot(jnp.concatenate([hi, lo], axis=1), w[...])
            hi = jnp.concatenate([hi1, hi2], axis=1)
            lo = jnp.concatenate([lo1, lo2], axis=1)
            both = dot(k_rows[...], jnp.concatenate([hi, lo], axis=0))
            north[0:block, :] = both[:, 0:COLS]
            north[block : 2 * block, :] = both[:, COLS : 2 * COLS]
        for n in range(2):
            copy(n, g).wait()
        for kk in range(CHUNK):
            k = g * CHUNK + kk
            here = pl.ds(rows_at + kk * ROWS, ROWS)
            m = lev > k
            me = east_lev > k
            mn = north_lev > k
            ve = None
            vn = None
            for t, (fe_ref, fn_ref) in enumerate(((fe1, fn1), (fe2, fn2))):
                at = slice(t * block + kk * ROWS, t * block + (kk + 1) * ROWS)
                fe = jnp.where(me, be[at, :], 0.0)
                fn = jnp.where(mn, bn[at, :], 0.0)
                fe_ref[here, :] = fe
                fn_ref[here, :] = fn
                ve_t = fe * ce[at, :]
                vn_t = fn * cn[at, :]
                ve = ve_t if ve is None else ve + ve_t
                vn = vn_t if vn is None else vn + vn_t
            ve = K1 * ve
            vn = K1 * vn
            es_k = es[here, :]
            ns_k = ns[here, :]
            u_k = u[here, :]
            v_k = v[here, :]
            et_k = cos * es_k - sin * ns_k + (ve + roll(ve, 1, 1))
            nt_k = sin * es_k + cos * ns_k + (vn + roll(vn, 1, 0))
            et[here, :] = et_k
            nt[here, :] = nt_k
            acc_e = acc_e + jnp.where(m, et_k, 0.0)
            acc_n = acc_n + jnp.where(m, nt_k, 0.0)
            acc_u = acc_u + jnp.where(m, u_k, 0.0)
            acc_v = acc_v + jnp.where(m, v_k, 0.0)

            def ends(x):
                return jnp.where(lane128 < 2, x[:, :128], x[:, 128:])

            spot = (lane128 // 4) == kk
            packed = [ends(r[here, :]) for r in (t1, t2, b1, b2)]
            packed.append(cos[:, :128] * ends(u_k) - sin[:, :128] * ends(v_k))
            for n in range(5):
                packs[n] = jnp.where(spot, roll(packed[n], 4 * kk + 2, 1), packs[n])

        for n in range(5):
            at = slice(n * ROWS, (n + 1) * ROWS)
            edges[at, :] = edges[at, :] + pltpu.roll(packs[n], g * (4 * CHUNK), 1)
        f2d[field(TE), :] = f2d[field(TE), :] + (cos * acc_u - sin * acc_v)
        f2d[field(TN), :] = f2d[field(TN), :] + (sin * acc_u + cos * acc_v)
        f2d[field(CE), :] = f2d[field(CE), :] + acc_e
        f2d[field(CN), :] = f2d[field(CN), :] + acc_n
        return carry

    lax.fori_loop(0, STEPS, step, 0)
    f2d[field(D), :] = lev.astype(F32)
    f2d[field(X0), :] = x0_ref[...]
    f2d[field(SS), :] = ss_ref[...]
    for out, first in ((far, 8 * odd), (near, 8 - 8 * odd)):
        for f, spot in MADE_AT.items():
            out[spot : spot + 8, :] = f2d[pl.ds(pl.multiple_of(f * ROWS + first, 8), 8), :]
        for n in range(4):
            at = YE + 8 * (n // 2)
            side = 128 * (n % 2)
            out[at : at + 8, side : side + 128] = edges[pl.ds(pl.multiple_of(n * ROWS + first, 8), 8), :]


def row_boundary(low, high, lev_a2, lev_a1, lev_b1, lev_b2):
    level = iota((LEVELS, COLS), 0).astype(F32)
    mask_a = level < jnp.minimum(lev_a2, lev_a1)
    mask_0 = level < jnp.minimum(lev_a1, lev_b1)
    mask_b = level < jnp.minimum(lev_b1, lev_b2)

    def part(ref, a, r):
        return ref[(2 * a + r) * LEVELS : (2 * a + r + 1) * LEVELS, :]

    va = v0 = vb = None
    diffs = []
    for t in range(2):
        ca2, ca1 = part(low, t, 0), part(low, t, 1)
        cb1, cb2 = part(high, t, 0), part(high, t, 1)
        ga2, ga1 = part(low, 2 + t, 0), part(low, 2 + t, 1)
        gb1, gb2 = part(high, 2 + t, 0), part(high, 2 + t, 1)
        fa = jnp.where(mask_a, ga1 - ga2, 0.0)
        f0 = jnp.where(mask_0, gb1 - ga1, 0.0)
        fb = jnp.where(mask_b, gb2 - gb1, 0.0)
        diffs.append((fa, f0, fb))
        fa = fa * (-K1 * cb1)
        f0 = f0 * (K7 * (ca1 + cb1) - K1 * (ca2 + cb2))
        fb = fb * (-K1 * ca1)
        va = fa if va is None else va + fa
        v0 = f0 if v0 is None else v0 + f0
        vb = fb if vb is None else vb + fb
    vel = [part(low, 4, 0), part(low, 4, 1), part(high, 4, 0), part(high, 4, 1)]
    return va, va + v0, v0 + vb, vb, diffs, vel


def packed(x):
    half = iota((8, 128), 0) < 4
    return jnp.concatenate([x[0:ROWS, :], jnp.where(half, x[16:24, :], x[24:32, :])], axis=0)


def unpacked(x):
    a, b = x[32:56, :], x[56:80, :]
    return jnp.concatenate([x[0:32, :], a, a[16:24, :], b, b[16:24, :], x[80:96, :]], axis=0)


def rows_kernel(far_in, near_in, far_out, near_out, made_far, made_near, *rest):
    odd = odd_place("ty")

    @pl.when(odd == 1)
    def _():
        rows_body(near_in, far_in, far_out, near_out, made_near, made_far, *rest)

    @pl.when(odd == 0)
    def _():
        rows_body(far_in, near_in, near_out, far_out, made_far, made_near, *rest)


def rows_body(ylo, yhi, yup, ydn, mlo, mhi, f2d, edges, xfar, xnear, ext, edges_ext, nt_fix, row_seam):
    d0 = f2d[0:1, :]
    d1 = f2d[1:2, :]
    d14 = f2d[ROWS - 2 : ROWS - 1, :]
    d15 = f2d[ROWS - 1 : ROWS, :]
    dlo = ylo[RAW_AT[D] : RAW_AT[D] + 8, :]
    dhi = yhi[RAW_AT[D] : RAW_AT[D] + 8, :]
    lo = row_boundary(ylo, ydn, dlo[6:7, :], dlo[7:8, :], d0, d1)
    hi = row_boundary(yup, yhi, d14, d15, dhi[0:1, :], dhi[1:2, :])
    for side, (out, at) in enumerate(((lo, 0), (hi, 1))):
        diffs, vel = out[4], out[5]
        for i in range(2):
            spot = (6 * side + i) * LEVELS
            row_seam[spot : spot + LEVELS, :] = vel[at + i] + vel[at + i + 1]
            for t in range(2):
                spot = (6 * side + 2 + 2 * t + i) * LEVELS
                row_seam[spot : spot + LEVELS, :] = diffs[t][at + i]
    for n, value in enumerate((lo[2], lo[3], hi[0], hi[1])):
        nt_fix[n * LEVELS : (n + 1) * LEVELS, :] = value
    for f in range(FIELDS):
        ext[f * TALL : f * TALL + ROWS, :] = f2d[f * ROWS : (f + 1) * ROWS, :]
        above, below, spot = (yhi, ylo, RAW_AT[f]) if f in RAW_AT else (mhi, mlo, MADE_AT[f])
        ext[f * TALL + 16 : f * TALL + 24, :] = above[spot : spot + 8, :]
        ext[f * TALL + 24 : f * TALL + 32, :] = below[spot : spot + 8, :]
    spots = ((30, lo[0]), (31, lo[1]), (0, lo[2]), (1, lo[3]),
             (14, hi[0]), (15, hi[1]), (16, hi[2]), (17, hi[3]))
    for r, value in spots:
        at = slice(CN * TALL + r, CN * TALL + r + 1)
        ext[at, :] = ext[at, :] + jnp.sum(value, axis=0, keepdims=True)
    for n in range(4):
        at = YE + 8 * (n // 2)
        side = 128 * (n % 2)
        edges_ext[n * TALL : n * TALL + ROWS, :] = edges[n * ROWS : (n + 1) * ROWS, :]
        edges_ext[n * TALL + 16 : n * TALL + 24, :] = mhi[at : at + 8, side : side + 128]
        edges_ext[n * TALL + 24 : n * TALL + 32, :] = mlo[at : at + 8, side : side + 128]
    lane = iota((TALL, 128), 1)
    pr = jnp.zeros((TALL, 128), F32)
    pl_ = jnp.zeros((TALL, 128), F32)
    for f in range(FIELDS):
        spot = (lane // 8) == f
        z = ext[f * TALL : (f + 1) * TALL, :]
        pr = jnp.where(spot, roll(z[:, 128:], 8 * f + 8, 1), pr)
        pl_ = jnp.where(spot, roll(z[:, :128], 8 * f, 1), pl_)
    oddx = odd_place("tx") == 1

    def send(at, right, left):
        xfar[at, :] = jnp.where(oddx, right, left)
        xnear[at, :] = jnp.where(oddx, left, right)

    send(slice(0, TALL), pr, pl_)
    first = (lane % 4) < 2
    for pair in range(2):
        p = edges_ext[2 * pair * TALL : (2 * pair + 1) * TALL, :]
        s = edges_ext[(2 * pair + 1) * TALL : (2 * pair + 2) * TALL, :]
        at = slice(TALL + 24 * pair, TALL + 24 * pair + 24)
        send(at, packed(jnp.where(first, p, roll(s, 2, 1))), packed(jnp.where(first, roll(s, -2, 1), p)))
    own = edges[4 * ROWS : 5 * ROWS, :]
    send(slice(80, 96), own, own)


def spread(x):
    lane = iota(x.shape, 1)
    x = jnp.where(lane < 4, x, 0.0)
    for s in (4, 8, 16, 32, 64):
        x = x + roll(x, s, 1)
    return x


def seam(left_tile, right_tile):
    lane = iota(left_tile.shape, 1)
    return roll(jnp.where(lane >= 126, left_tile, right_tile), 2, 1)


def joined(lo_ref, hi_ref, edges_ext, pair, which, rows):
    own = edges_ext[(2 * pair + which) * TALL : (2 * pair + which) * TALL + rows, :]
    first = (iota((rows, 128), 1) % 4) < 2
    at = slice((1 + pair) * TALL, (1 + pair) * TALL + rows)
    lo = lo_ref[at, :]
    hi = hi_ref[at, :]
    if which == 1:
        lo = roll(lo, -2, 1)
        hi = roll(hi, 2, 1)
    return jnp.where(first, lo, own), jnp.where(first, own, hi)


def columns_kernel(far_in, near_in, ext, edges_ext, edges, seams, he, hn, basis, et_fix, lane_seam, moments):
    oddx = odd_place("tx") == 1
    xlo = unpacked(jnp.where(oddx, near_in[...], far_in[...]))
    xhi = unpacked(jnp.where(oddx, far_in[...], near_in[...]))
    lane = iota((TALL, 128), 1)
    group = lane % 4
    level = (lane // 4).astype(F32)
    tiles = []
    for f in range(FIELDS):
        z = ext[f * TALL : (f + 1) * TALL, :]
        right = roll(xhi[0:TALL, :], -8 * f, 1)
        left = roll(xlo[0:TALL, :], 120 - 8 * f, 1)
        third = jnp.where(lane < 8, right, jnp.where(lane >= 120, left, 0.0))
        tiles.append([z[:, :128], z[:, 128:], third])
    coef7 = jnp.where(group == 1, K7, 0.0)
    coefm = jnp.where((group == 1) | (group == 2), -K1, 0.0)
    coefp = jnp.where(group < 2, -K1, 0.0)
    cells = []
    for side in range(2):
        d = tiles[D]
        near = jnp.where(lane >= 126, d[2], d[0]) if side == 0 else jnp.where(lane >= 126, d[1], d[2])
        lev = dot(near.astype(BF16), seams[0:128, :])
        wet = (level < jnp.minimum(lev, roll(lev, -1, 1))) & (group < 3)
        w = None
        for t in range(2):
            c = joined(xlo, xhi, edges_ext, 0, t, TALL)[side]
            b = joined(xlo, xhi, edges_ext, 1, t, TALL)[side]
            f = jnp.where(wet, roll(b, -1, 1) - b, 0.0)
            spot = (3 * side + 1 + t) * ROWS
            lane_seam[spot : spot + ROWS, :] = f[0:ROWS, :]
            term = f * (coef7 * (c + roll(c, -1, 1)) + coefm * roll(c, 1, 1) + coefp * roll(c, -2, 1))
            w = term if w is None else w + term
        cell = w + roll(w, 1, 1)
        cells.append(cell)
        hi, lo = split(cell)
        total = dot(jnp.concatenate([hi, lo], axis=0), seams[128:256, :])
        total = total[0:TALL, :] + total[TALL : 2 * TALL, :]
        a, b = (2, 0) if side == 0 else (1, 2)
        tiles[CE][a] = tiles[CE][a] + jnp.where(lane >= 126, total, 0.0)
        tiles[CE][b] = tiles[CE][b] + jnp.where(lane < 2, total, 0.0)
    et_fix[...] = jnp.where(group < 2, cells[1], cells[0])[0:ROWS, :]
    own_u = edges[4 * ROWS : 5 * ROWS, :]
    half = group[0:ROWS, :] < 2
    for side, uu in enumerate((jnp.where(half, xlo[96:112, :], own_u), jnp.where(half, own_u, xhi[96:112, :]))):
        lane_seam[3 * side * ROWS : (3 * side + 1) * ROWS, :] = uu + roll(uu, -1, 1)

    full = [jnp.concatenate(t, axis=1) for t in tiles]
    d = full[D]
    near_e = jnp.minimum(d, roll(d, -1, 1))
    near_n = jnp.minimum(d, roll(d, -1, 0))
    we = STIFF * near_e
    wn = STIFF * near_n
    half_e = jnp.where(near_e > 0.0, 0.5, 0.0)
    half_n = jnp.where(near_n > 0.0, 0.5, 0.0)
    x0 = full[X0]
    flux_e = half_e * (full[TE] + roll(full[TE], -1, 1)) + we * (x0 - roll(x0, -1, 1))
    flux_n = half_n * (full[TN] + roll(full[TN], -1, 0)) + wn * (x0 - roll(x0, -1, 0))
    r = (roll(flux_e, 1, 1) - flux_e) + (roll(flux_n, 1, 0) - flux_n)
    b = full[SS] + (0.5 * GRAVITY) * (
        (roll(full[CE], -1, 1) - roll(full[CE], 1, 1)) + (roll(full[CN], -1, 0) - roll(full[CN], 1, 0))
    )

    def own_sum(x):
        part = x[0:ROWS, 0:128] + x[0:ROWS, 128:256]
        return jnp.sum(part, axis=0, keepdims=True)

    sums = []
    for n, start in enumerate((r, b)):
        vec = start
        for power in range(3):
            basis[(4 * n + power) * TALL : (4 * n + power + 1) * TALL, :] = vec
            sums.append(own_sum(vec * vec))
            de = vec - roll(vec, -1, 1)
            dn = vec - roll(vec, -1, 0)
            he = we * de
            hn = wn * dn
            sums.append(own_sum(he * de + hn * dn))
            if power < 2:
                vec = (he - roll(he, 1, 1)) + (hn - roll(hn, 1, 0))
    basis[3 * TALL : 4 * TALL, :] = x0
    basis[7 * TALL : 8 * TALL, :] = half_e
    basis[8 * TALL : 9 * TALL, :] = half_n
    spot_lane = iota((1, 128), 1)
    line = jnp.zeros((1, 128), F32)
    for n, s in enumerate(sums):
        line = line + jnp.where(spot_lane == n, jnp.sum(s, axis=1, keepdims=True), 0.0)
    moments[...] = jnp.broadcast_to(line, (128, 128))


def safe_ratio(top, bottom, limit):
    ok = bottom > 0.0
    return jnp.clip(jnp.where(ok, top / jnp.where(ok, bottom, 1.0), 0.0), 0.0, limit)


def solve_small(m):
    bound = 8.0 * STIFF * LEVELS
    a0 = m[1] / m[0]
    n1 = m[2] - a0 * m[1]
    b1 = safe_ratio(n1, m[0], bound * bound)
    a1 = safe_ratio(m[3] - a0 * (2.0 * m[2] - a0 * m[1]), n1, bound)
    s = a0 + a1
    t = a0 * a1 - b1
    n2 = m[4] - s * m[3] + t * m[2]
    b2 = safe_ratio(n2, n1, bound * bound)
    top = m[5] - 2.0 * s * m[4] + (s * s + 2.0 * t) * m[3] - 2.0 * s * t * m[2] + t * t * m[1]
    a2 = safe_ratio(top, n2, bound)
    e2 = 1.0 + a2
    e1 = jnp.maximum(1.0 + a1 - b2 / e2, 1.0)
    e0 = jnp.maximum(1.0 + a0 - b1 / e1, 1.0)
    y0 = 1.0 / e0
    y1 = -y0 / e1
    y2 = -y1 / e2
    return y0 - a0 * y1 + t * y2, y1 - s * y2, y2


def vec(ref, n):
    return ref[n * TALL : (n + 1) * TALL, :]


def prepare_kernel(u, v, q_ref, he, hn, wd, kd, seams):
    r = iota((128, 128), 0)
    c = iota((128, 128), 1)
    near = jnp.where(lax.rem(c, 4) < 2, lax.rem(c, 4) + 126, lax.rem(c, 4) - 2)
    seams[0:128, :] = jnp.where(r == near, 1.0, 0.0).astype(BF16)
    seams[128:256, :] = jnp.where(lax.rem(r, 4) == lax.rem(c + 2, 4), 1.0, 0.0).astype(BF16)
    cos, sin = frame(q_ref)
    cos = K1 * cos
    sin = K1 * sin
    fill_lanes(wd, BACK_TAPS)
    fill_rows(kd, BACK_TAPS)

    def step(g, carry):
        for kk in range(4):
            here = pl.ds(pl.multiple_of(g * (4 * ROWS), 4 * ROWS) + kk * ROWS, ROWS)
            east = cos * u[here, :] - sin * v[here, :]
            north = sin * u[here, :] + cos * v[here, :]
            he[here, :] = east + roll(east, -1, 1)
            hn[here, :] = north + roll(north, -1, 0)
        return carry

    lax.fori_loop(0, LEVELS // 4, step, 0)


def final_kernel(mom, basis, row_seam, nt_fix, lane_seam, et_fix, lev_ref, q_ref, b1, b2, he_ref, hn_ref,
                 fe1, fe2, fn1, fn2, wd, kd, et, nt, th_out, sa_out, ea_out, na_out, xb,
                 row_fix, lane_fix, th, sa, ea, na, out_sems):
    outs = ((th, th_out), (sa, sa_out), (ea, ea_out), (na, na_out))

    def put(n, g):
        at = pl.ds(g * CHUNK * ROWS, CHUNK * ROWS)
        return pltpu.make_async_copy(outs[n][0].at[at, :], outs[n][1].at[at, :], out_sems.at[n, g])

    cos, sin = frame(q_ref)
    lev = lev_ref[...]
    lane = iota((ROWS, COLS), 1)
    line = jnp.sum(mom[...], axis=0, keepdims=True)
    spot = iota((1, 128), 1)
    m = [jnp.sum(jnp.where(spot == n, line, 0.0), axis=1, keepdims=True) for n in range(12)]
    cf = solve_small(m[0:6])
    cb = solve_small(m[6:12])
    end = vec(basis, 3) + (cf[0] * vec(basis, 0) + cf[1] * vec(basis, 1) + cf[2] * vec(basis, 2))
    adj = cb[0] * vec(basis, 4) + cb[1] * vec(basis, 5) + cb[2] * vec(basis, 6)
    xb[...] = adj[0:ROWS, 0:COLS]
    side_e, side_n = end[0:ROWS, :], end[:, 0:COLS]
    ge = (0.5 * GRAVITY) * (roll(side_e, -1, 1) - roll(side_e, 1, 1))
    gn = (0.5 * GRAVITY) * (roll(side_n, -1, 0) - roll(side_n, 1, 0))
    wide_e = ge + roll(ge, -1, 1)
    wide_n = gn + roll(gn, -1, 0)
    sum_e = K1 * wide_e[:, 0:COLS]
    sum_n = K1 * wide_n[0:ROWS, :]
    side_e, side_n = adj[0:ROWS, :], adj[:, 0:COLS]
    fe = vec(basis, 7)[0:ROWS, :] * (roll(side_e, -1, 1) - side_e)
    fn = vec(basis, 8)[:, 0:COLS] * (roll(side_n, -1, 0) - side_n)
    be = (fe + roll(fe, 1, 1))[:, 0:COLS]
    bn = (fn + roll(fn, 1, 0))[0:ROWS, :]

    for side, first in enumerate((-2, 15)):
        vel = []
        for i in range(2):
            r = (first + i) % TALL
            vel.append(row_seam[(6 * side + i) * LEVELS : (6 * side + i + 1) * LEVELS, :] - wide_n[r : r + 1, :])
        for t in range(2):
            spots = [(6 * side + 2 + 2 * t + i) * LEVELS for i in range(2)]
            qa, qb = [row_seam[s : s + LEVELS, :] * w for s, w in zip(spots, vel)]
            values = (K7 * qb - K1 * qa, -K1 * qb) if side == 0 else (-K1 * qa, K7 * qa - K1 * qb)
            for i in range(2):
                at = (4 * t + 2 * side + i) * LEVELS
                row_fix[at : at + LEVELS, :] = values[i]
    group = iota((ROWS, 128), 1) % 4
    tiles = [wide_e[:, 128 * n : 128 * n + 128] for n in range(3)]
    for side in range(2):
        gg = spread(seam(tiles[2], tiles[0]) if side == 0 else seam(tiles[1], tiles[2]))
        vel = lane_seam[3 * side * ROWS : (3 * side + 1) * ROWS, :] - gg
        keep = (group < 2) if side == 0 else ((group == 1) | (group == 2))
        for t in range(2):
            spot = (3 * side + 1 + t) * ROWS
            f = jnp.where(keep, lane_seam[spot : spot + ROWS, :] * vel, 0.0)
            at = slice(t * ROWS, (t + 1) * ROWS)
            if side == 0:
                fix = jnp.where(group == 2, K7 * roll(f, 1, 1), 0.0) - K1 * roll(f, 2, 1)
                lane_fix[at, :] = jnp.where(group >= 2, fix, 0.0)
            else:
                fix = jnp.where(group == 1, K7 * f, 0.0) - K1 * roll(f, -1, 1)
                lane_fix[at, :] = jnp.where(group < 2, fix, lane_fix[at, :])

    edge = (lane < 2) | (lane >= COLS - 2)
    line8 = iota((8, COLS), 0)

    def step(g, carry):
        turn = 128 - g * (4 * CHUNK)
        packs = [lane_fix[0:ROWS, :], lane_fix[ROWS : 2 * ROWS, :], et_fix[...]]
        packs = [pltpu.roll(p, turn, 1) for p in packs]

        def fix_rows(ref, n):
            return ref.at[pl.ds(pl.multiple_of(n * LEVELS + g * CHUNK, CHUNK), CHUNK), :]

        fixes = [[fix_rows(row_fix, n) for n in range(4)], [fix_rows(row_fix, 4 + n) for n in range(4)],
                 [fix_rows(nt_fix, n) for n in range(4)]]
        block = CHUNK * ROWS
        rows_at = pl.multiple_of(g * block, block)
        east = [[], []]
        north = [[], []]
        for kk in range(CHUNK):
            here = pl.ds(rows_at + kk * ROWS, ROWS)
            he = he_ref[here, :] - sum_e
            hn = hn_ref[here, :] - sum_n
            for t, (fe_ref, fn_ref) in enumerate(((fe1, fn1), (fe2, fn2))):
                east[t].append(fe_ref[here, :] * he)
                north[t].append(fn_ref[here, :] * hn)
        flow = split(jnp.concatenate(east[0] + east[1], axis=0))
        de = dot(jnp.concatenate(flow, axis=1), wd[...])
        flow = [split(jnp.concatenate(x, axis=0)) for x in north]
        hi = jnp.concatenate([flow[0][0], flow[1][0]], axis=1)
        lo = jnp.concatenate([flow[0][1], flow[1][1]], axis=1)
        dn = dot(kd[...], jnp.concatenate([hi, lo], axis=0))
        at = pl.ds(rows_at, block)
        th[at, :] = b1[at, :] + (de[0:block, :] + dn[:, 0:COLS])
        sa[at, :] = b2[at, :] + (de[block : 2 * block, :] + dn[:, COLS : 2 * COLS])
        for which, kk in [((0, 1), kk) for kk in range(CHUNK)] + [((2, 3), kk) for kk in range(CHUNK)]:
            k = g * CHUNK + kk
            here = pl.ds(rows_at + kk * ROWS, ROWS)
            m = lev > k
            if kk == 0 and 2 in which:
                for n in range(2):
                    put(n, g).start()

            def lane_fixed(x, n):
                z = roll(packs[n], -(4 * kk + 2), 1)
                return jnp.where(edge, x + jnp.concatenate([z, z], axis=1), x)

            def row_fixed(x, n):
                r0, r1, r14, r15 = [f[kk : kk + 1, :] for f in fixes[n]]
                top = jnp.where(line8 == 0, r0, jnp.where(line8 == 1, r1, 0.0))
                low = jnp.where(line8 == 6, r14, jnp.where(line8 == 7, r15, 0.0))
                return x + jnp.concatenate([top, low], axis=0)

            for n in which:
                if n < 2:
                    out = (th, sa)[n]
                    out[here, :] = row_fixed(lane_fixed(out[here, :], n), n)
            if 2 not in which:
                continue
            eg = jnp.where(m, lane_fixed(et[here, :], 2) + be, 0.0)
            ng = jnp.where(m, row_fixed(nt[here, :], 2) + bn, 0.0)
            ea[here, :] = cos * eg + sin * ng
            na[here, :] = cos * ng - sin * eg
        for n in range(2, 4):
            put(n, g).start()
        return carry

    lax.fori_loop(0, STEPS, step, 0)
    for g in range(STEPS):
        for n in range(4):
            put(n, g).wait()


def params(mib):
    return pltpu.CompilerParams(vmem_limit_bytes=mib * 1024 * 1024)


def far(x):
    return pltpu.with_memory_space_constraint(x, pltpu.HBM)


def sds(*shape):
    return jax.ShapeDtypeStruct(shape, F32)


def swaps(count):
    far, near = [], []
    for i in range(count - 1):
        (far if i % 2 else near).extend([(i, i + 1), (i + 1, i)])
    return far, near


def on_device(theta_start, salt_start, east_velocity, north_velocity, surface_start, wet_levels,
              face_frame, theta_sense, salt_sense, east_sense, north_sense, surface_sense):
    flat = lambda x: x.reshape(LEVELS * ROWS, COLS)
    c1, c2, u, v = map(flat, (theta_start, salt_start, east_velocity, north_velocity))
    b1, b2, es, ns = map(flat, (theta_sense, salt_sense, east_sense, north_sense))
    vol = sds(LEVELS * ROWS, COLS)
    c1, c2, b1, b2, u, v, es, ns = [far(x) for x in (c1, c2, b1, b2, u, v, es, ns)]
    hbm = pl.BlockSpec(memory_space=pltpu.HBM)
    vmem = pl.BlockSpec(memory_space=pltpu.VMEM)
    cubes = pltpu.VMEM((LEVELS * ROWS, COLS), F32)
    sems = lambda n: pltpu.SemaphoreType.DMA((n, STEPS))
    ints = jax.ShapeDtypeStruct((ROWS, COLS), jnp.int32)
    small = [far(x) for x in (wet_levels, face_frame, surface_start, surface_sense)]
    raw_far, raw_near, c1, c2, b1, b2, u, v, lev, turns, x0, ss = pl.pallas_call(
        gather_kernel,
        in_specs=[hbm] * 10,
        out_specs=[vmem] * 12,
        out_shape=[sds(RAW_ROWS, COLS)] * 2 + [vol] * 6 + [ints] * 2 + [sds(ROWS, COLS)] * 2,
        scratch_shapes=[sems(6), pltpu.SemaphoreType.DMA((4,))],
        compiler_params=params(4),
        cost_estimate=pl.CostEstimate(flops=4000000, bytes_accessed=6000000, transcendentals=0),
        name="gather",
    )(c1, c2, b1, b2, u, v, *small)
    y_far, y_near = swaps(lax.axis_size("ty"))
    x_far, x_near = swaps(lax.axis_size("tx"))
    raw_far_in = lax.ppermute(raw_far, "ty", y_far)
    raw_near_in = lax.ppermute(raw_near, "ty", y_near)

    made_far, made_near, f2d, edges, et, nt, fe1, fe2, fn1, fn2 = pl.pallas_call(
        local_kernel,
        in_specs=[vmem] * 6 + [hbm] * 2 + [vmem] * 4,
        out_specs=[vmem] * 10,
        out_shape=[sds(MADE_ROWS, COLS)] * 2 + [sds(FIELDS * ROWS, COLS), sds(5 * ROWS, 128)] + [vol] * 6,
        scratch_shapes=[cubes] * 2 + [pltpu.VMEM((2 * COLS, COLS), BF16)] * 2
        + [pltpu.VMEM((CHUNK * ROWS, 2 * CHUNK * ROWS), BF16)] * 2
        + [pltpu.VMEM((2 * CHUNK * ROWS, COLS), F32)] * 4 + [sems(2)],
        compiler_params=params(8),
        cost_estimate=pl.CostEstimate(flops=20000000, bytes_accessed=8000000, transcendentals=0),
        name="local",
    )(c1, c2, b1, b2, u, v, es, ns, lev, turns, x0, ss)
    made_far_in = lax.ppermute(made_far, "ty", y_far)
    made_near_in = lax.ppermute(made_near, "ty", y_near)

    he, hn, wd, kd, seams = pl.pallas_call(
        prepare_kernel,
        in_specs=[vmem] * 3,
        out_specs=[vmem] * 5,
        out_shape=[vol] * 2 + [jax.ShapeDtypeStruct((2 * COLS, COLS), BF16),
                               jax.ShapeDtypeStruct((CHUNK * ROWS, 2 * CHUNK * ROWS), BF16),
                               jax.ShapeDtypeStruct((256, 128), BF16)],
        compiler_params=params(4),
        cost_estimate=pl.CostEstimate(flops=2000000, bytes_accessed=2000000, transcendentals=0),
        name="prepare",
    )(u, v, turns)

    xfar, xnear, ext, edges_ext, nt_fix, row_seam = pl.pallas_call(
        rows_kernel,
        out_shape=[sds(XROWS, 128), sds(XROWS, 128), sds(FIELDS * TALL, COLS),
                   sds(4 * TALL, 128), sds(4 * LEVELS, COLS), sds(12 * LEVELS, COLS)],
        compiler_params=params(4),
        name="rows",
    )(raw_far_in, raw_near_in, raw_far, raw_near, made_far_in, made_near_in, f2d, edges)
    xfar_in = lax.ppermute(xfar, "tx", x_far)
    xnear_in = lax.ppermute(xnear, "tx", x_near)

    basis, et_fix, lane_seam, moments = pl.pallas_call(
        columns_kernel,
        in_specs=[vmem] * 6 + [pl.BlockSpec(memory_space=pl.ANY)] * 2,
        out_shape=[sds(9 * TALL, WIDE), sds(ROWS, 128), sds(6 * ROWS, 128), sds(128, 128)],
        compiler_params=params(4),
        name="columns",
    )(xfar_in, xnear_in, ext, edges_ext, edges, seams, he, hn)
    moments = lax.all_to_all(moments, ALL, 0, 0, tiled=True)
    th, sa, ea, na, xb = pl.pallas_call(
        final_kernel,
        in_specs=[vmem] * 20,
        out_specs=[hbm] * 4 + [vmem],
        out_shape=[vol] * 4 + [sds(ROWS, COLS)],
        scratch_shapes=[pltpu.VMEM((8 * LEVELS, COLS), F32), pltpu.VMEM((2 * ROWS, 128), F32)]
        + [cubes] * 4 + [sems(4)],
        compiler_params=params(8),
        name="final",
    )(moments, basis, row_seam, nt_fix, lane_seam, et_fix, lev, turns, b1, b2, he, hn, fe1, fe2, fn1, fn2, wd, kd, et, nt)
    cube = lambda x: x.reshape(LEVELS, ROWS, COLS)
    return cube(th), cube(sa), cube(ea), cube(na), xb


def solution(mesh):
    cube = P(None, "ty", "tx")
    plane = P("ty", "tx")
    return jax.shard_map(
        on_device,
        mesh=mesh,
        in_specs=(cube, cube, cube, cube, plane, plane, plane, cube, cube, cube, cube, plane),
        out_specs=(cube, cube, cube, cube, plane),
        check_vma=False,
    )
```

```python
import functools

import jax
import jax.numpy as jnp
from jax import lax
from jax.experimental import pallas as pl
from jax.experimental.pallas import tpu as pltpu
from jax.sharding import PartitionSpec as P

F32 = jnp.float32
BF16 = jnp.bfloat16
LEVELS = 32
ROWS = 16
COLS = 256
WIDE = 384
TALL = 32
CHUNK = 8
STEPS = LEVELS // CHUNK
FIELDS = 7
D, X0, TE, TN, SS, CE, CN = range(FIELDS)
RAW_AT = {D: 320, X0: 328, SS: 336}
MADE_AT = {TE: 0, TN: 8, CE: 16, CN: 24}
YE = 32
RAW_ROWS = 344
MADE_ROWS = 48
XROWS = 96

RATE = 0.2
GRAVITY = 0.25
STIFF = 2.0 / LEVELS
K7 = 0.5 * RATE * 7.0 / 12.0
K1 = 0.5 * RATE / 12.0
ALL = ("ty", "tx")


def roll(x, shift, axis):
    return pltpu.roll(x, shift % x.shape[axis], axis)


def iota(shape, axis):
    return lax.broadcasted_iota(jnp.int32, shape, axis)


def frame(q_ref):
    q = q_ref[...]
    cos = jnp.where(q == 0, 1.0, jnp.where(q == 2, -1.0, 0.0))
    sin = jnp.where(q == 1, 1.0, jnp.where(q == 3, -1.0, 0.0))
    return cos, sin


def face_levels(lev):
    lane = iota((ROWS, COLS), 1)
    row = iota((ROWS, COLS), 0)
    east = jnp.where(lane < COLS - 1, jnp.minimum(lev, roll(lev, -1, 1)), 0)
    north = jnp.where(row < ROWS - 1, jnp.minimum(lev, roll(lev, -1, 0)), 0)
    return east, north


def split(x):
    hi = x.astype(BF16)
    return hi, (x - hi.astype(F32)).astype(BF16)


def odd_place(axis):
    return lax.rem(lax.axis_index(axis), 2)


def band(delta, taps):
    out = jnp.zeros(delta.shape, F32)
    for at, value in taps:
        out = jnp.where(delta == at, value, out)
    return out


def fill_lanes(ref, taps):
    w = band(iota((COLS, COLS), 0) - iota((COLS, COLS), 1), taps).astype(BF16)
    ref[0:COLS, :] = w
    ref[COLS : 2 * COLS, :] = w


def fill_rows(ref, taps):
    block = CHUNK * ROWS
    r = iota((block, block), 0)
    c = iota((block, block), 1)
    m = jnp.where((r // ROWS) == (c // ROWS), band(c - r, taps), 0.0).astype(BF16)
    ref[:, 0:block] = m
    ref[:, block : 2 * block] = m


def dot(a, b):
    return jnp.dot(a, b, preferred_element_type=F32)


VALUE_TAPS = ((0, 7.0), (1, 7.0), (-1, -1.0), (2, -1.0))
SENSE_TAPS = ((0, -1.0), (1, 1.0))
BACK_TAPS = ((0, 7.0), (-1, 7.0), (1, -1.0), (-2, -1.0))


def rows_of(ref, start, r):
    line = iota((CHUNK, COLS), 0)
    block = ref.at[pl.ds(start, CHUNK * ROWS), :]
    got = jnp.zeros((CHUNK, COLS), F32)
    for kk in range(CHUNK):
        at = kk * ROWS + r
        got = jnp.where(line == kk, block[at : at + 1, :], got)
    return got


def gather_kernel(c1_in, c2_in, b1_in, b2_in, u_in, v_in, lev_in, q_in, x0_in, ss_in,
                  far, near, c1, c2, b1, b2, u, v, lev, q, x0, ss, sems, small_sems):
    small = ((q_in, q), (lev_in, lev), (x0_in, x0), (ss_in, ss))
    small = [pltpu.make_async_copy(a, b, small_sems.at[n]) for n, (a, b) in enumerate(small)]
    moves = ((c1_in, c1), (c2_in, c2), (b1_in, b1), (b2_in, b2), (u_in, u), (v_in, v))

    def copy(n, g):
        at = pl.ds(g * CHUNK * ROWS, CHUNK * ROWS)
        return pltpu.make_async_copy(moves[n][0].at[at, :], moves[n][1].at[at, :], sems.at[n, g])

    for c in small:
        c.start()
    for g in range(STEPS):
        for n in range(6):
            copy(n, g).start()
    for c in small:
        c.wait()
    odd = odd_place("ty")
    cos, sin = frame(q)
    cos = cos[:CHUNK, :]
    sin = sin[:CHUNK, :]

    def step(g, carry):
        for n in range(6):
            copy(n, g).wait()
        start = pl.multiple_of(g * (CHUNK * ROWS), CHUNK * ROWS)
        for a in range(5):
            for r in range(2):
                if a < 4:
                    high, low = [rows_of(moves[a][1], start, n + r) for n in (ROWS - 2, 0)]
                else:
                    high, low = [sin * rows_of(u, start, n + r) + cos * rows_of(v, start, n + r) for n in (ROWS - 2, 0)]
                at = pl.ds(pl.multiple_of((2 * a + r) * LEVELS + g * CHUNK, CHUNK), CHUNK)
                far[at, :] = jnp.where(odd == 1, high, low)
                near[at, :] = jnp.where(odd == 1, low, high)
        return carry

    lax.fori_loop(0, STEPS, step, 0)
    for out, first in ((far, 8 * odd), (near, 8 - 8 * odd)):
        at = pl.ds(pl.multiple_of(first, 8), 8)
        out[RAW_AT[D] : RAW_AT[D] + 8, :] = lev[at, :].astype(F32)
        out[RAW_AT[X0] : RAW_AT[X0] + 8, :] = x0[at, :]
        out[RAW_AT[SS] : RAW_AT[SS] + 8, :] = ss[at, :]


def local_kernel(t1, t2, b1, b2, u, v, es_in, ns_in, lev_ref, q_ref, x0_ref, ss_ref,
                 far, near, f2d, edges, et, nt, fe1, fe2, fn1, fn2, es, ns, wc, wb, kc, kb, ce, cn, be, bn, sems):
    moves = ((es_in, es), (ns_in, ns))

    def copy(n, g):
        at = pl.ds(g * CHUNK * ROWS, CHUNK * ROWS)
        return pltpu.make_async_copy(moves[n][0].at[at, :], moves[n][1].at[at, :], sems.at[n, g])

    for g in range(STEPS):
        for n in range(2):
            copy(n, g).start()
    fill_lanes(wc, VALUE_TAPS)
    fill_lanes(wb, SENSE_TAPS)
    odd = odd_place("ty")
    fill_rows(kc, VALUE_TAPS)
    fill_rows(kb, SENSE_TAPS)
    cos, sin = frame(q_ref)
    lev = lev_ref[...]
    east_lev, north_lev = face_levels(lev)
    lane128 = iota((ROWS, 128), 1)
    f2d[...] = jnp.zeros_like(f2d)
    edges[...] = jnp.zeros_like(edges)

    def field(f):
        return slice(f * ROWS, (f + 1) * ROWS)

    def step(g, carry):
        acc_u = jnp.zeros((ROWS, COLS), F32)
        acc_v = jnp.zeros((ROWS, COLS), F32)
        acc_e = jnp.zeros((ROWS, COLS), F32)
        acc_n = jnp.zeros((ROWS, COLS), F32)
        packs = [jnp.zeros((ROWS, 128), F32) for _ in range(5)]
        block = CHUNK * ROWS
        rows_at = pl.multiple_of(g * block, block)
        at = pl.ds(rows_at, block)
        for one, two, w, k_rows, east, north in ((t1, t2, wc, kc, ce, cn), (b1, b2, wb, kb, be, bn)):
            hi1, lo1 = split(one[at, :])
            hi2, lo2 = split(two[at, :])
            hi = jnp.concatenate([hi1, hi2], axis=0)
            lo = jnp.concatenate([lo1, lo2], axis=0)
            east[...] = dot(jnp.concatenate([hi, lo], axis=1), w[...])
            hi = jnp.concatenate([hi1, hi2], axis=1)
            lo = jnp.concatenate([lo1, lo2], axis=1)
            both = dot(k_rows[...], jnp.concatenate([hi, lo], axis=0))
            north[0:block, :] = both[:, 0:COLS]
            north[block : 2 * block, :] = both[:, COLS : 2 * COLS]
        for n in range(2):
            copy(n, g).wait()
        for kk in range(CHUNK):
            k = g * CHUNK + kk
            here = pl.ds(rows_at + kk * ROWS, ROWS)
            m = lev > k
            me = east_lev > k
            mn = north_lev > k
            ve = None
            vn = None
            for t, (fe_ref, fn_ref) in enumerate(((fe1, fn1), (fe2, fn2))):
                at = slice(t * block + kk * ROWS, t * block + (kk + 1) * ROWS)
                fe = jnp.where(me, be[at, :], 0.0)
                fn = jnp.where(mn, bn[at, :], 0.0)
                fe_ref[here, :] = fe
                fn_ref[here, :] = fn
                ve_t = fe * ce[at, :]
                vn_t = fn * cn[at, :]
                ve = ve_t if ve is None else ve + ve_t
                vn = vn_t if vn is None else vn + vn_t
            ve = K1 * ve
            vn = K1 * vn
            es_k = es[here, :]
            ns_k = ns[here, :]
            u_k = u[here, :]
            v_k = v[here, :]
            et_k = cos * es_k - sin * ns_k + (ve + roll(ve, 1, 1))
            nt_k = sin * es_k + cos * ns_k + (vn + roll(vn, 1, 0))
            et[here, :] = et_k
            nt[here, :] = nt_k
            acc_e = acc_e + jnp.where(m, et_k, 0.0)
            acc_n = acc_n + jnp.where(m, nt_k, 0.0)
            acc_u = acc_u + jnp.where(m, u_k, 0.0)
            acc_v = acc_v + jnp.where(m, v_k, 0.0)

            def ends(x):
                return jnp.where(lane128 < 2, x[:, :128], x[:, 128:])

            spot = (lane128 // 4) == kk
            packed = [ends(r[here, :]) for r in (t1, t2, b1, b2)]
            packed.append(cos[:, :128] * ends(u_k) - sin[:, :128] * ends(v_k))
            for n in range(5):
                packs[n] = jnp.where(spot, roll(packed[n], 4 * kk + 2, 1), packs[n])

        for n in range(5):
            at = slice(n * ROWS, (n + 1) * ROWS)
            edges[at, :] = edges[at, :] + pltpu.roll(packs[n], g * (4 * CHUNK), 1)
        f2d[field(TE), :] = f2d[field(TE), :] + (cos * acc_u - sin * acc_v)
        f2d[field(TN), :] = f2d[field(TN), :] + (sin * acc_u + cos * acc_v)
        f2d[field(CE), :] = f2d[field(CE), :] + acc_e
        f2d[field(CN), :] = f2d[field(CN), :] + acc_n
        return carry

    lax.fori_loop(0, STEPS, step, 0)
    f2d[field(D), :] = lev.astype(F32)
    f2d[field(X0), :] = x0_ref[...]
    f2d[field(SS), :] = ss_ref[...]
    for out, first in ((far, 8 * odd), (near, 8 - 8 * odd)):
        for f, spot in MADE_AT.items():
            out[spot : spot + 8, :] = f2d[pl.ds(pl.multiple_of(f * ROWS + first, 8), 8), :]
        for n in range(4):
            at = YE + 8 * (n // 2)
            side = 128 * (n % 2)
            out[at : at + 8, side : side + 128] = edges[pl.ds(pl.multiple_of(n * ROWS + first, 8), 8), :]


def row_boundary(low, high, lev_a2, lev_a1, lev_b1, lev_b2):
    level = iota((LEVELS, COLS), 0).astype(F32)
    mask_a = level < jnp.minimum(lev_a2, lev_a1)
    mask_0 = level < jnp.minimum(lev_a1, lev_b1)
    mask_b = level < jnp.minimum(lev_b1, lev_b2)

    def part(ref, a, r):
        return ref[(2 * a + r) * LEVELS : (2 * a + r + 1) * LEVELS, :]

    va = v0 = vb = None
    diffs = []
    for t in range(2):
        ca2, ca1 = part(low, t, 0), part(low, t, 1)
        cb1, cb2 = part(high, t, 0), part(high, t, 1)
        ga2, ga1 = part(low, 2 + t, 0), part(low, 2 + t, 1)
        gb1, gb2 = part(high, 2 + t, 0), part(high, 2 + t, 1)
        fa = jnp.where(mask_a, ga1 - ga2, 0.0)
        f0 = jnp.where(mask_0, gb1 - ga1, 0.0)
        fb = jnp.where(mask_b, gb2 - gb1, 0.0)
        diffs.append((fa, f0, fb))
        fa = fa * (-K1 * cb1)
        f0 = f0 * (K7 * (ca1 + cb1) - K1 * (ca2 + cb2))
        fb = fb * (-K1 * ca1)
        va = fa if va is None else va + fa
        v0 = f0 if v0 is None else v0 + f0
        vb = fb if vb is None else vb + fb
    vel = [part(low, 4, 0), part(low, 4, 1), part(high, 4, 0), part(high, 4, 1)]
    return va, va + v0, v0 + vb, vb, diffs, vel


def packed(x):
    half = iota((8, 128), 0) < 4
    return jnp.concatenate([x[0:ROWS, :], jnp.where(half, x[16:24, :], x[24:32, :])], axis=0)


def unpacked(x):
    a, b = x[32:56, :], x[56:80, :]
    return jnp.concatenate([x[0:32, :], a, a[16:24, :], b, b[16:24, :], x[80:96, :]], axis=0)


def rows_kernel(far_in, near_in, far_out, near_out, made_far, made_near, *rest):
    odd = odd_place("ty")

    @pl.when(odd == 1)
    def _():
        rows_body(near_in, far_in, far_out, near_out, made_near, made_far, *rest)

    @pl.when(odd == 0)
    def _():
        rows_body(far_in, near_in, near_out, far_out, made_far, made_near, *rest)


def rows_body(ylo, yhi, yup, ydn, mlo, mhi, f2d, edges, xfar, xnear, ext, edges_ext, nt_fix, row_seam):
    d0 = f2d[0:1, :]
    d1 = f2d[1:2, :]
    d14 = f2d[ROWS - 2 : ROWS - 1, :]
    d15 = f2d[ROWS - 1 : ROWS, :]
    dlo = ylo[RAW_AT[D] : RAW_AT[D] + 8, :]
    dhi = yhi[RAW_AT[D] : RAW_AT[D] + 8, :]
    lo = row_boundary(ylo, ydn, dlo[6:7, :], dlo[7:8, :], d0, d1)
    hi = row_boundary(yup, yhi, d14, d15, dhi[0:1, :], dhi[1:2, :])
    for side, (out, at) in enumerate(((lo, 0), (hi, 1))):
        diffs, vel = out[4], out[5]
        for i in range(2):
            spot = (6 * side + i) * LEVELS
            row_seam[spot : spot + LEVELS, :] = vel[at + i] + vel[at + i + 1]
            for t in range(2):
                spot = (6 * side + 2 + 2 * t + i) * LEVELS
                row_seam[spot : spot + LEVELS, :] = diffs[t][at + i]
    for n, value in enumerate((lo[2], lo[3], hi[0], hi[1])):
        nt_fix[n * LEVELS : (n + 1) * LEVELS, :] = value
    for f in range(FIELDS):
        ext[f * TALL : f * TALL + ROWS, :] = f2d[f * ROWS : (f + 1) * ROWS, :]
        above, below, spot = (yhi, ylo, RAW_AT[f]) if f in RAW_AT else (mhi, mlo, MADE_AT[f])
        ext[f * TALL + 16 : f * TALL + 24, :] = above[spot : spot + 8, :]
        ext[f * TALL + 24 : f * TALL + 32, :] = below[spot : spot + 8, :]
    spots = ((30, lo[0]), (31, lo[1]), (0, lo[2]), (1, lo[3]),
             (14, hi[0]), (15, hi[1]), (16, hi[2]), (17, hi[3]))
    for r, value in spots:
        at = slice(CN * TALL + r, CN * TALL + r + 1)
        ext[at, :] = ext[at, :] + jnp.sum(value, axis=0, keepdims=True)
    for n in range(4):
        at = YE + 8 * (n // 2)
        side = 128 * (n % 2)
        edges_ext[n * TALL : n * TALL + ROWS, :] = edges[n * ROWS : (n + 1) * ROWS, :]
        edges_ext[n * TALL + 16 : n * TALL + 24, :] = mhi[at : at + 8, side : side + 128]
        edges_ext[n * TALL + 24 : n * TALL + 32, :] = mlo[at : at + 8, side : side + 128]
    lane = iota((TALL, 128), 1)
    pr = jnp.zeros((TALL, 128), F32)
    pl_ = jnp.zeros((TALL, 128), F32)
    for f in range(FIELDS):
        spot = (lane // 8) == f
        z = ext[f * TALL : (f + 1) * TALL, :]
        pr = jnp.where(spot, roll(z[:, 128:], 8 * f + 8, 1), pr)
        pl_ = jnp.where(spot, roll(z[:, :128], 8 * f, 1), pl_)
    oddx = odd_place("tx") == 1

    def send(at, right, left):
        xfar[at, :] = jnp.where(oddx, right, left)
        xnear[at, :] = jnp.where(oddx, left, right)

    send(slice(0, TALL), pr, pl_)
    first = (lane % 4) < 2
    for pair in range(2):
        p = edges_ext[2 * pair * TALL : (2 * pair + 1) * TALL, :]
        s = edges_ext[(2 * pair + 1) * TALL : (2 * pair + 2) * TALL, :]
        at = slice(TALL + 24 * pair, TALL + 24 * pair + 24)
        send(at, packed(jnp.where(first, p, roll(s, 2, 1))), packed(jnp.where(first, roll(s, -2, 1), p)))
    own = edges[4 * ROWS : 5 * ROWS, :]
    send(slice(80, 96), own, own)


def joined(lo_ref, hi_ref, edges_ext, pair, which, rows):
    own = edges_ext[(2 * pair + which) * TALL : (2 * pair + which) * TALL + rows, :]
    first = (iota((rows, 128), 1) % 4) < 2
    at = slice((1 + pair) * TALL, (1 + pair) * TALL + rows)
    lo = lo_ref[at, :]
    hi = hi_ref[at, :]
    if which == 1:
        lo = roll(lo, -2, 1)
        hi = roll(hi, 2, 1)
    return jnp.where(first, lo, own), jnp.where(first, own, hi)


def columns_kernel(far_in, near_in, ext, edges_ext, edges, seams, he, hn, basis, et_fix, lane_seam, moments):
    oddx = odd_place("tx") == 1
    xlo = unpacked(jnp.where(oddx, near_in[...], far_in[...]))
    xhi = unpacked(jnp.where(oddx, far_in[...], near_in[...]))
    lane = iota((TALL, 128), 1)
    group = lane % 4
    level = (lane // 4).astype(F32)
    tiles = []
    for f in range(FIELDS):
        z = ext[f * TALL : (f + 1) * TALL, :]
        right = roll(xhi[0:TALL, :], -8 * f, 1)
        left = roll(xlo[0:TALL, :], 120 - 8 * f, 1)
        third = jnp.where(lane < 8, right, jnp.where(lane >= 120, left, 0.0))
        tiles.append([z[:, :128], z[:, 128:], third])
    def product(x, n):
        return dot(jnp.concatenate(split(x), axis=1), seams[256 * n : 256 * n + 256, :])

    pairs = [[joined(xlo, xhi, edges_ext, pair, t, TALL) for t in range(2)] for pair in range(2)]
    stacked = [jnp.concatenate([p[t][side] for side in range(2) for t in range(2)], axis=0) for p in pairs]
    values = product(stacked[0], 2)
    senses = product(stacked[1], 3)
    cells = []
    for side in range(2):
        d = tiles[D]
        near = jnp.where(lane >= 126, d[2], d[0]) if side == 0 else jnp.where(lane >= 126, d[1], d[2])
        lev = dot(near.astype(BF16), seams[0:128, :])
        wet = level < jnp.minimum(lev, roll(lev, -1, 1))
        w = None
        for t in range(2):
            at = slice((2 * side + t) * TALL, (2 * side + t + 1) * TALL)
            f = jnp.where(wet, senses[at, :], 0.0)
            spot = (3 * side + 1 + t) * ROWS
            lane_seam[spot : spot + ROWS, :] = f[0:ROWS, :]
            term = f * values[at, :]
            w = term if w is None else w + term
        w = K1 * w
        cell = w + roll(w, 1, 1)
        cells.append(cell)
        total = product(cell, 1)
        a, b = (2, 0) if side == 0 else (1, 2)
        tiles[CE][a] = tiles[CE][a] + jnp.where(lane >= 126, total, 0.0)
        tiles[CE][b] = tiles[CE][b] + jnp.where(lane < 2, total, 0.0)
    et_fix[...] = jnp.where(group < 2, cells[1], cells[0])[0:ROWS, :]
    own_u = edges[4 * ROWS : 5 * ROWS, :]
    half = group[0:ROWS, :] < 2
    for side, uu in enumerate((jnp.where(half, xlo[96:112, :], own_u), jnp.where(half, own_u, xhi[96:112, :]))):
        lane_seam[3 * side * ROWS : (3 * side + 1) * ROWS, :] = uu + roll(uu, -1, 1)

    full = [jnp.concatenate(t, axis=1) for t in tiles]
    d = full[D]
    near_e = jnp.minimum(d, roll(d, -1, 1))
    near_n = jnp.minimum(d, roll(d, -1, 0))
    we = STIFF * near_e
    wn = STIFF * near_n
    half_e = jnp.where(near_e > 0.0, 0.5, 0.0)
    half_n = jnp.where(near_n > 0.0, 0.5, 0.0)
    x0 = full[X0]
    flux_e = half_e * (full[TE] + roll(full[TE], -1, 1)) + we * (x0 - roll(x0, -1, 1))
    flux_n = half_n * (full[TN] + roll(full[TN], -1, 0)) + wn * (x0 - roll(x0, -1, 0))
    r = (roll(flux_e, 1, 1) - flux_e) + (roll(flux_n, 1, 0) - flux_n)
    b = full[SS] + (0.5 * GRAVITY) * (
        (roll(full[CE], -1, 1) - roll(full[CE], 1, 1)) + (roll(full[CN], -1, 0) - roll(full[CN], 1, 0))
    )

    def own_sum(x):
        part = x[0:ROWS, 0:128] + x[0:ROWS, 128:256]
        return jnp.sum(part, axis=0, keepdims=True)

    sums = []
    for n, start in enumerate((r, b)):
        vec = start
        for power in range(3):
            basis[(4 * n + power) * TALL : (4 * n + power + 1) * TALL, :] = vec
            sums.append(own_sum(vec * vec))
            de = vec - roll(vec, -1, 1)
            dn = vec - roll(vec, -1, 0)
            he = we * de
            hn = wn * dn
            sums.append(own_sum(he * de + hn * dn))
            if power < 2:
                vec = (he - roll(he, 1, 1)) + (hn - roll(hn, 1, 0))
    basis[3 * TALL : 4 * TALL, :] = x0
    basis[7 * TALL : 8 * TALL, :] = half_e
    basis[8 * TALL : 9 * TALL, :] = half_n
    spot_lane = iota((1, 128), 1)
    line = jnp.zeros((1, 128), F32)
    for n, s in enumerate(sums):
        line = line + jnp.where(spot_lane == n, jnp.sum(s, axis=1, keepdims=True), 0.0)
    moments[...] = jnp.broadcast_to(line, (128, 128))


def safe_ratio(top, bottom, limit):
    ok = bottom > 0.0
    return jnp.clip(jnp.where(ok, top / jnp.where(ok, bottom, 1.0), 0.0), 0.0, limit)


def solve_small(m):
    bound = 8.0 * STIFF * LEVELS
    a0 = m[1] / m[0]
    n1 = m[2] - a0 * m[1]
    b1 = safe_ratio(n1, m[0], bound * bound)
    a1 = safe_ratio(m[3] - a0 * (2.0 * m[2] - a0 * m[1]), n1, bound)
    s = a0 + a1
    t = a0 * a1 - b1
    n2 = m[4] - s * m[3] + t * m[2]
    b2 = safe_ratio(n2, n1, bound * bound)
    top = m[5] - 2.0 * s * m[4] + (s * s + 2.0 * t) * m[3] - 2.0 * s * t * m[2] + t * t * m[1]
    a2 = safe_ratio(top, n2, bound)
    e2 = 1.0 + a2
    e1 = jnp.maximum(1.0 + a1 - b2 / e2, 1.0)
    e0 = jnp.maximum(1.0 + a0 - b1 / e1, 1.0)
    y0 = 1.0 / e0
    y1 = -y0 / e1
    y2 = -y1 / e2
    return y0 - a0 * y1 + t * y2, y1 - s * y2, y2


def vec(ref, n):
    return ref[n * TALL : (n + 1) * TALL, :]


def prepare_kernel(u, v, q_ref, he, hn, wd, kd, seams):
    r = iota((128, 128), 0)
    c = iota((128, 128), 1)
    a = lax.rem(c, 4)
    d = r - c
    near = jnp.where(a < 2, a + 126, a - 2)
    value = jnp.where((a == 1) & ((d == 0) | (d == 1)), 7.0, 0.0)
    value = jnp.where((d == -1) & ((a == 1) | (a == 2)), -1.0, value)
    value = jnp.where((d == 2) & (a < 2), -1.0, value)
    sense = jnp.where(a < 3, band(d, ((0, -1.0), (1, 1.0))), 0.0)
    same = jnp.where(lax.rem(r, 4) == lax.rem(c + 2, 4), 1.0, 0.0)
    for n, m in enumerate((jnp.where(r == near, 1.0, 0.0), same, value, sense)):
        m = m.astype(BF16)
        seams[256 * n : 256 * n + 128, :] = m
        seams[256 * n + 128 : 256 * n + 256, :] = m
    cos, sin = frame(q_ref)
    cos = K1 * cos
    sin = K1 * sin
    fill_lanes(wd, BACK_TAPS)
    fill_rows(kd, BACK_TAPS)

    def step(g, carry):
        for kk in range(4):
            here = pl.ds(pl.multiple_of(g * (4 * ROWS), 4 * ROWS) + kk * ROWS, ROWS)
            east = cos * u[here, :] - sin * v[here, :]
            north = sin * u[here, :] + cos * v[here, :]
            he[here, :] = east + roll(east, -1, 1)
            hn[here, :] = north + roll(north, -1, 0)
        return carry

    lax.fori_loop(0, LEVELS // 4, step, 0)


def final_kernel(mom, basis, row_seam, nt_fix, lane_seam, et_fix, lev_ref, q_ref, b1, b2, he_ref, hn_ref,
                 fe1, fe2, fn1, fn2, wd, kd, seams, et, nt, th_out, sa_out, ea_out, na_out, xb,
                 row_fix, lane_fix, th, sa, ea, na, out_sems):
    outs = ((th, th_out), (sa, sa_out), (ea, ea_out), (na, na_out))

    def put(n, g):
        at = pl.ds(g * CHUNK * ROWS, CHUNK * ROWS)
        return pltpu.make_async_copy(outs[n][0].at[at, :], outs[n][1].at[at, :], out_sems.at[n, g])

    cos, sin = frame(q_ref)
    lev = lev_ref[...]
    lane = iota((ROWS, COLS), 1)
    line = jnp.sum(mom[...], axis=0, keepdims=True)
    spot = iota((1, 128), 1)
    m = [jnp.sum(jnp.where(spot == n, line, 0.0), axis=1, keepdims=True) for n in range(12)]
    cf = solve_small(m[0:6])
    cb = solve_small(m[6:12])
    end = vec(basis, 3) + (cf[0] * vec(basis, 0) + cf[1] * vec(basis, 1) + cf[2] * vec(basis, 2))
    adj = cb[0] * vec(basis, 4) + cb[1] * vec(basis, 5) + cb[2] * vec(basis, 6)
    xb[...] = adj[0:ROWS, 0:COLS]
    side_e, side_n = end[0:ROWS, :], end[:, 0:COLS]
    ge = (0.5 * GRAVITY) * (roll(side_e, -1, 1) - roll(side_e, 1, 1))
    gn = (0.5 * GRAVITY) * (roll(side_n, -1, 0) - roll(side_n, 1, 0))
    wide_e = ge + roll(ge, -1, 1)
    wide_n = gn + roll(gn, -1, 0)
    sum_e = K1 * wide_e[:, 0:COLS]
    sum_n = K1 * wide_n[0:ROWS, :]
    side_e, side_n = adj[0:ROWS, :], adj[:, 0:COLS]
    fe = vec(basis, 7)[0:ROWS, :] * (roll(side_e, -1, 1) - side_e)
    fn = vec(basis, 8)[:, 0:COLS] * (roll(side_n, -1, 0) - side_n)
    be = (fe + roll(fe, 1, 1))[:, 0:COLS]
    bn = (fn + roll(fn, 1, 0))[0:ROWS, :]

    for side, first in enumerate((-2, 15)):
        vel = []
        for i in range(2):
            r = (first + i) % TALL
            vel.append(row_seam[(6 * side + i) * LEVELS : (6 * side + i + 1) * LEVELS, :] - wide_n[r : r + 1, :])
        for t in range(2):
            spots = [(6 * side + 2 + 2 * t + i) * LEVELS for i in range(2)]
            qa, qb = [row_seam[s : s + LEVELS, :] * w for s, w in zip(spots, vel)]
            values = (K7 * qb - K1 * qa, -K1 * qb) if side == 0 else (-K1 * qa, K7 * qa - K1 * qb)
            for i in range(2):
                at = (4 * t + 2 * side + i) * LEVELS
                row_fix[at : at + LEVELS, :] = values[i]
    lane128 = iota((ROWS, 128), 1)
    group = lane128 % 4
    tiles = [wide_e[:, 128 * n : 128 * n + 128] for n in range(3)]
    for side in range(2):
        near = jnp.where(lane128 >= 126, *((tiles[2], tiles[0]) if side == 0 else (tiles[1], tiles[2])))
        gg = dot(jnp.concatenate(split(near), axis=1), seams[0:256, :])
        vel = lane_seam[3 * side * ROWS : (3 * side + 1) * ROWS, :] - gg
        keep = (group < 2) if side == 0 else ((group == 1) | (group == 2))
        for t in range(2):
            spot = (3 * side + 1 + t) * ROWS
            f = jnp.where(keep, lane_seam[spot : spot + ROWS, :] * vel, 0.0)
            at = slice(t * ROWS, (t + 1) * ROWS)
            if side == 0:
                fix = jnp.where(group == 2, K7 * roll(f, 1, 1), 0.0) - K1 * roll(f, 2, 1)
                lane_fix[at, :] = jnp.where(group >= 2, fix, 0.0)
            else:
                fix = jnp.where(group == 1, K7 * f, 0.0) - K1 * roll(f, -1, 1)
                lane_fix[at, :] = jnp.where(group < 2, fix, lane_fix[at, :])

    edge = (lane < 2) | (lane >= COLS - 2)
    line8 = iota((8, COLS), 0)

    def step(g, carry):
        turn = 128 - g * (4 * CHUNK)
        packs = [lane_fix[0:ROWS, :], lane_fix[ROWS : 2 * ROWS, :], et_fix[...]]
        packs = [pltpu.roll(p, turn, 1) for p in packs]

        def fix_rows(ref, n):
            return ref.at[pl.ds(pl.multiple_of(n * LEVELS + g * CHUNK, CHUNK), CHUNK), :]

        fixes = [[fix_rows(row_fix, n) for n in range(4)], [fix_rows(row_fix, 4 + n) for n in range(4)],
                 [fix_rows(nt_fix, n) for n in range(4)]]
        block = CHUNK * ROWS
        rows_at = pl.multiple_of(g * block, block)
        east = [[], []]
        north = [[], []]
        for kk in range(CHUNK):
            here = pl.ds(rows_at + kk * ROWS, ROWS)
            he = he_ref[here, :] - sum_e
            hn = hn_ref[here, :] - sum_n
            for t, (fe_ref, fn_ref) in enumerate(((fe1, fn1), (fe2, fn2))):
                east[t].append(fe_ref[here, :] * he)
                north[t].append(fn_ref[here, :] * hn)
        flow = split(jnp.concatenate(east[0] + east[1], axis=0))
        de = dot(jnp.concatenate(flow, axis=1), wd[...])
        flow = [split(jnp.concatenate(x, axis=0)) for x in north]
        hi = jnp.concatenate([flow[0][0], flow[1][0]], axis=1)
        lo = jnp.concatenate([flow[0][1], flow[1][1]], axis=1)
        dn = dot(kd[...], jnp.concatenate([hi, lo], axis=0))
        at = pl.ds(rows_at, block)
        th[at, :] = b1[at, :] + (de[0:block, :] + dn[:, 0:COLS])
        sa[at, :] = b2[at, :] + (de[block : 2 * block, :] + dn[:, COLS : 2 * COLS])
        for which, kk in [((0, 1), kk) for kk in range(CHUNK)] + [((2, 3), kk) for kk in range(CHUNK)]:
            k = g * CHUNK + kk
            here = pl.ds(rows_at + kk * ROWS, ROWS)
            m = lev > k
            if kk == 0 and 2 in which:
                for n in range(2):
                    put(n, g).start()

            def lane_fixed(x, n):
                z = roll(packs[n], -(4 * kk + 2), 1)
                return jnp.where(edge, x + jnp.concatenate([z, z], axis=1), x)

            def row_fixed(x, n):
                r0, r1, r14, r15 = [f[kk : kk + 1, :] for f in fixes[n]]
                top = jnp.where(line8 == 0, r0, jnp.where(line8 == 1, r1, 0.0))
                low = jnp.where(line8 == 6, r14, jnp.where(line8 == 7, r15, 0.0))
                return x + jnp.concatenate([top, low], axis=0)

            for n in which:
                if n < 2:
                    out = (th, sa)[n]
                    out[here, :] = row_fixed(lane_fixed(out[here, :], n), n)
            if 2 not in which:
                continue
            eg = jnp.where(m, lane_fixed(et[here, :], 2) + be, 0.0)
            ng = jnp.where(m, row_fixed(nt[here, :], 2) + bn, 0.0)
            ea[here, :] = cos * eg + sin * ng
            na[here, :] = cos * ng - sin * eg
        for n in range(2, 4):
            put(n, g).start()
        return carry

    lax.fori_loop(0, STEPS, step, 0)
    for g in range(STEPS):
        for n in range(4):
            put(n, g).wait()


def params(mib):
    return pltpu.CompilerParams(vmem_limit_bytes=mib * 1024 * 1024)


def far(x):
    return pltpu.with_memory_space_constraint(x, pltpu.HBM)


def sds(*shape):
    return jax.ShapeDtypeStruct(shape, F32)


def swaps(count):
    far, near = [], []
    for i in range(count - 1):
        (far if i % 2 else near).extend([(i, i + 1), (i + 1, i)])
    return far, near


def on_device(theta_start, salt_start, east_velocity, north_velocity, surface_start, wet_levels,
              face_frame, theta_sense, salt_sense, east_sense, north_sense, surface_sense):
    flat = lambda x: x.reshape(LEVELS * ROWS, COLS)
    c1, c2, u, v = map(flat, (theta_start, salt_start, east_velocity, north_velocity))
    b1, b2, es, ns = map(flat, (theta_sense, salt_sense, east_sense, north_sense))
    vol = sds(LEVELS * ROWS, COLS)
    c1, c2, b1, b2, u, v, es, ns = [far(x) for x in (c1, c2, b1, b2, u, v, es, ns)]
    hbm = pl.BlockSpec(memory_space=pltpu.HBM)
    vmem = pl.BlockSpec(memory_space=pltpu.VMEM)
    cubes = pltpu.VMEM((LEVELS * ROWS, COLS), F32)
    sems = lambda n: pltpu.SemaphoreType.DMA((n, STEPS))
    ints = jax.ShapeDtypeStruct((ROWS, COLS), jnp.int32)
    small = [far(x) for x in (wet_levels, face_frame, surface_start, surface_sense)]
    raw_far, raw_near, c1, c2, b1, b2, u, v, lev, turns, x0, ss = pl.pallas_call(
        gather_kernel,
        in_specs=[hbm] * 10,
        out_specs=[vmem] * 12,
        out_shape=[sds(RAW_ROWS, COLS)] * 2 + [vol] * 6 + [ints] * 2 + [sds(ROWS, COLS)] * 2,
        scratch_shapes=[sems(6), pltpu.SemaphoreType.DMA((4,))],
        compiler_params=params(4),
        cost_estimate=pl.CostEstimate(flops=4000000, bytes_accessed=6000000, transcendentals=0),
        name="gather",
    )(c1, c2, b1, b2, u, v, *small)
    y_far, y_near = swaps(lax.axis_size("ty"))
    x_far, x_near = swaps(lax.axis_size("tx"))
    raw_far_in = lax.ppermute(raw_far, "ty", y_far)
    raw_near_in = lax.ppermute(raw_near, "ty", y_near)

    made_far, made_near, f2d, edges, et, nt, fe1, fe2, fn1, fn2 = pl.pallas_call(
        local_kernel,
        in_specs=[vmem] * 6 + [hbm] * 2 + [vmem] * 4,
        out_specs=[vmem] * 10,
        out_shape=[sds(MADE_ROWS, COLS)] * 2 + [sds(FIELDS * ROWS, COLS), sds(5 * ROWS, 128)] + [vol] * 6,
        scratch_shapes=[cubes] * 2 + [pltpu.VMEM((2 * COLS, COLS), BF16)] * 2
        + [pltpu.VMEM((CHUNK * ROWS, 2 * CHUNK * ROWS), BF16)] * 2
        + [pltpu.VMEM((2 * CHUNK * ROWS, COLS), F32)] * 4 + [sems(2)],
        compiler_params=params(8),
        cost_estimate=pl.CostEstimate(flops=20000000, bytes_accessed=8000000, transcendentals=0),
        name="local",
    )(c1, c2, b1, b2, u, v, es, ns, lev, turns, x0, ss)
    made_far_in = lax.ppermute(made_far, "ty", y_far)
    made_near_in = lax.ppermute(made_near, "ty", y_near)

    he, hn, wd, kd, seams = pl.pallas_call(
        prepare_kernel,
        in_specs=[vmem] * 3,
        out_specs=[vmem] * 5,
        out_shape=[vol] * 2 + [jax.ShapeDtypeStruct((2 * COLS, COLS), BF16),
                               jax.ShapeDtypeStruct((CHUNK * ROWS, 2 * CHUNK * ROWS), BF16),
                               jax.ShapeDtypeStruct((1024, 128), BF16)],
        compiler_params=params(4),
        cost_estimate=pl.CostEstimate(flops=2000000, bytes_accessed=2000000, transcendentals=0),
        name="prepare",
    )(u, v, turns)

    xfar, xnear, ext, edges_ext, nt_fix, row_seam = pl.pallas_call(
        rows_kernel,
        out_shape=[sds(XROWS, 128), sds(XROWS, 128), sds(FIELDS * TALL, COLS),
                   sds(4 * TALL, 128), sds(4 * LEVELS, COLS), sds(12 * LEVELS, COLS)],
        compiler_params=params(4),
        name="rows",
    )(raw_far_in, raw_near_in, raw_far, raw_near, made_far_in, made_near_in, f2d, edges)
    xfar_in = lax.ppermute(xfar, "tx", x_far)
    xnear_in = lax.ppermute(xnear, "tx", x_near)

    basis, et_fix, lane_seam, moments = pl.pallas_call(
        columns_kernel,
        in_specs=[vmem] * 6 + [pl.BlockSpec(memory_space=pl.ANY)] * 2,
        out_shape=[sds(9 * TALL, WIDE), sds(ROWS, 128), sds(6 * ROWS, 128), sds(128, 128)],
        compiler_params=params(4),
        name="columns",
    )(xfar_in, xnear_in, ext, edges_ext, edges, seams, he, hn)
    moments = lax.all_to_all(moments, ALL, 0, 0, tiled=True)
    th, sa, ea, na, xb = pl.pallas_call(
        final_kernel,
        in_specs=[vmem] * 21,
        out_specs=[hbm] * 4 + [vmem],
        out_shape=[vol] * 4 + [sds(ROWS, COLS)],
        scratch_shapes=[pltpu.VMEM((8 * LEVELS, COLS), F32), pltpu.VMEM((2 * ROWS, 128), F32)]
        + [cubes] * 4 + [sems(4)],
        compiler_params=params(8),
        name="final",
    )(moments, basis, row_seam, nt_fix, lane_seam, et_fix, lev, turns, b1, b2, he, hn, fe1, fe2, fn1, fn2, wd, kd, seams, et, nt)
    cube = lambda x: x.reshape(LEVELS, ROWS, COLS)
    return cube(th), cube(sa), cube(ea), cube(na), xb


def solution(mesh):
    cube = P(None, "ty", "tx")
    plane = P("ty", "tx")
    return jax.shard_map(
        on_device,
        mesh=mesh,
        in_specs=(cube, cube, cube, cube, plane, plane, plane, cube, cube, cube, cube, plane),
        out_specs=(cube, cube, cube, cube, plane),
        check_vma=False,
    )
```

```python
import functools

import jax
import jax.numpy as jnp
from jax import lax
from jax.experimental import pallas as pl
from jax.experimental.pallas import tpu as pltpu
from jax.sharding import PartitionSpec as P

F32 = jnp.float32
BF16 = jnp.bfloat16
LEVELS = 32
ROWS = 16
COLS = 256
WIDE = 384
TALL = 32
CHUNK = 8
STEPS = LEVELS // CHUNK
FIELDS = 7
D, X0, TE, TN, SS, CE, CN = range(FIELDS)
RAW_AT = {D: 256, X0: 264, SS: 272}
MADE_AT = {TE: 0, TN: 8, CE: 16, CN: 24}
YE = 32
RAW_ROWS = 280
YV = 48
MADE_ROWS = 112
XROWS = 96

RATE = 0.2
GRAVITY = 0.25
STIFF = 2.0 / LEVELS
K7 = 0.5 * RATE * 7.0 / 12.0
K1 = 0.5 * RATE / 12.0
ALL = ("ty", "tx")


def roll(x, shift, axis):
    return pltpu.roll(x, shift % x.shape[axis], axis)


def iota(shape, axis):
    return lax.broadcasted_iota(jnp.int32, shape, axis)


def frame(q_ref):
    q = q_ref[...]
    cos = jnp.where(q == 0, 1.0, jnp.where(q == 2, -1.0, 0.0))
    sin = jnp.where(q == 1, 1.0, jnp.where(q == 3, -1.0, 0.0))
    return cos, sin


def face_levels(lev):
    lane = iota((ROWS, COLS), 1)
    row = iota((ROWS, COLS), 0)
    east = jnp.where(lane < COLS - 1, jnp.minimum(lev, roll(lev, -1, 1)), 0)
    north = jnp.where(row < ROWS - 1, jnp.minimum(lev, roll(lev, -1, 0)), 0)
    return east, north


def split(x):
    hi = x.astype(BF16)
    return hi, (x - hi.astype(F32)).astype(BF16)


def odd_place(axis):
    return lax.rem(lax.axis_index(axis), 2)


def band(delta, taps):
    out = jnp.zeros(delta.shape, F32)
    for at, value in taps:
        out = jnp.where(delta == at, value, out)
    return out


def fill_lanes(ref, taps):
    w = band(iota((COLS, COLS), 0) - iota((COLS, COLS), 1), taps).astype(BF16)
    ref[0:COLS, :] = w
    ref[COLS : 2 * COLS, :] = w


def fill_rows(ref, taps):
    block = CHUNK * ROWS
    r = iota((block, block), 0)
    c = iota((block, block), 1)
    m = jnp.where((r // ROWS) == (c // ROWS), band(c - r, taps), 0.0).astype(BF16)
    ref[:, 0:block] = m
    ref[:, block : 2 * block] = m


def dot(a, b):
    return jnp.dot(a, b, preferred_element_type=F32)


VALUE_TAPS = ((0, 7.0), (1, 7.0), (-1, -1.0), (2, -1.0))
SENSE_TAPS = ((0, -1.0), (1, 1.0))
BACK_TAPS = ((0, 7.0), (-1, 7.0), (1, -1.0), (-2, -1.0))


def rows_of(ref, start, r):
    line = iota((CHUNK, COLS), 0)
    block = ref.at[pl.ds(start, CHUNK * ROWS), :]
    got = jnp.zeros((CHUNK, COLS), F32)
    for kk in range(CHUNK):
        at = kk * ROWS + r
        got = jnp.where(line == kk, block[at : at + 1, :], got)
    return got


def gather_kernel(c1_in, c2_in, b1_in, b2_in, lev_in, q_in, x0_in, ss_in,
                  far, near, c1, c2, b1, b2, lev, q, x0, ss, sems, small_sems):
    small = ((q_in, q), (lev_in, lev), (x0_in, x0), (ss_in, ss))
    small = [pltpu.make_async_copy(a, b, small_sems.at[n]) for n, (a, b) in enumerate(small)]
    moves = ((c1_in, c1), (c2_in, c2), (b1_in, b1), (b2_in, b2))

    def copy(n, g):
        at = pl.ds(g * CHUNK * ROWS, CHUNK * ROWS)
        return pltpu.make_async_copy(moves[n][0].at[at, :], moves[n][1].at[at, :], sems.at[n, g])

    for c in small:
        c.start()
    for g in range(STEPS):
        for n in range(4):
            copy(n, g).start()
    for c in small:
        c.wait()
    odd = odd_place("ty")

    def step(g, carry):
        for n in range(4):
            copy(n, g).wait()
        start = pl.multiple_of(g * (CHUNK * ROWS), CHUNK * ROWS)
        for a in range(4):
            for r in range(2):
                high, low = [rows_of(moves[a][1], start, n + r) for n in (ROWS - 2, 0)]
                at = pl.ds(pl.multiple_of((2 * a + r) * LEVELS + g * CHUNK, CHUNK), CHUNK)
                far[at, :] = jnp.where(odd == 1, high, low)
                near[at, :] = jnp.where(odd == 1, low, high)
        return carry

    lax.fori_loop(0, STEPS, step, 0)
    for out, first in ((far, 8 * odd), (near, 8 - 8 * odd)):
        at = pl.ds(pl.multiple_of(first, 8), 8)
        out[RAW_AT[D] : RAW_AT[D] + 8, :] = lev[at, :].astype(F32)
        out[RAW_AT[X0] : RAW_AT[X0] + 8, :] = x0[at, :]
        out[RAW_AT[SS] : RAW_AT[SS] + 8, :] = ss[at, :]


def local_kernel(t1, t2, b1, b2, u, v, es, ns, lev_ref, q_ref, x0_ref, ss_ref,
                 far, near, f2d, edges, et, nt, fe1, fe2, fn1, fn2, wc, wb, kc, kb, ce, cn, be, bn):
    fill_lanes(wc, VALUE_TAPS)
    fill_lanes(wb, SENSE_TAPS)
    odd = odd_place("ty")
    fill_rows(kc, VALUE_TAPS)
    fill_rows(kb, SENSE_TAPS)
    cos, sin = frame(q_ref)
    lev = lev_ref[...]
    east_lev, north_lev = face_levels(lev)
    lane128 = iota((ROWS, 128), 1)
    f2d[...] = jnp.zeros_like(f2d)
    edges[...] = jnp.zeros_like(edges)

    def field(f):
        return slice(f * ROWS, (f + 1) * ROWS)

    def step(g, carry):
        acc_u = jnp.zeros((ROWS, COLS), F32)
        acc_v = jnp.zeros((ROWS, COLS), F32)
        acc_e = jnp.zeros((ROWS, COLS), F32)
        acc_n = jnp.zeros((ROWS, COLS), F32)
        packs = [jnp.zeros((ROWS, 128), F32) for _ in range(5)]
        block = CHUNK * ROWS
        rows_at = pl.multiple_of(g * block, block)
        at = pl.ds(rows_at, block)
        for one, two, w, k_rows, east, north in ((t1, t2, wc, kc, ce, cn), (b1, b2, wb, kb, be, bn)):
            hi1, lo1 = split(one[at, :])
            hi2, lo2 = split(two[at, :])
            hi = jnp.concatenate([hi1, hi2], axis=0)
            lo = jnp.concatenate([lo1, lo2], axis=0)
            east[...] = dot(jnp.concatenate([hi, lo], axis=1), w[...])
            hi = jnp.concatenate([hi1, hi2], axis=1)
            lo = jnp.concatenate([lo1, lo2], axis=1)
            both = dot(k_rows[...], jnp.concatenate([hi, lo], axis=0))
            north[0:block, :] = both[:, 0:COLS]
            north[block : 2 * block, :] = both[:, COLS : 2 * COLS]
        for kk in range(CHUNK):
            k = g * CHUNK + kk
            here = pl.ds(rows_at + kk * ROWS, ROWS)
            m = lev > k
            me = east_lev > k
            mn = north_lev > k
            ve = None
            vn = None
            for t, (fe_ref, fn_ref) in enumerate(((fe1, fn1), (fe2, fn2))):
                at = slice(t * block + kk * ROWS, t * block + (kk + 1) * ROWS)
                fe = jnp.where(me, be[at, :], 0.0)
                fn = jnp.where(mn, bn[at, :], 0.0)
                fe_ref[here, :] = fe
                fn_ref[here, :] = fn
                ve_t = fe * ce[at, :]
                vn_t = fn * cn[at, :]
                ve = ve_t if ve is None else ve + ve_t
                vn = vn_t if vn is None else vn + vn_t
            ve = K1 * ve
            vn = K1 * vn
            es_k = es[here, :]
            ns_k = ns[here, :]
            u_k = u[here, :]
            v_k = v[here, :]
            et_k = cos * es_k - sin * ns_k + (ve + roll(ve, 1, 1))
            nt_k = sin * es_k + cos * ns_k + (vn + roll(vn, 1, 0))
            et[here, :] = et_k
            nt[here, :] = nt_k
            acc_e = acc_e + jnp.where(m, et_k, 0.0)
            acc_n = acc_n + jnp.where(m, nt_k, 0.0)
            acc_u = acc_u + jnp.where(m, u_k, 0.0)
            acc_v = acc_v + jnp.where(m, v_k, 0.0)

            def ends(x):
                return jnp.where(lane128 < 2, x[:, :128], x[:, 128:])

            spot = (lane128 // 4) == kk
            packed = [ends(r[here, :]) for r in (t1, t2, b1, b2)]
            packed.append(cos[:, :128] * ends(u_k) - sin[:, :128] * ends(v_k))
            for n in range(5):
                packs[n] = jnp.where(spot, roll(packed[n], 4 * kk + 2, 1), packs[n])

        for n in range(5):
            at = slice(n * ROWS, (n + 1) * ROWS)
            edges[at, :] = edges[at, :] + pltpu.roll(packs[n], g * (4 * CHUNK), 1)
        for r in range(2):
            high, low = [
                sin[:CHUNK, :] * rows_of(u, rows_at, n + r) + cos[:CHUNK, :] * rows_of(v, rows_at, n + r)
                for n in (ROWS - 2, 0)
            ]
            at = pl.ds(pl.multiple_of(YV + r * LEVELS + g * CHUNK, CHUNK), CHUNK)
            far[at, :] = jnp.where(odd == 1, high, low)
            near[at, :] = jnp.where(odd == 1, low, high)
        f2d[field(TE), :] = f2d[field(TE), :] + (cos * acc_u - sin * acc_v)
        f2d[field(TN), :] = f2d[field(TN), :] + (sin * acc_u + cos * acc_v)
        f2d[field(CE), :] = f2d[field(CE), :] + acc_e
        f2d[field(CN), :] = f2d[field(CN), :] + acc_n
        return carry

    lax.fori_loop(0, STEPS, step, 0)
    f2d[field(D), :] = lev.astype(F32)
    f2d[field(X0), :] = x0_ref[...]
    f2d[field(SS), :] = ss_ref[...]
    for out, first in ((far, 8 * odd), (near, 8 - 8 * odd)):
        for f, spot in MADE_AT.items():
            out[spot : spot + 8, :] = f2d[pl.ds(pl.multiple_of(f * ROWS + first, 8), 8), :]
        for n in range(4):
            at = YE + 8 * (n // 2)
            side = 128 * (n % 2)
            out[at : at + 8, side : side + 128] = edges[pl.ds(pl.multiple_of(n * ROWS + first, 8), 8), :]


def row_boundary(low, high, lev_a2, lev_a1, lev_b1, lev_b2):
    level = iota((LEVELS, COLS), 0).astype(F32)
    mask_a = level < jnp.minimum(lev_a2, lev_a1)
    mask_0 = level < jnp.minimum(lev_a1, lev_b1)
    mask_b = level < jnp.minimum(lev_b1, lev_b2)

    def part(ref, a, r):
        return ref[(2 * a + r) * LEVELS : (2 * a + r + 1) * LEVELS, :]

    va = v0 = vb = None
    diffs = []
    for t in range(2):
        ca2, ca1 = part(low, t, 0), part(low, t, 1)
        cb1, cb2 = part(high, t, 0), part(high, t, 1)
        ga2, ga1 = part(low, 2 + t, 0), part(low, 2 + t, 1)
        gb1, gb2 = part(high, 2 + t, 0), part(high, 2 + t, 1)
        fa = jnp.where(mask_a, ga1 - ga2, 0.0)
        f0 = jnp.where(mask_0, gb1 - ga1, 0.0)
        fb = jnp.where(mask_b, gb2 - gb1, 0.0)
        diffs.append((fa, f0, fb))
        fa = fa * (-K1 * cb1)
        f0 = f0 * (K7 * (ca1 + cb1) - K1 * (ca2 + cb2))
        fb = fb * (-K1 * ca1)
        va = fa if va is None else va + fa
        v0 = f0 if v0 is None else v0 + f0
        vb = fb if vb is None else vb + fb
    return va, va + v0, v0 + vb, vb, diffs


def packed(x):
    half = iota((8, 128), 0) < 4
    return jnp.concatenate([x[0:ROWS, :], jnp.where(half, x[16:24, :], x[24:32, :])], axis=0)


def unpacked(x):
    a, b = x[32:56, :], x[56:80, :]
    return jnp.concatenate([x[0:32, :], a, a[16:24, :], b, b[16:24, :], x[80:96, :]], axis=0)


def rows_kernel(far_in, near_in, far_out, near_out, mfar_in, mnear_in, mfar_out, mnear_out, *rest):
    odd = odd_place("ty")

    @pl.when(odd == 1)
    def _():
        rows_body(near_in, far_in, far_out, near_out, mnear_in, mfar_in, mfar_out, mnear_out, *rest)

    @pl.when(odd == 0)
    def _():
        rows_body(far_in, near_in, near_out, far_out, mfar_in, mnear_in, mnear_out, mfar_out, *rest)


def rows_body(ylo, yhi, yup, ydn, mlo, mhi, mup, mdn, f2d, edges, xfar, xnear, ext, edges_ext, nt_fix, row_seam):
    d0 = f2d[0:1, :]
    d1 = f2d[1:2, :]
    d14 = f2d[ROWS - 2 : ROWS - 1, :]
    d15 = f2d[ROWS - 1 : ROWS, :]
    dlo = ylo[RAW_AT[D] : RAW_AT[D] + 8, :]
    dhi = yhi[RAW_AT[D] : RAW_AT[D] + 8, :]
    lo = row_boundary(ylo, ydn, dlo[6:7, :], dlo[7:8, :], d0, d1)
    hi = row_boundary(yup, yhi, d14, d15, dhi[0:1, :], dhi[1:2, :])
    for side, (out, at) in enumerate(((lo, 0), (hi, 1))):
        diffs = out[4]
        low, high = ((mlo, mdn), (mup, mhi))[side]
        vel = [m[YV + r * LEVELS : YV + (r + 1) * LEVELS, :] for m in (low, high) for r in range(2)]
        for i in range(2):
            spot = (6 * side + i) * LEVELS
            row_seam[spot : spot + LEVELS, :] = vel[at + i] + vel[at + i + 1]
            for t in range(2):
                spot = (6 * side + 2 + 2 * t + i) * LEVELS
                row_seam[spot : spot + LEVELS, :] = diffs[t][at + i]
    for n, value in enumerate((lo[2], lo[3], hi[0], hi[1])):
        nt_fix[n * LEVELS : (n + 1) * LEVELS, :] = value
    for f in range(FIELDS):
        ext[f * TALL : f * TALL + ROWS, :] = f2d[f * ROWS : (f + 1) * ROWS, :]
        above, below, spot = (yhi, ylo, RAW_AT[f]) if f in RAW_AT else (mhi, mlo, MADE_AT[f])
        ext[f * TALL + 16 : f * TALL + 24, :] = above[spot : spot + 8, :]
        ext[f * TALL + 24 : f * TALL + 32, :] = below[spot : spot + 8, :]
    spots = ((30, lo[0]), (31, lo[1]), (0, lo[2]), (1, lo[3]),
             (14, hi[0]), (15, hi[1]), (16, hi[2]), (17, hi[3]))
    for r, value in spots:
        at = slice(CN * TALL + r, CN * TALL + r + 1)
        ext[at, :] = ext[at, :] + jnp.sum(value, axis=0, keepdims=True)
    for n in range(4):
        at = YE + 8 * (n // 2)
        side = 128 * (n % 2)
        edges_ext[n * TALL : n * TALL + ROWS, :] = edges[n * ROWS : (n + 1) * ROWS, :]
        edges_ext[n * TALL + 16 : n * TALL + 24, :] = mhi[at : at + 8, side : side + 128]
        edges_ext[n * TALL + 24 : n * TALL + 32, :] = mlo[at : at + 8, side : side + 128]
    lane = iota((TALL, 128), 1)
    pr = jnp.zeros((TALL, 128), F32)
    pl_ = jnp.zeros((TALL, 128), F32)
    for f in range(FIELDS):
        spot = (lane // 8) == f
        z = ext[f * TALL : (f + 1) * TALL, :]
        pr = jnp.where(spot, roll(z[:, 128:], 8 * f + 8, 1), pr)
        pl_ = jnp.where(spot, roll(z[:, :128], 8 * f, 1), pl_)
    oddx = odd_place("tx") == 1

    def send(at, right, left):
        xfar[at, :] = jnp.where(oddx, right, left)
        xnear[at, :] = jnp.where(oddx, left, right)

    send(slice(0, TALL), pr, pl_)
    first = (lane % 4) < 2
    for pair in range(2):
        p = edges_ext[2 * pair * TALL : (2 * pair + 1) * TALL, :]
        s = edges_ext[(2 * pair + 1) * TALL : (2 * pair + 2) * TALL, :]
        at = slice(TALL + 24 * pair, TALL + 24 * pair + 24)
        send(at, packed(jnp.where(first, p, roll(s, 2, 1))), packed(jnp.where(first, roll(s, -2, 1), p)))
    own = edges[4 * ROWS : 5 * ROWS, :]
    send(slice(80, 96), own, own)


def joined(lo_ref, hi_ref, edges_ext, pair, which, rows):
    own = edges_ext[(2 * pair + which) * TALL : (2 * pair + which) * TALL + rows, :]
    first = (iota((rows, 128), 1) % 4) < 2
    at = slice((1 + pair) * TALL, (1 + pair) * TALL + rows)
    lo = lo_ref[at, :]
    hi = hi_ref[at, :]
    if which == 1:
        lo = roll(lo, -2, 1)
        hi = roll(hi, 2, 1)
    return jnp.where(first, lo, own), jnp.where(first, own, hi)


def columns_kernel(far_in, near_in, ext, edges_ext, edges, seams, he, hn, basis, et_fix, lane_seam, moments):
    oddx = odd_place("tx") == 1
    xlo = unpacked(jnp.where(oddx, near_in[...], far_in[...]))
    xhi = unpacked(jnp.where(oddx, far_in[...], near_in[...]))
    lane = iota((TALL, 128), 1)
    group = lane % 4
    level = (lane // 4).astype(F32)
    tiles = []
    for f in range(FIELDS):
        z = ext[f * TALL : (f + 1) * TALL, :]
        right = roll(xhi[0:TALL, :], -8 * f, 1)
        left = roll(xlo[0:TALL, :], 120 - 8 * f, 1)
        third = jnp.where(lane < 8, right, jnp.where(lane >= 120, left, 0.0))
        tiles.append([z[:, :128], z[:, 128:], third])
    def product(x, n):
        return dot(jnp.concatenate(split(x), axis=1), seams[256 * n : 256 * n + 256, :])

    pairs = [[joined(xlo, xhi, edges_ext, pair, t, TALL) for t in range(2)] for pair in range(2)]
    stacked = [jnp.concatenate([p[t][side] for side in range(2) for t in range(2)], axis=0) for p in pairs]
    values = product(stacked[0], 2)
    senses = product(stacked[1], 3)
    cells = []
    for side in range(2):
        d = tiles[D]
        near = jnp.where(lane >= 126, d[2], d[0]) if side == 0 else jnp.where(lane >= 126, d[1], d[2])
        lev = dot(near.astype(BF16), seams[0:128, :])
        wet = level < jnp.minimum(lev, roll(lev, -1, 1))
        w = None
        for t in range(2):
            at = slice((2 * side + t) * TALL, (2 * side + t + 1) * TALL)
            f = jnp.where(wet, senses[at, :], 0.0)
            spot = (3 * side + 1 + t) * ROWS
            lane_seam[spot : spot + ROWS, :] = f[0:ROWS, :]
            term = f * values[at, :]
            w = term if w is None else w + term
        w = K1 * w
        cell = w + roll(w, 1, 1)
        cells.append(cell)
        total = product(cell, 1)
        a, b = (2, 0) if side == 0 else (1, 2)
        tiles[CE][a] = tiles[CE][a] + jnp.where(lane >= 126, total, 0.0)
        tiles[CE][b] = tiles[CE][b] + jnp.where(lane < 2, total, 0.0)
    et_fix[...] = jnp.where(group < 2, cells[1], cells[0])[0:ROWS, :]
    own_u = edges[4 * ROWS : 5 * ROWS, :]
    half = group[0:ROWS, :] < 2
    for side, uu in enumerate((jnp.where(half, xlo[96:112, :], own_u), jnp.where(half, own_u, xhi[96:112, :]))):
        lane_seam[3 * side * ROWS : (3 * side + 1) * ROWS, :] = uu + roll(uu, -1, 1)

    full = [jnp.concatenate(t, axis=1) for t in tiles]
    d = full[D]
    near_e = jnp.minimum(d, roll(d, -1, 1))
    near_n = jnp.minimum(d, roll(d, -1, 0))
    we = STIFF * near_e
    wn = STIFF * near_n
    half_e = jnp.where(near_e > 0.0, 0.5, 0.0)
    half_n = jnp.where(near_n > 0.0, 0.5, 0.0)
    x0 = full[X0]
    flux_e = half_e * (full[TE] + roll(full[TE], -1, 1)) + we * (x0 - roll(x0, -1, 1))
    flux_n = half_n * (full[TN] + roll(full[TN], -1, 0)) + wn * (x0 - roll(x0, -1, 0))
    r = (roll(flux_e, 1, 1) - flux_e) + (roll(flux_n, 1, 0) - flux_n)
    b = full[SS] + (0.5 * GRAVITY) * (
        (roll(full[CE], -1, 1) - roll(full[CE], 1, 1)) + (roll(full[CN], -1, 0) - roll(full[CN], 1, 0))
    )

    def own_sum(x):
        part = x[0:ROWS, 0:128] + x[0:ROWS, 128:256]
        return jnp.sum(part, axis=0, keepdims=True)

    sums = []
    for n, start in enumerate((r, b)):
        vec = start
        for power in range(3):
            basis[(4 * n + power) * TALL : (4 * n + power + 1) * TALL, :] = vec
            sums.append(own_sum(vec * vec))
            de = vec - roll(vec, -1, 1)
            dn = vec - roll(vec, -1, 0)
            he = we * de
            hn = wn * dn
            sums.append(own_sum(he * de + hn * dn))
            if power < 2:
                vec = (he - roll(he, 1, 1)) + (hn - roll(hn, 1, 0))
    basis[3 * TALL : 4 * TALL, :] = x0
    basis[7 * TALL : 8 * TALL, :] = half_e
    basis[8 * TALL : 9 * TALL, :] = half_n
    spot_lane = iota((1, 128), 1)
    line = jnp.zeros((1, 128), F32)
    for n, s in enumerate(sums):
        line = line + jnp.where(spot_lane == n, jnp.sum(s, axis=1, keepdims=True), 0.0)
    moments[...] = jnp.broadcast_to(line, (128, 128))


def safe_ratio(top, bottom, limit):
    ok = bottom > 0.0
    return jnp.clip(jnp.where(ok, top / jnp.where(ok, bottom, 1.0), 0.0), 0.0, limit)


def solve_small(m):
    bound = 8.0 * STIFF * LEVELS
    a0 = m[1] / m[0]
    n1 = m[2] - a0 * m[1]
    b1 = safe_ratio(n1, m[0], bound * bound)
    a1 = safe_ratio(m[3] - a0 * (2.0 * m[2] - a0 * m[1]), n1, bound)
    s = a0 + a1
    t = a0 * a1 - b1
    n2 = m[4] - s * m[3] + t * m[2]
    b2 = safe_ratio(n2, n1, bound * bound)
    top = m[5] - 2.0 * s * m[4] + (s * s + 2.0 * t) * m[3] - 2.0 * s * t * m[2] + t * t * m[1]
    a2 = safe_ratio(top, n2, bound)
    e2 = 1.0 + a2
    e1 = jnp.maximum(1.0 + a1 - b2 / e2, 1.0)
    e0 = jnp.maximum(1.0 + a0 - b1 / e1, 1.0)
    y0 = 1.0 / e0
    y1 = -y0 / e1
    y2 = -y1 / e2
    return y0 - a0 * y1 + t * y2, y1 - s * y2, y2


def vec(ref, n):
    return ref[n * TALL : (n + 1) * TALL, :]


def prepare_kernel(u, v, q_ref, he, hn, wd, kd, seams):
    r = iota((128, 128), 0)
    c = iota((128, 128), 1)
    a = lax.rem(c, 4)
    d = r - c
    near = jnp.where(a < 2, a + 126, a - 2)
    value = jnp.where((a == 1) & ((d == 0) | (d == 1)), 7.0, 0.0)
    value = jnp.where((d == -1) & ((a == 1) | (a == 2)), -1.0, value)
    value = jnp.where((d == 2) & (a < 2), -1.0, value)
    sense = jnp.where(a < 3, band(d, ((0, -1.0), (1, 1.0))), 0.0)
    same = jnp.where(lax.rem(r, 4) == lax.rem(c + 2, 4), 1.0, 0.0)
    for n, m in enumerate((jnp.where(r == near, 1.0, 0.0), same, value, sense)):
        m = m.astype(BF16)
        seams[256 * n : 256 * n + 128, :] = m
        seams[256 * n + 128 : 256 * n + 256, :] = m
    cos, sin = frame(q_ref)
    cos = K1 * cos
    sin = K1 * sin
    fill_lanes(wd, BACK_TAPS)
    fill_rows(kd, BACK_TAPS)

    def step(g, carry):
        for kk in range(4):
            here = pl.ds(pl.multiple_of(g * (4 * ROWS), 4 * ROWS) + kk * ROWS, ROWS)
            east = cos * u[here, :] - sin * v[here, :]
            north = sin * u[here, :] + cos * v[here, :]
            he[here, :] = east + roll(east, -1, 1)
            hn[here, :] = north + roll(north, -1, 0)
        return carry

    lax.fori_loop(0, LEVELS // 4, step, 0)


def final_kernel(mom, basis, row_seam, nt_fix, lane_seam, et_fix, lev_ref, q_ref, b1, b2, he_ref, hn_ref,
                 fe1, fe2, fn1, fn2, wd, kd, seams, et, nt, th_out, sa_out, ea_out, na_out, xb,
                 row_fix, lane_fix, th, sa, ea, na, out_sems):
    outs = ((th, th_out), (sa, sa_out), (ea, ea_out), (na, na_out))

    def put(n, g):
        at = pl.ds(g * CHUNK * ROWS, CHUNK * ROWS)
        return pltpu.make_async_copy(outs[n][0].at[at, :], outs[n][1].at[at, :], out_sems.at[n, g])

    cos, sin = frame(q_ref)
    lev = lev_ref[...]
    lane = iota((ROWS, COLS), 1)
    line = jnp.sum(mom[...], axis=0, keepdims=True)
    spot = iota((1, 128), 1)
    m = [jnp.sum(jnp.where(spot == n, line, 0.0), axis=1, keepdims=True) for n in range(12)]
    cf = solve_small(m[0:6])
    cb = solve_small(m[6:12])
    end = vec(basis, 3) + (cf[0] * vec(basis, 0) + cf[1] * vec(basis, 1) + cf[2] * vec(basis, 2))
    adj = cb[0] * vec(basis, 4) + cb[1] * vec(basis, 5) + cb[2] * vec(basis, 6)
    xb[...] = adj[0:ROWS, 0:COLS]
    side_e, side_n = end[0:ROWS, :], end[:, 0:COLS]
    ge = (0.5 * GRAVITY) * (roll(side_e, -1, 1) - roll(side_e, 1, 1))
    gn = (0.5 * GRAVITY) * (roll(side_n, -1, 0) - roll(side_n, 1, 0))
    wide_e = ge + roll(ge, -1, 1)
    wide_n = gn + roll(gn, -1, 0)
    sum_e = K1 * wide_e[:, 0:COLS]
    sum_n = K1 * wide_n[0:ROWS, :]
    side_e, side_n = adj[0:ROWS, :], adj[:, 0:COLS]
    fe = vec(basis, 7)[0:ROWS, :] * (roll(side_e, -1, 1) - side_e)
    fn = vec(basis, 8)[:, 0:COLS] * (roll(side_n, -1, 0) - side_n)
    be = (fe + roll(fe, 1, 1))[:, 0:COLS]
    bn = (fn + roll(fn, 1, 0))[0:ROWS, :]

    for side, first in enumerate((-2, 15)):
        vel = []
        for i in range(2):
            r = (first + i) % TALL
            vel.append(row_seam[(6 * side + i) * LEVELS : (6 * side + i + 1) * LEVELS, :] - wide_n[r : r + 1, :])
        for t in range(2):
            spots = [(6 * side + 2 + 2 * t + i) * LEVELS for i in range(2)]
            qa, qb = [row_seam[s : s + LEVELS, :] * w for s, w in zip(spots, vel)]
            values = (K7 * qb - K1 * qa, -K1 * qb) if side == 0 else (-K1 * qa, K7 * qa - K1 * qb)
            for i in range(2):
                at = (4 * t + 2 * side + i) * LEVELS
                row_fix[at : at + LEVELS, :] = values[i]
    lane128 = iota((ROWS, 128), 1)
    group = lane128 % 4
    tiles = [wide_e[:, 128 * n : 128 * n + 128] for n in range(3)]
    for side in range(2):
        near = jnp.where(lane128 >= 126, *((tiles[2], tiles[0]) if side == 0 else (tiles[1], tiles[2])))
        gg = dot(jnp.concatenate(split(near), axis=1), seams[0:256, :])
        vel = lane_seam[3 * side * ROWS : (3 * side + 1) * ROWS, :] - gg
        keep = (group < 2) if side == 0 else ((group == 1) | (group == 2))
        for t in range(2):
            spot = (3 * side + 1 + t) * ROWS
            f = jnp.where(keep, lane_seam[spot : spot + ROWS, :] * vel, 0.0)
            at = slice(t * ROWS, (t + 1) * ROWS)
            if side == 0:
                fix = jnp.where(group == 2, K7 * roll(f, 1, 1), 0.0) - K1 * roll(f, 2, 1)
                lane_fix[at, :] = jnp.where(group >= 2, fix, 0.0)
            else:
                fix = jnp.where(group == 1, K7 * f, 0.0) - K1 * roll(f, -1, 1)
                lane_fix[at, :] = jnp.where(group < 2, fix, lane_fix[at, :])

    edge = (lane < 2) | (lane >= COLS - 2)
    line8 = iota((8, COLS), 0)

    def step(g, carry):
        turn = 128 - g * (4 * CHUNK)
        packs = [lane_fix[0:ROWS, :], lane_fix[ROWS : 2 * ROWS, :], et_fix[...]]
        packs = [pltpu.roll(p, turn, 1) for p in packs]

        def fix_rows(ref, n):
            return ref.at[pl.ds(pl.multiple_of(n * LEVELS + g * CHUNK, CHUNK), CHUNK), :]

        fixes = [[fix_rows(row_fix, n) for n in range(4)], [fix_rows(row_fix, 4 + n) for n in range(4)],
                 [fix_rows(nt_fix, n) for n in range(4)]]
        block = CHUNK * ROWS
        rows_at = pl.multiple_of(g * block, block)
        east = [[], []]
        north = [[], []]
        for kk in range(CHUNK):
            here = pl.ds(rows_at + kk * ROWS, ROWS)
            he = he_ref[here, :] - sum_e
            hn = hn_ref[here, :] - sum_n
            for t, (fe_ref, fn_ref) in enumerate(((fe1, fn1), (fe2, fn2))):
                east[t].append(fe_ref[here, :] * he)
                north[t].append(fn_ref[here, :] * hn)
        flow = split(jnp.concatenate(east[0] + east[1], axis=0))
        de = dot(jnp.concatenate(flow, axis=1), wd[...])
        flow = [split(jnp.concatenate(x, axis=0)) for x in north]
        hi = jnp.concatenate([flow[0][0], flow[1][0]], axis=1)
        lo = jnp.concatenate([flow[0][1], flow[1][1]], axis=1)
        dn = dot(kd[...], jnp.concatenate([hi, lo], axis=0))
        at = pl.ds(rows_at, block)
        th[at, :] = b1[at, :] + (de[0:block, :] + dn[:, 0:COLS])
        sa[at, :] = b2[at, :] + (de[block : 2 * block, :] + dn[:, COLS : 2 * COLS])
        for which, kk in [((0, 1), kk) for kk in range(CHUNK)] + [((2, 3), kk) for kk in range(CHUNK)]:
            k = g * CHUNK + kk
            here = pl.ds(rows_at + kk * ROWS, ROWS)
            m = lev > k
            if kk == 0 and 2 in which:
                for n in range(2):
                    put(n, g).start()

            def lane_fixed(x, n):
                z = roll(packs[n], -(4 * kk + 2), 1)
                return jnp.where(edge, x + jnp.concatenate([z, z], axis=1), x)

            def row_fixed(x, n):
                r0, r1, r14, r15 = [f[kk : kk + 1, :] for f in fixes[n]]
                top = jnp.where(line8 == 0, r0, jnp.where(line8 == 1, r1, 0.0))
                low = jnp.where(line8 == 6, r14, jnp.where(line8 == 7, r15, 0.0))
                return x + jnp.concatenate([top, low], axis=0)

            for n in which:
                if n < 2:
                    out = (th, sa)[n]
                    out[here, :] = row_fixed(lane_fixed(out[here, :], n), n)
            if 2 not in which:
                continue
            eg = jnp.where(m, lane_fixed(et[here, :], 2) + be, 0.0)
            ng = jnp.where(m, row_fixed(nt[here, :], 2) + bn, 0.0)
            ea[here, :] = cos * eg + sin * ng
            na[here, :] = cos * ng - sin * eg
        for n in range(2, 4):
            put(n, g).start()
        return carry

    lax.fori_loop(0, STEPS, step, 0)
    for g in range(STEPS):
        for n in range(4):
            put(n, g).wait()


def params(mib):
    return pltpu.CompilerParams(vmem_limit_bytes=mib * 1024 * 1024)


def far(x):
    return pltpu.with_memory_space_constraint(x, pltpu.HBM)


def sds(*shape):
    return jax.ShapeDtypeStruct(shape, F32)


def swaps(count):
    far, near = [], []
    for i in range(count - 1):
        (far if i % 2 else near).extend([(i, i + 1), (i + 1, i)])
    return far, near


def on_device(theta_start, salt_start, east_velocity, north_velocity, surface_start, wet_levels,
              face_frame, theta_sense, salt_sense, east_sense, north_sense, surface_sense):
    flat = lambda x: x.reshape(LEVELS * ROWS, COLS)
    c1, c2, u, v = map(flat, (theta_start, salt_start, east_velocity, north_velocity))
    b1, b2, es, ns = map(flat, (theta_sense, salt_sense, east_sense, north_sense))
    vol = sds(LEVELS * ROWS, COLS)
    c1, c2, b1, b2 = [far(x) for x in (c1, c2, b1, b2)]
    hbm = pl.BlockSpec(memory_space=pltpu.HBM)
    vmem = pl.BlockSpec(memory_space=pltpu.VMEM)
    cubes = pltpu.VMEM((LEVELS * ROWS, COLS), F32)
    sems = lambda n: pltpu.SemaphoreType.DMA((n, STEPS))
    ints = jax.ShapeDtypeStruct((ROWS, COLS), jnp.int32)
    small = [far(x) for x in (wet_levels, face_frame, surface_start, surface_sense)]
    raw_far, raw_near, c1, c2, b1, b2, lev, turns, x0, ss = pl.pallas_call(
        gather_kernel,
        in_specs=[hbm] * 8,
        out_specs=[vmem] * 10,
        out_shape=[sds(RAW_ROWS, COLS)] * 2 + [vol] * 4 + [ints] * 2 + [sds(ROWS, COLS)] * 2,
        scratch_shapes=[sems(4), pltpu.SemaphoreType.DMA((4,))],
        compiler_params=params(4),
        cost_estimate=pl.CostEstimate(flops=4000000, bytes_accessed=6000000, transcendentals=0),
        name="gather",
    )(c1, c2, b1, b2, *small)
    y_far, y_near = swaps(lax.axis_size("ty"))
    x_far, x_near = swaps(lax.axis_size("tx"))
    raw_far_in = lax.ppermute(raw_far, "ty", y_far)
    raw_near_in = lax.ppermute(raw_near, "ty", y_near)

    made_far, made_near, f2d, edges, et, nt, fe1, fe2, fn1, fn2 = pl.pallas_call(
        local_kernel,
        in_specs=[vmem] * 12,
        out_specs=[vmem] * 10,
        out_shape=[sds(MADE_ROWS, COLS)] * 2 + [sds(FIELDS * ROWS, COLS), sds(5 * ROWS, 128)] + [vol] * 6,
        scratch_shapes=[pltpu.VMEM((2 * COLS, COLS), BF16)] * 2
        + [pltpu.VMEM((CHUNK * ROWS, 2 * CHUNK * ROWS), BF16)] * 2
        + [pltpu.VMEM((2 * CHUNK * ROWS, COLS), F32)] * 4,
        compiler_params=params(8),
        cost_estimate=pl.CostEstimate(flops=20000000, bytes_accessed=8000000, transcendentals=0),
        name="local",
    )(c1, c2, b1, b2, u, v, es, ns, lev, turns, x0, ss)
    made_far_in = lax.ppermute(made_far, "ty", y_far)
    made_near_in = lax.ppermute(made_near, "ty", y_near)

    he, hn, wd, kd, seams = pl.pallas_call(
        prepare_kernel,
        in_specs=[vmem] * 3,
        out_specs=[vmem] * 5,
        out_shape=[vol] * 2 + [jax.ShapeDtypeStruct((2 * COLS, COLS), BF16),
                               jax.ShapeDtypeStruct((CHUNK * ROWS, 2 * CHUNK * ROWS), BF16),
                               jax.ShapeDtypeStruct((1024, 128), BF16)],
        compiler_params=params(4),
        cost_estimate=pl.CostEstimate(flops=2000000, bytes_accessed=2000000, transcendentals=0),
        name="prepare",
    )(u, v, turns)

    xfar, xnear, ext, edges_ext, nt_fix, row_seam = pl.pallas_call(
        rows_kernel,
        out_shape=[sds(XROWS, 128), sds(XROWS, 128), sds(FIELDS * TALL, COLS),
                   sds(4 * TALL, 128), sds(4 * LEVELS, COLS), sds(12 * LEVELS, COLS)],
        compiler_params=params(4),
        name="rows",
    )(raw_far_in, raw_near_in, raw_far, raw_near, made_far_in, made_near_in, made_far, made_near,
      f2d, edges)
    xfar_in = lax.ppermute(xfar, "tx", x_far)
    xnear_in = lax.ppermute(xnear, "tx", x_near)

    basis, et_fix, lane_seam, moments = pl.pallas_call(
        columns_kernel,
        in_specs=[vmem] * 6 + [pl.BlockSpec(memory_space=pl.ANY)] * 2,
        out_shape=[sds(9 * TALL, WIDE), sds(ROWS, 128), sds(6 * ROWS, 128), sds(128, 128)],
        compiler_params=params(4),
        name="columns",
    )(xfar_in, xnear_in, ext, edges_ext, edges, seams, he, hn)
    moments = lax.all_to_all(moments, ALL, 0, 0, tiled=True)
    th, sa, ea, na, xb = pl.pallas_call(
        final_kernel,
        in_specs=[vmem] * 21,
        out_specs=[hbm] * 4 + [vmem],
        out_shape=[vol] * 4 + [sds(ROWS, COLS)],
        scratch_shapes=[pltpu.VMEM((8 * LEVELS, COLS), F32), pltpu.VMEM((2 * ROWS, 128), F32)]
        + [cubes] * 4 + [sems(4)],
        compiler_params=params(8),
        name="final",
    )(moments, basis, row_seam, nt_fix, lane_seam, et_fix, lev, turns, b1, b2, he, hn, fe1, fe2, fn1, fn2, wd, kd, seams, et, nt)
    cube = lambda x: x.reshape(LEVELS, ROWS, COLS)
    return cube(th), cube(sa), cube(ea), cube(na), xb


def solution(mesh):
    cube = P(None, "ty", "tx")
    plane = P("ty", "tx")
    return jax.shard_map(
        on_device,
        mesh=mesh,
        in_specs=(cube, cube, cube, cube, plane, plane, plane, cube, cube, cube, cube, plane),
        out_specs=(cube, cube, cube, cube, plane),
        check_vma=False,
    )
```

```python
import functools

import jax
import jax.numpy as jnp
from jax import lax
from jax.experimental import pallas as pl
from jax.experimental.pallas import tpu as pltpu
from jax.sharding import PartitionSpec as P

F32 = jnp.float32
BF16 = jnp.bfloat16
LEVELS = 32
ROWS = 16
COLS = 256
WIDE = 384
TALL = 32
CHUNK = 8
STEPS = LEVELS // CHUNK
FIELDS = 7
D, X0, TE, TN, SS, CE, CN = range(FIELDS)
RAW_AT = {D: 256, X0: 264, SS: 272}
MADE_AT = {TE: 0, TN: 8, CE: 16, CN: 24}
YE = 32
RAW_ROWS = 280
YV = 40
MADE_ROWS = 104
XROWS = 96

RATE = 0.2
GRAVITY = 0.25
STIFF = 2.0 / LEVELS
K7 = 0.5 * RATE * 7.0 / 12.0
K1 = 0.5 * RATE / 12.0
ALL = ("ty", "tx")


def roll(x, shift, axis):
    return pltpu.roll(x, shift % x.shape[axis], axis)


def iota(shape, axis):
    return lax.broadcasted_iota(jnp.int32, shape, axis)


def frame(q_ref):
    q = q_ref[...]
    cos = jnp.where(q == 0, 1.0, jnp.where(q == 2, -1.0, 0.0))
    sin = jnp.where(q == 1, 1.0, jnp.where(q == 3, -1.0, 0.0))
    return cos, sin


def face_levels(lev):
    lane = iota((ROWS, COLS), 1)
    row = iota((ROWS, COLS), 0)
    east = jnp.where(lane < COLS - 1, jnp.minimum(lev, roll(lev, -1, 1)), 0)
    north = jnp.where(row < ROWS - 1, jnp.minimum(lev, roll(lev, -1, 0)), 0)
    return east, north


def split(x):
    hi = x.astype(BF16)
    return hi, (x - hi.astype(F32)).astype(BF16)


def odd_place(axis):
    return lax.rem(lax.axis_index(axis), 2)


def band(delta, taps):
    out = jnp.zeros(delta.shape, F32)
    for at, value in taps:
        out = jnp.where(delta == at, value, out)
    return out


def fill_lanes(ref, taps):
    w = band(iota((COLS, COLS), 0) - iota((COLS, COLS), 1), taps).astype(BF16)
    ref[0:COLS, :] = w
    ref[COLS : 2 * COLS, :] = w


def fill_rows(ref, taps):
    block = CHUNK * ROWS
    r = iota((block, block), 0)
    c = iota((block, block), 1)
    m = jnp.where((r // ROWS) == (c // ROWS), band(c - r, taps), 0.0).astype(BF16)
    ref[:, 0:block] = m
    ref[:, block : 2 * block] = m


def dot(a, b):
    return jnp.dot(a, b, preferred_element_type=F32)


VALUE_TAPS = ((0, 7.0), (1, 7.0), (-1, -1.0), (2, -1.0))
SENSE_TAPS = ((0, -1.0), (1, 1.0))
BACK_TAPS = ((0, 7.0), (-1, 7.0), (1, -1.0), (-2, -1.0))


def rows_of(ref, start, r):
    line = iota((CHUNK, COLS), 0)
    block = ref.at[pl.ds(start, CHUNK * ROWS), :]
    got = jnp.zeros((CHUNK, COLS), F32)
    for kk in range(CHUNK):
        at = kk * ROWS + r
        got = jnp.where(line == kk, block[at : at + 1, :], got)
    return got


def gather_kernel(c1_in, c2_in, b1_in, b2_in, lev_in, q_in, x0_in, ss_in,
                  far, near, c1, c2, b1, b2, lev, q, x0, ss, sems, small_sems):
    small = ((q_in, q), (lev_in, lev), (x0_in, x0), (ss_in, ss))
    small = [pltpu.make_async_copy(a, b, small_sems.at[n]) for n, (a, b) in enumerate(small)]
    moves = ((c1_in, c1), (c2_in, c2), (b1_in, b1), (b2_in, b2))

    def copy(n, g):
        at = pl.ds(g * CHUNK * ROWS, CHUNK * ROWS)
        return pltpu.make_async_copy(moves[n][0].at[at, :], moves[n][1].at[at, :], sems.at[n, g])

    for c in small:
        c.start()
    for g in range(STEPS):
        for n in range(4):
            copy(n, g).start()
    for c in small:
        c.wait()
    odd = odd_place("ty")

    def step(g, carry):
        for n in range(4):
            copy(n, g).wait()
        start = pl.multiple_of(g * (CHUNK * ROWS), CHUNK * ROWS)
        for a in range(4):
            for r in range(2):
                high, low = [rows_of(moves[a][1], start, n + r) for n in (ROWS - 2, 0)]
                at = pl.ds(pl.multiple_of((2 * a + r) * LEVELS + g * CHUNK, CHUNK), CHUNK)
                far[at, :] = jnp.where(odd == 1, high, low)
                near[at, :] = jnp.where(odd == 1, low, high)
        return carry

    lax.fori_loop(0, STEPS, step, 0)
    for out, first in ((far, 8 * odd), (near, 8 - 8 * odd)):
        at = pl.ds(pl.multiple_of(first, 8), 8)
        out[RAW_AT[D] : RAW_AT[D] + 8, :] = lev[at, :].astype(F32)
        out[RAW_AT[X0] : RAW_AT[X0] + 8, :] = x0[at, :]
        out[RAW_AT[SS] : RAW_AT[SS] + 8, :] = ss[at, :]


def local_kernel(t1, t2, b1, b2, u, v, es, ns, lev_ref, q_ref, x0_ref, ss_ref,
                 far, near, f2d, edges, et, nt, fe1, fe2, fn1, fn2, wc, wb, kc, kb, ce, cn, be, bn):
    fill_lanes(wc, VALUE_TAPS)
    fill_lanes(wb, SENSE_TAPS)
    odd = odd_place("ty")
    fill_rows(kc, VALUE_TAPS)
    fill_rows(kb, SENSE_TAPS)
    cos, sin = frame(q_ref)
    lev = lev_ref[...]
    east_lev, north_lev = face_levels(lev)
    lane128 = iota((ROWS, 128), 1)
    f2d[...] = jnp.zeros_like(f2d)
    edges[...] = jnp.zeros_like(edges)

    def field(f):
        return slice(f * ROWS, (f + 1) * ROWS)

    def step(g, carry):
        acc_u = jnp.zeros((ROWS, COLS), F32)
        acc_v = jnp.zeros((ROWS, COLS), F32)
        acc_e = jnp.zeros((ROWS, COLS), F32)
        acc_n = jnp.zeros((ROWS, COLS), F32)
        packs = [jnp.zeros((ROWS, 128), F32) for _ in range(5)]
        block = CHUNK * ROWS
        rows_at = pl.multiple_of(g * block, block)
        at = pl.ds(rows_at, block)
        for one, two, w, k_rows, east, north in ((t1, t2, wc, kc, ce, cn), (b1, b2, wb, kb, be, bn)):
            hi1, lo1 = split(one[at, :])
            hi2, lo2 = split(two[at, :])
            hi = jnp.concatenate([hi1, hi2], axis=0)
            lo = jnp.concatenate([lo1, lo2], axis=0)
            east[...] = dot(jnp.concatenate([hi, lo], axis=1), w[...])
            hi = jnp.concatenate([hi1, hi2], axis=1)
            lo = jnp.concatenate([lo1, lo2], axis=1)
            both = dot(k_rows[...], jnp.concatenate([hi, lo], axis=0))
            north[0:block, :] = both[:, 0:COLS]
            north[block : 2 * block, :] = both[:, COLS : 2 * COLS]
        for kk in range(CHUNK):
            k = g * CHUNK + kk
            here = pl.ds(rows_at + kk * ROWS, ROWS)
            m = lev > k
            me = east_lev > k
            mn = north_lev > k
            ve = None
            vn = None
            for t, (fe_ref, fn_ref) in enumerate(((fe1, fn1), (fe2, fn2))):
                at = slice(t * block + kk * ROWS, t * block + (kk + 1) * ROWS)
                fe = jnp.where(me, be[at, :], 0.0)
                fn = jnp.where(mn, bn[at, :], 0.0)
                fe_ref[here, :] = fe
                fn_ref[here, :] = fn
                ve_t = fe * ce[at, :]
                vn_t = fn * cn[at, :]
                ve = ve_t if ve is None else ve + ve_t
                vn = vn_t if vn is None else vn + vn_t
            ve = K1 * ve
            vn = K1 * vn
            es_k = es[here, :]
            ns_k = ns[here, :]
            u_k = u[here, :]
            v_k = v[here, :]
            et_k = cos * es_k - sin * ns_k + (ve + roll(ve, 1, 1))
            nt_k = sin * es_k + cos * ns_k + (vn + roll(vn, 1, 0))
            et[here, :] = et_k
            nt[here, :] = nt_k
            acc_e = acc_e + jnp.where(m, et_k, 0.0)
            acc_n = acc_n + jnp.where(m, nt_k, 0.0)
            acc_u = acc_u + jnp.where(m, u_k, 0.0)
            acc_v = acc_v + jnp.where(m, v_k, 0.0)

            def ends(x):
                return jnp.where(lane128 < 2, x[:, :128], x[:, 128:])

            spot = (lane128 // 4) == kk
            packed = [ends(r[here, :]) for r in (t1, t2, b1, b2)]
            packed.append(cos[:, :128] * ends(u_k) - sin[:, :128] * ends(v_k))
            for n in range(5):
                packs[n] = jnp.where(spot, roll(packed[n], 4 * kk + 2, 1), packs[n])

        for n in range(5):
            at = slice(n * ROWS, (n + 1) * ROWS)
            edges[at, :] = edges[at, :] + pltpu.roll(packs[n], g * (4 * CHUNK), 1)
        for r in range(2):
            high, low = [
                sin[:CHUNK, :] * rows_of(u, rows_at, n + r) + cos[:CHUNK, :] * rows_of(v, rows_at, n + r)
                for n in (ROWS - 2, 0)
            ]
            at = pl.ds(pl.multiple_of(YV + r * LEVELS + g * CHUNK, CHUNK), CHUNK)
            far[at, :] = jnp.where(odd == 1, high, low)
            near[at, :] = jnp.where(odd == 1, low, high)
        f2d[field(TE), :] = f2d[field(TE), :] + (cos * acc_u - sin * acc_v)
        f2d[field(TN), :] = f2d[field(TN), :] + (sin * acc_u + cos * acc_v)
        f2d[field(CE), :] = f2d[field(CE), :] + acc_e
        f2d[field(CN), :] = f2d[field(CN), :] + acc_n
        return carry

    lax.fori_loop(0, STEPS, step, 0)
    f2d[field(D), :] = lev.astype(F32)
    f2d[field(X0), :] = x0_ref[...]
    f2d[field(SS), :] = ss_ref[...]
    for out, first in ((far, 8 * odd), (near, 8 - 8 * odd)):
        for f, spot in MADE_AT.items():
            out[spot : spot + 8, :] = f2d[pl.ds(pl.multiple_of(f * ROWS + first, 8), 8), :]
        parts = [edges[pl.ds(pl.multiple_of(n * ROWS + first, 8), 8), :] for n in range(4)]
        keep = (iota((8, COLS), 0) // 4) * 8 == first
        a = jnp.concatenate(parts[0:2], axis=1)
        b = jnp.concatenate(parts[2:4], axis=1)
        out[YE : YE + 8, :] = jnp.where(keep, a, roll(b, 4, 0))


def row_boundary(low, high, lev_a2, lev_a1, lev_b1, lev_b2):
    level = iota((LEVELS, COLS), 0).astype(F32)
    mask_a = level < jnp.minimum(lev_a2, lev_a1)
    mask_0 = level < jnp.minimum(lev_a1, lev_b1)
    mask_b = level < jnp.minimum(lev_b1, lev_b2)

    def part(ref, a, r):
        return ref[(2 * a + r) * LEVELS : (2 * a + r + 1) * LEVELS, :]

    va = v0 = vb = None
    diffs = []
    for t in range(2):
        ca2, ca1 = part(low, t, 0), part(low, t, 1)
        cb1, cb2 = part(high, t, 0), part(high, t, 1)
        ga2, ga1 = part(low, 2 + t, 0), part(low, 2 + t, 1)
        gb1, gb2 = part(high, 2 + t, 0), part(high, 2 + t, 1)
        fa = jnp.where(mask_a, ga1 - ga2, 0.0)
        f0 = jnp.where(mask_0, gb1 - ga1, 0.0)
        fb = jnp.where(mask_b, gb2 - gb1, 0.0)
        diffs.append((fa, f0, fb))
        fa = fa * (-K1 * cb1)
        f0 = f0 * (K7 * (ca1 + cb1) - K1 * (ca2 + cb2))
        fb = fb * (-K1 * ca1)
        va = fa if va is None else va + fa
        v0 = f0 if v0 is None else v0 + f0
        vb = fb if vb is None else vb + fb
    return va, va + v0, v0 + vb, vb, diffs


def packed(x):
    half = iota((8, 128), 0) < 4
    return jnp.concatenate([x[0:ROWS, :], jnp.where(half, x[16:24, :], x[24:32, :])], axis=0)


def unpacked(x):
    a, b = x[32:56, :], x[56:80, :]
    return jnp.concatenate([x[0:32, :], a, a[16:24, :], b, b[16:24, :], x[80:96, :]], axis=0)


def rows_kernel(far_in, near_in, far_out, near_out, mfar_in, mnear_in, mfar_out, mnear_out, *rest):
    odd = odd_place("ty")

    @pl.when(odd == 1)
    def _():
        rows_body(near_in, far_in, far_out, near_out, mnear_in, mfar_in, mfar_out, mnear_out, *rest)

    @pl.when(odd == 0)
    def _():
        rows_body(far_in, near_in, near_out, far_out, mfar_in, mnear_in, mnear_out, mfar_out, *rest)


def rows_body(ylo, yhi, yup, ydn, mlo, mhi, mup, mdn, f2d, edges, xfar, xnear, ext, edges_ext, nt_fix, row_seam):
    d0 = f2d[0:1, :]
    d1 = f2d[1:2, :]
    d14 = f2d[ROWS - 2 : ROWS - 1, :]
    d15 = f2d[ROWS - 1 : ROWS, :]
    dlo = ylo[RAW_AT[D] : RAW_AT[D] + 8, :]
    dhi = yhi[RAW_AT[D] : RAW_AT[D] + 8, :]
    lo = row_boundary(ylo, ydn, dlo[6:7, :], dlo[7:8, :], d0, d1)
    hi = row_boundary(yup, yhi, d14, d15, dhi[0:1, :], dhi[1:2, :])
    for side, (out, at) in enumerate(((lo, 0), (hi, 1))):
        diffs = out[4]
        low, high = ((mlo, mdn), (mup, mhi))[side]
        vel = [m[YV + r * LEVELS : YV + (r + 1) * LEVELS, :] for m in (low, high) for r in range(2)]
        for i in range(2):
            spot = (6 * side + i) * LEVELS
            row_seam[spot : spot + LEVELS, :] = vel[at + i] + vel[at + i + 1]
            for t in range(2):
                spot = (6 * side + 2 + 2 * t + i) * LEVELS
                row_seam[spot : spot + LEVELS, :] = diffs[t][at + i]
    for n, value in enumerate((lo[2], lo[3], hi[0], hi[1])):
        nt_fix[n * LEVELS : (n + 1) * LEVELS, :] = value
    for f in range(FIELDS):
        ext[f * TALL : f * TALL + ROWS, :] = f2d[f * ROWS : (f + 1) * ROWS, :]
        above, below, spot = (yhi, ylo, RAW_AT[f]) if f in RAW_AT else (mhi, mlo, MADE_AT[f])
        ext[f * TALL + 16 : f * TALL + 24, :] = above[spot : spot + 8, :]
        ext[f * TALL + 24 : f * TALL + 32, :] = below[spot : spot + 8, :]
    spots = ((30, lo[0]), (31, lo[1]), (0, lo[2]), (1, lo[3]),
             (14, hi[0]), (15, hi[1]), (16, hi[2]), (17, hi[3]))
    for r, value in spots:
        at = slice(CN * TALL + r, CN * TALL + r + 1)
        ext[at, :] = ext[at, :] + jnp.sum(value, axis=0, keepdims=True)
    for n in range(4):
        side = slice(128 * (n % 2), 128 * (n % 2) + 128)
        above, below = [m[YE : YE + 8, side] for m in (mhi, mlo)]
        if n >= 2:
            above, below = roll(above, 4, 0), roll(below, 4, 0)
        edges_ext[n * TALL : n * TALL + ROWS, :] = edges[n * ROWS : (n + 1) * ROWS, :]
        edges_ext[n * TALL + 16 : n * TALL + 24, :] = above
        edges_ext[n * TALL + 24 : n * TALL + 32, :] = below
    lane = iota((TALL, 128), 1)
    pr = jnp.zeros((TALL, 128), F32)
    pl_ = jnp.zeros((TALL, 128), F32)
    for f in range(FIELDS):
        spot = (lane // 8) == f
        z = ext[f * TALL : (f + 1) * TALL, :]
        pr = jnp.where(spot, roll(z[:, 128:], 8 * f + 8, 1), pr)
        pl_ = jnp.where(spot, roll(z[:, :128], 8 * f, 1), pl_)
    oddx = odd_place("tx") == 1

    def send(at, right, left):
        xfar[at, :] = jnp.where(oddx, right, left)
        xnear[at, :] = jnp.where(oddx, left, right)

    send(slice(0, TALL), pr, pl_)
    first = (lane % 4) < 2
    for pair in range(2):
        p = edges_ext[2 * pair * TALL : (2 * pair + 1) * TALL, :]
        s = edges_ext[(2 * pair + 1) * TALL : (2 * pair + 2) * TALL, :]
        at = slice(TALL + 24 * pair, TALL + 24 * pair + 24)
        send(at, packed(jnp.where(first, p, roll(s, 2, 1))), packed(jnp.where(first, roll(s, -2, 1), p)))
    own = edges[4 * ROWS : 5 * ROWS, :]
    send(slice(80, 96), own, own)


def joined(lo_ref, hi_ref, edges_ext, pair, which, rows):
    own = edges_ext[(2 * pair + which) * TALL : (2 * pair + which) * TALL + rows, :]
    first = (iota((rows, 128), 1) % 4) < 2
    at = slice((1 + pair) * TALL, (1 + pair) * TALL + rows)
    lo = lo_ref[at, :]
    hi = hi_ref[at, :]
    if which == 1:
        lo = roll(lo, -2, 1)
        hi = roll(hi, 2, 1)
    return jnp.where(first, lo, own), jnp.where(first, own, hi)


def columns_kernel(far_in, near_in, ext, edges_ext, edges, seams, he, hn, basis, et_fix, lane_seam, moments):
    oddx = odd_place("tx") == 1
    xlo = unpacked(jnp.where(oddx, near_in[...], far_in[...]))
    xhi = unpacked(jnp.where(oddx, far_in[...], near_in[...]))
    lane = iota((TALL, 128), 1)
    group = lane % 4
    level = (lane // 4).astype(F32)
    tiles = []
    for f in range(FIELDS):
        z = ext[f * TALL : (f + 1) * TALL, :]
        right = roll(xhi[0:TALL, :], -8 * f, 1)
        left = roll(xlo[0:TALL, :], 120 - 8 * f, 1)
        third = jnp.where(lane < 8, right, jnp.where(lane >= 120, left, 0.0))
        tiles.append([z[:, :128], z[:, 128:], third])
    def product(x, n):
        return dot(jnp.concatenate(split(x), axis=1), seams[256 * n : 256 * n + 256, :])

    pairs = [[joined(xlo, xhi, edges_ext, pair, t, TALL) for t in range(2)] for pair in range(2)]
    stacked = [jnp.concatenate([p[t][side] for side in range(2) for t in range(2)], axis=0) for p in pairs]
    values = product(stacked[0], 2)
    senses = product(stacked[1], 3)
    cells = []
    for side in range(2):
        d = tiles[D]
        near = jnp.where(lane >= 126, d[2], d[0]) if side == 0 else jnp.where(lane >= 126, d[1], d[2])
        lev = dot(near.astype(BF16), seams[0:128, :])
        wet = level < jnp.minimum(lev, roll(lev, -1, 1))
        w = None
        for t in range(2):
            at = slice((2 * side + t) * TALL, (2 * side + t + 1) * TALL)
            f = jnp.where(wet, senses[at, :], 0.0)
            spot = (3 * side + 1 + t) * ROWS
            lane_seam[spot : spot + ROWS, :] = f[0:ROWS, :]
            term = f * values[at, :]
            w = term if w is None else w + term
        w = K1 * w
        cell = w + roll(w, 1, 1)
        cells.append(cell)
        total = product(cell, 1)
        a, b = (2, 0) if side == 0 else (1, 2)
        tiles[CE][a] = tiles[CE][a] + jnp.where(lane >= 126, total, 0.0)
        tiles[CE][b] = tiles[CE][b] + jnp.where(lane < 2, total, 0.0)
    et_fix[...] = jnp.where(group < 2, cells[1], cells[0])[0:ROWS, :]
    own_u = edges[4 * ROWS : 5 * ROWS, :]
    half = group[0:ROWS, :] < 2
    for side, uu in enumerate((jnp.where(half, xlo[96:112, :], own_u), jnp.where(half, own_u, xhi[96:112, :]))):
        lane_seam[3 * side * ROWS : (3 * side + 1) * ROWS, :] = uu + roll(uu, -1, 1)

    full = [jnp.concatenate(t, axis=1) for t in tiles]
    d = full[D]
    near_e = jnp.minimum(d, roll(d, -1, 1))
    near_n = jnp.minimum(d, roll(d, -1, 0))
    we = STIFF * near_e
    wn = STIFF * near_n
    half_e = jnp.where(near_e > 0.0, 0.5, 0.0)
    half_n = jnp.where(near_n > 0.0, 0.5, 0.0)
    x0 = full[X0]
    flux_e = half_e * (full[TE] + roll(full[TE], -1, 1)) + we * (x0 - roll(x0, -1, 1))
    flux_n = half_n * (full[TN] + roll(full[TN], -1, 0)) + wn * (x0 - roll(x0, -1, 0))
    r = (roll(flux_e, 1, 1) - flux_e) + (roll(flux_n, 1, 0) - flux_n)
    b = full[SS] + (0.5 * GRAVITY) * (
        (roll(full[CE], -1, 1) - roll(full[CE], 1, 1)) + (roll(full[CN], -1, 0) - roll(full[CN], 1, 0))
    )

    def own_sum(x):
        part = x[0:ROWS, 0:128] + x[0:ROWS, 128:256]
        return jnp.sum(part, axis=0, keepdims=True)

    sums = []
    for n, start in enumerate((r, b)):
        vec = start
        for power in range(3):
            basis[(4 * n + power) * TALL : (4 * n + power + 1) * TALL, :] = vec
            sums.append(own_sum(vec * vec))
            de = vec - roll(vec, -1, 1)
            dn = vec - roll(vec, -1, 0)
            he = we * de
            hn = wn * dn
            sums.append(own_sum(he * de + hn * dn))
            if power < 2:
                vec = (he - roll(he, 1, 1)) + (hn - roll(hn, 1, 0))
    basis[3 * TALL : 4 * TALL, :] = x0
    basis[7 * TALL : 8 * TALL, :] = half_e
    basis[8 * TALL : 9 * TALL, :] = half_n
    spot_lane = iota((1, 128), 1)
    line = jnp.zeros((1, 128), F32)
    for n, s in enumerate(sums):
        line = line + jnp.where(spot_lane == n, jnp.sum(s, axis=1, keepdims=True), 0.0)
    moments[...] = jnp.broadcast_to(line, (128, 128))


def safe_ratio(top, bottom, limit):
    ok = bottom > 0.0
    return jnp.clip(jnp.where(ok, top / jnp.where(ok, bottom, 1.0), 0.0), 0.0, limit)


def solve_small(m):
    bound = 8.0 * STIFF * LEVELS
    a0 = m[1] / m[0]
    n1 = m[2] - a0 * m[1]
    b1 = safe_ratio(n1, m[0], bound * bound)
    a1 = safe_ratio(m[3] - a0 * (2.0 * m[2] - a0 * m[1]), n1, bound)
    s = a0 + a1
    t = a0 * a1 - b1
    n2 = m[4] - s * m[3] + t * m[2]
    b2 = safe_ratio(n2, n1, bound * bound)
    top = m[5] - 2.0 * s * m[4] + (s * s + 2.0 * t) * m[3] - 2.0 * s * t * m[2] + t * t * m[1]
    a2 = safe_ratio(top, n2, bound)
    e2 = 1.0 + a2
    e1 = jnp.maximum(1.0 + a1 - b2 / e2, 1.0)
    e0 = jnp.maximum(1.0 + a0 - b1 / e1, 1.0)
    y0 = 1.0 / e0
    y1 = -y0 / e1
    y2 = -y1 / e2
    return y0 - a0 * y1 + t * y2, y1 - s * y2, y2


def vec(ref, n):
    return ref[n * TALL : (n + 1) * TALL, :]


def prepare_kernel(u, v, q_ref, he, hn, wd, kd, seams):
    r = iota((128, 128), 0)
    c = iota((128, 128), 1)
    a = lax.rem(c, 4)
    d = r - c
    near = jnp.where(a < 2, a + 126, a - 2)
    value = jnp.where((a == 1) & ((d == 0) | (d == 1)), 7.0, 0.0)
    value = jnp.where((d == -1) & ((a == 1) | (a == 2)), -1.0, value)
    value = jnp.where((d == 2) & (a < 2), -1.0, value)
    sense = jnp.where(a < 3, band(d, ((0, -1.0), (1, 1.0))), 0.0)
    same = jnp.where(lax.rem(r, 4) == lax.rem(c + 2, 4), 1.0, 0.0)
    for n, m in enumerate((jnp.where(r == near, 1.0, 0.0), same, value, sense)):
        m = m.astype(BF16)
        seams[256 * n : 256 * n + 128, :] = m
        seams[256 * n + 128 : 256 * n + 256, :] = m
    cos, sin = frame(q_ref)
    cos = K1 * cos
    sin = K1 * sin
    fill_lanes(wd, BACK_TAPS)
    fill_rows(kd, BACK_TAPS)

    def step(g, carry):
        for kk in range(4):
            here = pl.ds(pl.multiple_of(g * (4 * ROWS), 4 * ROWS) + kk * ROWS, ROWS)
            east = cos * u[here, :] - sin * v[here, :]
            north = sin * u[here, :] + cos * v[here, :]
            he[here, :] = east + roll(east, -1, 1)
            hn[here, :] = north + roll(north, -1, 0)
        return carry

    lax.fori_loop(0, LEVELS // 4, step, 0)


def final_kernel(mom, basis, row_seam, nt_fix, lane_seam, et_fix, lev_ref, q_ref, b1, b2, he_ref, hn_ref,
                 fe1, fe2, fn1, fn2, wd, kd, seams, et, nt, th_out, sa_out, ea_out, na_out, xb,
                 row_fix, lane_fix, th, sa, ea, na, out_sems):
    outs = ((th, th_out), (sa, sa_out), (ea, ea_out), (na, na_out))

    def put(n, g):
        at = pl.ds(g * CHUNK * ROWS, CHUNK * ROWS)
        return pltpu.make_async_copy(outs[n][0].at[at, :], outs[n][1].at[at, :], out_sems.at[n, g])

    cos, sin = frame(q_ref)
    lev = lev_ref[...]
    lane = iota((ROWS, COLS), 1)
    line = jnp.sum(mom[...], axis=0, keepdims=True)
    spot = iota((1, 128), 1)
    m = [jnp.sum(jnp.where(spot == n, line, 0.0), axis=1, keepdims=True) for n in range(12)]
    cf = solve_small(m[0:6])
    cb = solve_small(m[6:12])
    end = vec(basis, 3) + (cf[0] * vec(basis, 0) + cf[1] * vec(basis, 1) + cf[2] * vec(basis, 2))
    adj = cb[0] * vec(basis, 4) + cb[1] * vec(basis, 5) + cb[2] * vec(basis, 6)
    xb[...] = adj[0:ROWS, 0:COLS]
    side_e, side_n = end[0:ROWS, :], end[:, 0:COLS]
    ge = (0.5 * GRAVITY) * (roll(side_e, -1, 1) - roll(side_e, 1, 1))
    gn = (0.5 * GRAVITY) * (roll(side_n, -1, 0) - roll(side_n, 1, 0))
    wide_e = ge + roll(ge, -1, 1)
    wide_n = gn + roll(gn, -1, 0)
    sum_e = K1 * wide_e[:, 0:COLS]
    sum_n = K1 * wide_n[0:ROWS, :]
    side_e, side_n = adj[0:ROWS, :], adj[:, 0:COLS]
    fe = vec(basis, 7)[0:ROWS, :] * (roll(side_e, -1, 1) - side_e)
    fn = vec(basis, 8)[:, 0:COLS] * (roll(side_n, -1, 0) - side_n)
    be = (fe + roll(fe, 1, 1))[:, 0:COLS]
    bn = (fn + roll(fn, 1, 0))[0:ROWS, :]

    for side, first in enumerate((-2, 15)):
        vel = []
        for i in range(2):
            r = (first + i) % TALL
            vel.append(row_seam[(6 * side + i) * LEVELS : (6 * side + i + 1) * LEVELS, :] - wide_n[r : r + 1, :])
        for t in range(2):
            spots = [(6 * side + 2 + 2 * t + i) * LEVELS for i in range(2)]
            qa, qb = [row_seam[s : s + LEVELS, :] * w for s, w in zip(spots, vel)]
            values = (K7 * qb - K1 * qa, -K1 * qb) if side == 0 else (-K1 * qa, K7 * qa - K1 * qb)
            for i in range(2):
                at = (4 * t + 2 * side + i) * LEVELS
                row_fix[at : at + LEVELS, :] = values[i]
    lane128 = iota((ROWS, 128), 1)
    group = lane128 % 4
    tiles = [wide_e[:, 128 * n : 128 * n + 128] for n in range(3)]
    for side in range(2):
        near = jnp.where(lane128 >= 126, *((tiles[2], tiles[0]) if side == 0 else (tiles[1], tiles[2])))
        gg = dot(jnp.concatenate(split(near), axis=1), seams[0:256, :])
        vel = lane_seam[3 * side * ROWS : (3 * side + 1) * ROWS, :] - gg
        keep = (group < 2) if side == 0 else ((group == 1) | (group == 2))
        for t in range(2):
            spot = (3 * side + 1 + t) * ROWS
            f = jnp.where(keep, lane_seam[spot : spot + ROWS, :] * vel, 0.0)
            at = slice(t * ROWS, (t + 1) * ROWS)
            if side == 0:
                fix = jnp.where(group == 2, K7 * roll(f, 1, 1), 0.0) - K1 * roll(f, 2, 1)
                lane_fix[at, :] = jnp.where(group >= 2, fix, 0.0)
            else:
                fix = jnp.where(group == 1, K7 * f, 0.0) - K1 * roll(f, -1, 1)
                lane_fix[at, :] = jnp.where(group < 2, fix, lane_fix[at, :])

    edge = (lane < 2) | (lane >= COLS - 2)
    line8 = iota((8, COLS), 0)

    def step(g, carry):
        turn = 128 - g * (4 * CHUNK)
        packs = [lane_fix[0:ROWS, :], lane_fix[ROWS : 2 * ROWS, :], et_fix[...]]
        packs = [pltpu.roll(p, turn, 1) for p in packs]

        def fix_rows(ref, n):
            return ref.at[pl.ds(pl.multiple_of(n * LEVELS + g * CHUNK, CHUNK), CHUNK), :]

        fixes = [[fix_rows(row_fix, n) for n in range(4)], [fix_rows(row_fix, 4 + n) for n in range(4)],
                 [fix_rows(nt_fix, n) for n in range(4)]]
        block = CHUNK * ROWS
        rows_at = pl.multiple_of(g * block, block)
        east = [[], []]
        north = [[], []]
        for kk in range(CHUNK):
            here = pl.ds(rows_at + kk * ROWS, ROWS)
            he = he_ref[here, :] - sum_e
            hn = hn_ref[here, :] - sum_n
            for t, (fe_ref, fn_ref) in enumerate(((fe1, fn1), (fe2, fn2))):
                east[t].append(fe_ref[here, :] * he)
                north[t].append(fn_ref[here, :] * hn)
        flow = split(jnp.concatenate(east[0] + east[1], axis=0))
        de = dot(jnp.concatenate(flow, axis=1), wd[...])
        flow = [split(jnp.concatenate(x, axis=0)) for x in north]
        hi = jnp.concatenate([flow[0][0], flow[1][0]], axis=1)
        lo = jnp.concatenate([flow[0][1], flow[1][1]], axis=1)
        dn = dot(kd[...], jnp.concatenate([hi, lo], axis=0))
        at = pl.ds(rows_at, block)
        th[at, :] = b1[at, :] + (de[0:block, :] + dn[:, 0:COLS])
        sa[at, :] = b2[at, :] + (de[block : 2 * block, :] + dn[:, COLS : 2 * COLS])
        for which, kk in [((0, 1), kk) for kk in range(CHUNK)] + [((2, 3), kk) for kk in range(CHUNK)]:
            k = g * CHUNK + kk
            here = pl.ds(rows_at + kk * ROWS, ROWS)
            m = lev > k
            if kk == 0 and 2 in which:
                for n in range(2):
                    put(n, g).start()

            def lane_fixed(x, n):
                z = roll(packs[n], -(4 * kk + 2), 1)
                return jnp.where(edge, x + jnp.concatenate([z, z], axis=1), x)

            def row_fixed(x, n):
                r0, r1, r14, r15 = [f[kk : kk + 1, :] for f in fixes[n]]
                top = jnp.where(line8 == 0, r0, jnp.where(line8 == 1, r1, 0.0))
                low = jnp.where(line8 == 6, r14, jnp.where(line8 == 7, r15, 0.0))
                return x + jnp.concatenate([top, low], axis=0)

            for n in which:
                if n < 2:
                    out = (th, sa)[n]
                    out[here, :] = row_fixed(lane_fixed(out[here, :], n), n)
            if 2 not in which:
                continue
            eg = jnp.where(m, lane_fixed(et[here, :], 2) + be, 0.0)
            ng = jnp.where(m, row_fixed(nt[here, :], 2) + bn, 0.0)
            ea[here, :] = cos * eg + sin * ng
            na[here, :] = cos * ng - sin * eg
        for n in range(2, 4):
            put(n, g).start()
        return carry

    lax.fori_loop(0, STEPS, step, 0)
    for g in range(STEPS):
        for n in range(4):
            put(n, g).wait()


def params(mib):
    return pltpu.CompilerParams(vmem_limit_bytes=mib * 1024 * 1024)


def far(x):
    return pltpu.with_memory_space_constraint(x, pltpu.HBM)


def sds(*shape):
    return jax.ShapeDtypeStruct(shape, F32)


def swaps(count):
    far, near = [], []
    for i in range(count - 1):
        (far if i % 2 else near).extend([(i, i + 1), (i + 1, i)])
    return far, near


def on_device(theta_start, salt_start, east_velocity, north_velocity, surface_start, wet_levels,
              face_frame, theta_sense, salt_sense, east_sense, north_sense, surface_sense):
    flat = lambda x: x.reshape(LEVELS * ROWS, COLS)
    c1, c2, u, v = map(flat, (theta_start, salt_start, east_velocity, north_velocity))
    b1, b2, es, ns = map(flat, (theta_sense, salt_sense, east_sense, north_sense))
    vol = sds(LEVELS * ROWS, COLS)
    c1, c2, b1, b2 = [far(x) for x in (c1, c2, b1, b2)]
    hbm = pl.BlockSpec(memory_space=pltpu.HBM)
    vmem = pl.BlockSpec(memory_space=pltpu.VMEM)
    cubes = pltpu.VMEM((LEVELS * ROWS, COLS), F32)
    sems = lambda n: pltpu.SemaphoreType.DMA((n, STEPS))
    ints = jax.ShapeDtypeStruct((ROWS, COLS), jnp.int32)
    small = [far(x) for x in (wet_levels, face_frame, surface_start, surface_sense)]
    raw_far, raw_near, c1, c2, b1, b2, lev, turns, x0, ss = pl.pallas_call(
        gather_kernel,
        in_specs=[hbm] * 8,
        out_specs=[vmem] * 10,
        out_shape=[sds(RAW_ROWS, COLS)] * 2 + [vol] * 4 + [ints] * 2 + [sds(ROWS, COLS)] * 2,
        scratch_shapes=[sems(4), pltpu.SemaphoreType.DMA((4,))],
        compiler_params=params(4),
        cost_estimate=pl.CostEstimate(flops=4000000, bytes_accessed=6000000, transcendentals=0),
        name="gather",
    )(c1, c2, b1, b2, *small)
    y_far, y_near = swaps(lax.axis_size("ty"))
    x_far, x_near = swaps(lax.axis_size("tx"))
    raw_far_in = lax.ppermute(raw_far, "ty", y_far)
    raw_near_in = lax.ppermute(raw_near, "ty", y_near)

    made_far, made_near, f2d, edges, et, nt, fe1, fe2, fn1, fn2 = pl.pallas_call(
        local_kernel,
        in_specs=[vmem] * 12,
        out_specs=[vmem] * 10,
        out_shape=[sds(MADE_ROWS, COLS)] * 2 + [sds(FIELDS * ROWS, COLS), sds(5 * ROWS, 128)] + [vol] * 6,
        scratch_shapes=[pltpu.VMEM((2 * COLS, COLS), BF16)] * 2
        + [pltpu.VMEM((CHUNK * ROWS, 2 * CHUNK * ROWS), BF16)] * 2
        + [pltpu.VMEM((2 * CHUNK * ROWS, COLS), F32)] * 4,
        compiler_params=params(8),
        cost_estimate=pl.CostEstimate(flops=20000000, bytes_accessed=8000000, transcendentals=0),
        name="local",
    )(c1, c2, b1, b2, u, v, es, ns, lev, turns, x0, ss)
    made_far_in = lax.ppermute(made_far, "ty", y_far)
    made_near_in = lax.ppermute(made_near, "ty", y_near)

    he, hn, wd, kd, seams = pl.pallas_call(
        prepare_kernel,
        in_specs=[vmem] * 3,
        out_specs=[vmem] * 5,
        out_shape=[vol] * 2 + [jax.ShapeDtypeStruct((2 * COLS, COLS), BF16),
                               jax.ShapeDtypeStruct((CHUNK * ROWS, 2 * CHUNK * ROWS), BF16),
                               jax.ShapeDtypeStruct((1024, 128), BF16)],
        compiler_params=params(4),
        cost_estimate=pl.CostEstimate(flops=2000000, bytes_accessed=2000000, transcendentals=0),
        name="prepare",
    )(u, v, turns)

    xfar, xnear, ext, edges_ext, nt_fix, row_seam = pl.pallas_call(
        rows_kernel,
        out_shape=[sds(XROWS, 128), sds(XROWS, 128), sds(FIELDS * TALL, COLS),
                   sds(4 * TALL, 128), sds(4 * LEVELS, COLS), sds(12 * LEVELS, COLS)],
        compiler_params=params(4),
        name="rows",
    )(raw_far_in, raw_near_in, raw_far, raw_near, made_far_in, made_near_in, made_far, made_near,
      f2d, edges)
    xfar_in = lax.ppermute(xfar, "tx", x_far)
    xnear_in = lax.ppermute(xnear, "tx", x_near)

    basis, et_fix, lane_seam, moments = pl.pallas_call(
        columns_kernel,
        in_specs=[vmem] * 6 + [pl.BlockSpec(memory_space=pl.ANY)] * 2,
        out_shape=[sds(9 * TALL, WIDE), sds(ROWS, 128), sds(6 * ROWS, 128), sds(128, 128)],
        compiler_params=params(4),
        name="columns",
    )(xfar_in, xnear_in, ext, edges_ext, edges, seams, he, hn)
    moments = lax.all_to_all(moments, ALL, 0, 0, tiled=True)
    th, sa, ea, na, xb = pl.pallas_call(
        final_kernel,
        in_specs=[vmem] * 21,
        out_specs=[hbm] * 4 + [vmem],
        out_shape=[vol] * 4 + [sds(ROWS, COLS)],
        scratch_shapes=[pltpu.VMEM((8 * LEVELS, COLS), F32), pltpu.VMEM((2 * ROWS, 128), F32)]
        + [cubes] * 4 + [sems(4)],
        compiler_params=params(8),
        name="final",
    )(moments, basis, row_seam, nt_fix, lane_seam, et_fix, lev, turns, b1, b2, he, hn, fe1, fe2, fn1, fn2, wd, kd, seams, et, nt)
    cube = lambda x: x.reshape(LEVELS, ROWS, COLS)
    return cube(th), cube(sa), cube(ea), cube(na), xb


def solution(mesh):
    cube = P(None, "ty", "tx")
    plane = P("ty", "tx")
    return jax.shard_map(
        on_device,
        mesh=mesh,
        in_specs=(cube, cube, cube, cube, plane, plane, plane, cube, cube, cube, cube, plane),
        out_specs=(cube, cube, cube, cube, plane),
        check_vma=False,
    )
```
